256 devices in a mesh: seq: 64 (over x_hi, y, z), head: 4 (over x_lo, core).
Axes of the slice: x: 4 (x_hi: 2, x_lo: 2; x = x_hi * 2 + x_lo), y: 4, z: 8, core: 2. Of those that a mesh axis runs over, the one named last changes fastest.
Arguments:
- queries: bfloat16 [32768, 2048], P('seq', 'head'), may hold values from -256 to 256
- keys_new: bfloat16 [32768, 2048], P('seq', 'head'), may hold values from -6 to 6
- values_new: bfloat16 [32768, 2048], P('seq', 'head'), may hold values from -6 to 6
- residual: bfloat16 [32768, 4096], P('seq', 'head'), may hold values from -6 to 6
- layer_scale: float32 [4096], P('head'), may hold values from 0.1 to 1.9
- out_weight: bfloat16 [2048, 4096], P('head'), may hold values from -0.125 to 0.125
- segment_ids: int32 [32768], P('seq'), may hold values from 0 to 203, never falling along the last dimension, each value on 1 to 201 neighbouring positions
- cache_keys: bfloat16 [8192, 2048], P('seq', 'head'), may hold values from -6 to 6
- cache_values: bfloat16 [8192, 2048], P('seq', 'head'), may hold values from -6 to 6
- block_live: int32 [512], P('seq'), may hold values from 0 to 1, as said below
- recompute_block: int32 [64], P('seq'), may hold values from 0 to 7
- recompute_hidden: bfloat16 [1024, 4096], P('seq'), may hold values from -6 to 6
- key_weight: bfloat16 [4096, 2048], P(None, 'head'), may hold values from -0.09375 to 0.09375
- owners: int32 [8192, 1], P('seq'), may hold values from 0 to 63; in each aligned block of 128 rows (0 to 127, 128 to 255, ...) at most 3 rows name the same one
Outputs:
- delivered: bfloat16 [12288, 16384], P('seq', 'head')
- refreshed_keys: bfloat16 [8192, 2048], P('seq', 'head')
The draws below stay inside these ranges and needn't reach their ends.
Inputs may be any that keep to these rules, and one draw needn't show every extreme that they name: `block_live`: one index of seq has between 2 and 6 live blocks, and some index has exactly 6. `owners`: out of the merged rows of one index of seq (aligned blocks of 128 rows), at most 3 have the same owner.
All inputs are finite; a program needn't handle non-finite values.
Results may differ from the reference program's by a relative error of at most 0.014.
Values may be sent and summed in bfloat16 or wider, within the bound.
No kernel may reach another device: no remote copies, remote signals or barrier semaphores. Data moves between devices by JAX's collectives and lax.ppermute only.
A program may use at most 128 MiB of HBM per device.

```python
import math
import jax
import jax.numpy as jnp
import numpy as np
from jax import lax

D = 4096
HD = 128
HEADS = 16
TOK_DEV = 512
CACHE_DEV = 128
BLK = 16
SEG_MOST = 201
TOKENS = 32768
CACHE = 8192
NBLK = 8
LIVE_MOST = 6
FRAMES = 204
MERGED = 8192
CAP = 3
N_SEQ = 64


def draw_queries(key, part):
    base = jnp.clip(jax.random.normal(key, (TOKENS, HEADS * HD), jnp.float32), -6.0, 6.0) * 2.5
    return base.astype(jnp.bfloat16)


def draw_block_live(key, part):
    count_key = jax.random.fold_in(key, 3)
    full_key = jax.random.fold_in(key, 5)
    order_key = jax.random.fold_in(key, 9)
    counts = jax.random.randint(count_key, (N_SEQ,), 2, LIVE_MOST + 1)
    full_one = jax.random.randint(full_key, (), 0, N_SEQ)
    counts = jnp.where(jnp.arange(N_SEQ) == full_one, LIVE_MOST, counts)
    scores = jax.random.randint(order_key, (N_SEQ, NBLK), 0, 1048576) * NBLK + jnp.arange(NBLK)[None, :]
    ranking = jnp.argsort(jnp.argsort(scores, axis=1), axis=1)
    return (ranking < counts[:, None]).astype(jnp.int32).reshape(-1)


def set_ends(result, stream_key, least, top_value):
    longest = result.shape.index(max(result.shape))
    spots = []
    for shift in (0, 1):
        where = [jax.random.randint(jax.random.fold_in(stream_key, axis), (), 0, length) for axis, length in enumerate(result.shape)]
        where[longest] = (where[longest] + shift) % result.shape[longest]
        spots.append(tuple(where))
    return result.at[spots[0]].set(least).at[spots[1]].set(top_value)


def block_scale(stream_key, extent, pieces, smallest, high):
    loudness = 1.0
    for dim, blocks in pieces:
        heights = jax.random.uniform(jax.random.fold_in(jax.random.fold_in(stream_key, 6), dim), (blocks,), jnp.float32, smallest / len(pieces), high / len(pieces))
        loudness = loudness * jnp.repeat(jnp.exp(heights), extent[dim] // blocks).reshape((-1,) + (1,) * (len(extent) - 1 - dim))
    return loudness


def split_up(count, total, limit, skew):
    loads = [(1 << 20) // math.isqrt(rank ** skew) + 1 for rank in range(2, count + 1)]
    rest, holding = total - limit - (count - 1), [1] * (count - 1)
    while rest > 0:
        movable = [i for i in range(count - 1) if holding[i] < limit]
        whole, budget = sum([loads[i] for i in movable]), rest
        for i in movable:
            addition = min(limit - holding[i], max(1, budget * loads[i] // whole), rest)
            holding[i] = holding[i] + addition
            rest = rest - addition
    return np.array([limit] + holding)


def ragged(stream_key, count, total, limit, skew):
    if count == 2:
        one = jax.random.randint(stream_key, (), max(1, total - limit), min(limit, total - 1) + 1)
        return jnp.stack([one, total - one])
    lengths = jnp.asarray(split_up(count, total, limit, skew), jnp.int32)
    couples = (count - 1) // 2
    giver, receiver = lengths[1:1 + 2 * couples:2], lengths[2:2 + 2 * couples:2]
    margin = jnp.minimum(giver - 1, limit - receiver)
    moved = jax.random.randint(jax.random.fold_in(stream_key, 1), (couples,), 0, 1 << 20) % (margin + 1)
    lengths = lengths.at[1:1 + 2 * couples:2].set(giver - moved).at[2:2 + 2 * couples:2].set(receiver + moved)
    return lengths[jax.random.permutation(jax.random.fold_in(stream_key, 2), count)]


def assign_block(rng, own, number, rows, number_of, top, bound, lean):
    order = jax.random.permutation(rng, number_of)
    heavy_load, common = portions_of(number_of, rows * top, bound, lean, True), portions_of(number_of, rows * top, bound, lean, False)
    places = jnp.arange(number_of)

    def named(tallies, rotation):
        used = int((tallies > 0).sum())
        fixed = max(1, used // 4)
        shifted = fixed + (places - fixed + rotation * (used - fixed)) % max(1, number_of - fixed)
        return jnp.zeros((number_of,), jnp.int32).at[order[jnp.where(places < fixed, places, shifted)]].set(jnp.asarray(tallies, jnp.int32))

    tallies = jnp.where(number % 4 == 0, named(heavy_load, number // 4), named(common, number - number // 4 - 1))
    mixed = jax.random.permutation(jax.random.fold_in(own, 3), number_of)
    donor, receiver = mixed[0:number_of // 2 * 2:2], mixed[1:number_of // 2 * 2:2]
    slack = jnp.minimum(tallies[donor] - 1, bound - tallies[receiver]) // 2
    slack = jnp.where((donor == order[0]) | (receiver == order[0]) | (tallies[receiver] == 0), 0, jnp.maximum(slack, 0))
    shifted = jax.random.randint(jax.random.fold_in(own, 4), (number_of // 2,), 0, 1 << 20) % (slack + 1)
    tallies = tallies.at[donor].add(-shifted).at[receiver].add(shifted)
    items = jnp.searchsorted(jnp.cumsum(tallies), jnp.arange(rows * top), side="right").astype(jnp.int32)
    grid = items.reshape(top, rows).T
    grid = grid[jax.random.permutation(jax.random.fold_in(own, 1), rows)]
    rotation = jax.random.randint(jax.random.fold_in(own, 2), (rows, 1), 0, top)
    return jnp.take_along_axis(grid, (jnp.arange(top)[None, :] + rotation) % top, axis=1)


def portions_of(number_of, total, most, slope, full):
    portions = [(1 << 20) // math.isqrt(rank ** slope) + 1 for rank in range(1, number_of + 1)]
    largest = most if full else min(most, max(-(-total // number_of), total * portions[0] // sum(portions)))
    least = 1 if total - largest >= number_of - 1 else 0
    holding, spare = [largest] + [least] * (number_of - 1), total - largest - least * (number_of - 1)
    while spare > 0:
        free = [i for i in range(1, number_of) if holding[i] < largest] or [i for i in range(1, number_of) if holding[i] < most]
        whole, budget = sum([portions[i] for i in free]), spare
        for i in free:
            more = min(most - holding[i], max(1, budget * portions[i] // whole), spare)
            holding[i] = holding[i] + more
            spare = spare - more
    return np.array(holding)


def bell_draw(own_key, dims, deviation, limit, split=(), kind=jnp.bfloat16):
    values = jax.random.normal(own_key, dims, jnp.float32) * deviation
    if len(split) > 0:
        values = block_scale(own_key, dims, split, -0.22, 0.18) * values
    return jnp.clip(values, min=-limit, max=limit).astype(kind)


def setup_inputs(seed: int = 0) -> dict:
    arg_keys = jax.random.split(jax.random.key(seed), 15)
    queries = draw_queries(jax.random.fold_in(arg_keys[14], 71), 0)
    keys_new = bell_draw(arg_keys[1], (TOKENS, HEADS * HD), 1.0, 6.0, ((0, 64), (1, 4)))
    values_new = bell_draw(arg_keys[2], (TOKENS, HEADS * HD), 1.0, 6.0, ((0, 64), (1, 4)))
    residual = bell_draw(arg_keys[3], (TOKENS, D), 1.0, 6.0, ((0, 64), (1, 4)))
    layer_scale = jnp.clip(1.0 + 0.18 * jax.random.normal(arg_keys[4], (D,), jnp.float32), 0.1, 1.9)
    out_weight = bell_draw(arg_keys[5], (HEADS * HD, D), (HEADS * HD) ** -0.5, 0.125, ((0, 4),))
    segment_ids = jnp.searchsorted(jnp.cumsum(ragged(arg_keys[6], FRAMES, TOKENS, SEG_MOST, 1)), jnp.arange(TOKENS), side="right").astype(jnp.int32)
    cache_keys = bell_draw(arg_keys[7], (CACHE, HEADS * HD), 1.0, 6.0, ((0, 64), (1, 4)))
    cache_values = bell_draw(arg_keys[8], (CACHE, HEADS * HD), 1.0, 6.0, ((0, 64), (1, 4)))
    block_live = draw_block_live(jax.random.fold_in(arg_keys[14], 71), 0)
    recompute_block = set_ends(jax.random.randint(arg_keys[10], (N_SEQ,), 0, NBLK), jax.random.fold_in(arg_keys[10], 1), 0, NBLK - 1).astype(jnp.int32)
    recompute_hidden = bell_draw(arg_keys[11], (N_SEQ * BLK, D), 1.0, 6.0, ((0, 64),))
    key_weight = bell_draw(arg_keys[12], (D, HEADS * HD), D ** -0.5, 0.09375, ((1, 4),))
    owners_keys = jax.random.split(jax.random.fold_in(arg_keys[13], 1), MERGED // (TOK_DEV // 4))
    owners_turns = jax.random.permutation(jax.random.fold_in(arg_keys[13], 3), MERGED // (TOK_DEV // 4))
    owners = jax.vmap(lambda own, number: assign_block(jax.random.fold_in(arg_keys[13], 2), own, number, TOK_DEV // 4, N_SEQ, 1, CAP, 2))(owners_keys, owners_turns).reshape((MERGED, 1))
    return dict(queries=queries, keys_new=keys_new, values_new=values_new, residual=residual, layer_scale=layer_scale, out_weight=out_weight, segment_ids=segment_ids, cache_keys=cache_keys, cache_values=cache_values, block_live=block_live, recompute_block=recompute_block, recompute_hidden=recompute_hidden, key_weight=key_weight, owners=owners)


def rounded(values):
    return lax.optimization_barrier(values.astype(jnp.bfloat16))

def rotate(vectors, positions):
    half_size = vectors.shape[-1] // 2
    freqs = 100.0 ** (-jnp.arange(half_size, dtype=jnp.float32) / half_size)
    angles = positions.astype(jnp.float32)[:, None] * freqs[None, :]
    cosine = jnp.cos(angles)[:, None, :]
    sine = jnp.sin(angles)[:, None, :]
    first_half = vectors[..., :half_size]
    second_half = vectors[..., half_size:]
    return jnp.concatenate([first_half * cosine - second_half * sine, second_half * cosine + first_half * sine], axis=-1)

def reference(queries, keys_new, values_new, residual, layer_scale, out_weight, segment_ids, cache_keys, cache_values, block_live, recompute_block, recompute_hidden, key_weight, owners):
    rim_rows = SEG_MOST - 1
    score_scale = 1.0 / math.sqrt(HD)
    index_all = jnp.arange(TOKENS, dtype=jnp.int32)
    is_first = jnp.concatenate([jnp.ones((1,), dtype=bool), segment_ids[1:] != segment_ids[:-1]])
    seg_start = lax.cummax(jnp.where(is_first, index_all, 0), axis=0)
    in_frame = index_all - seg_start
    q_rot = rounded(rotate(queries.astype(jnp.float32).reshape(TOKENS, HEADS, HD), in_frame)).astype(jnp.float32)
    k_rot = rounded(rotate(keys_new.astype(jnp.float32).reshape(TOKENS, HEADS, HD), in_frame)).astype(jnp.float32)
    v_new = values_new.astype(jnp.float32).reshape(TOKENS, HEADS, HD)
    fresh = jnp.dot(recompute_hidden, key_weight, preferred_element_type=jnp.float32)
    rows_fresh = (jnp.arange(N_SEQ, dtype=jnp.int32)[:, None] * CACHE_DEV + recompute_block.astype(jnp.int32)[:, None] * BLK + jnp.arange(BLK, dtype=jnp.int32)[None, :]).reshape(-1)
    fresh = rotate(fresh.reshape(N_SEQ * BLK, HEADS, HD), rows_fresh % SEG_MOST)
    refreshed = cache_keys.at[rows_fresh].set(fresh.reshape(N_SEQ * BLK, HEADS * HD).astype(jnp.bfloat16))
    refreshed = lax.optimization_barrier(refreshed)
    cache_k32 = refreshed.astype(jnp.float32).reshape(CACHE, HEADS, HD)
    cache_v32 = cache_values.astype(jnp.float32).reshape(CACHE, HEADS, HD)
    live_rows = jnp.repeat(block_live, BLK) > 0
    k_pad = jnp.pad(k_rot, ((rim_rows, rim_rows), (0, 0), (0, 0)))
    v_pad = jnp.pad(v_new, ((rim_rows, rim_rows), (0, 0), (0, 0)))
    seg_pad = jnp.pad(segment_ids, (rim_rows, rim_rows), constant_values=-1)

    def attend(cycle_slot):
        lower = cycle_slot * TOK_DEV
        q_block = lax.dynamic_slice_in_dim(q_rot, lower, TOK_DEV, 0)
        q_segs = lax.dynamic_slice_in_dim(segment_ids, lower, TOK_DEV, 0)
        k_block = lax.dynamic_slice_in_dim(k_pad, lower, TOK_DEV + 2 * rim_rows, 0)
        v_block = lax.dynamic_slice_in_dim(v_pad, lower, TOK_DEV + 2 * rim_rows, 0)
        k_segs = lax.dynamic_slice_in_dim(seg_pad, lower, TOK_DEV + 2 * rim_rows, 0)
        near = jnp.einsum('qhd,khd->hqk', q_block, k_block) * score_scale
        near = jnp.where((q_segs[:, None] == k_segs[None, :])[None], near, -jnp.inf)
        far = jnp.einsum('qhd,khd->hqk', q_block, cache_k32) * score_scale
        far = jnp.where(live_rows[None, None, :], far, -jnp.inf)
        top = jnp.maximum(lax.optimization_barrier(jnp.max(near, axis=-1)), lax.optimization_barrier(jnp.max(far, axis=-1)))
        near_w = jnp.exp(near - top[..., None])
        far_w = jnp.exp(far - top[..., None])
        weight_sum = lax.optimization_barrier(jnp.sum(near_w, axis=-1)) + lax.optimization_barrier(jnp.sum(far_w, axis=-1))
        numer = jnp.einsum('hqk,khd->hqd', rounded(near_w).astype(jnp.float32), v_block) + jnp.einsum('hqk,khd->hqd', rounded(far_w).astype(jnp.float32), cache_v32)
        return jnp.transpose(numer / weight_sum[..., None], (1, 0, 2)).astype(jnp.bfloat16)
    attended = lax.map(attend, jnp.arange(N_SEQ, dtype=jnp.int32)).reshape(TOKENS, HEADS * HD)
    projected = jnp.dot(attended, out_weight, preferred_element_type=jnp.float32)
    layer = (residual.astype(jnp.float32) + layer_scale[None, :] * projected).astype(jnp.bfloat16)
    merged = jnp.transpose(layer.reshape(MERGED, 4, D), (0, 2, 1)).reshape(MERGED, 4 * D)
    owner_rows = owners[:, 0].reshape(N_SEQ, MERGED // N_SEQ)
    hits = (owner_rows[:, :, None] == jnp.arange(N_SEQ, dtype=jnp.int32)[None, None, :]).astype(jnp.int32)
    before = jnp.cumsum(hits, axis=1) - hits
    slot_index = lax.optimization_barrier(jnp.sum(before * hits, axis=2))
    source = jnp.arange(N_SEQ, dtype=jnp.int32)[:, None]
    target = (owner_rows * (N_SEQ * CAP) + source * CAP + slot_index).reshape(-1)
    delivered = jnp.zeros((N_SEQ * N_SEQ * CAP, 4 * D), jnp.bfloat16).at[target].set(merged)
    return (delivered, refreshed)
```

```python
import math

import jax
import jax.numpy as jnp
import numpy as np
from jax import lax
from jax.experimental import pallas as pl
from jax.experimental.pallas import tpu as pltpu
from jax.sharding import Mesh, PartitionSpec as P

HD = 128
BLK = 16
SEG_MOST = 201
LIVE_MOST = 6
CAP = 3
HALO = 208
PAD = 256
TOK = 512
KT = 512
NEG = -1e30
SEQ = ("xh", "y", "zh", "zp")
HEAD = ("xl", "c")
bf16 = jnp.bfloat16
f32 = jnp.float32


def rope_parts(positions):
    half = HD // 2
    freqs = 100.0 ** (-jnp.arange(half, dtype=f32) / half)
    angles = positions.astype(f32)[:, None] * freqs[None, :]
    return jnp.cos(angles), jnp.sin(angles)


def rotate(vectors, cosine, sine):
    half = HD // 2
    a, b = vectors[..., :half], vectors[..., half:]
    c, s = cosine[:, None, :], sine[:, None, :]
    return jnp.concatenate([a * c - b * s, b * c + a * s], axis=-1)


def pack_kernel(idx, k_ref, v_ref, out_ref):
    heads = out_ref.shape[0]
    for j in range(LIVE_MOST):
        rows = pl.ds(pl.multiple_of(idx[j] * BLK, BLK), BLK)
        k = k_ref[rows, :]
        v = v_ref[rows, :]
        for p in range(heads):
            out_ref[p, j * BLK : (j + 1) * BLK, :HD] = k[:, p * HD : (p + 1) * HD]
            out_ref[p, j * BLK : (j + 1) * BLK, HD:] = v[:, p * HD : (p + 1) * HD]


def attention_kernel(
    off, tgt, zp, y0, y1, y2, y3, left, right, kvg, qid, kid, out, kc, vc, qs, kw, vw, ob, send
):
    i = pl.program_id(0)
    sources = off.shape[0] - 1
    slot_rows = LIVE_MOST * BLK
    coef = math.log2(math.e) / math.sqrt(HD)
    total = off[sources]

    @pl.when(i == 0)
    def _():
        def copy_source(s, carry):
            dst = pl.ds(pl.multiple_of(off[s], BLK), slot_rows)
            src = pl.ds(pl.multiple_of(s * slot_rows, BLK), slot_rows)
            kc[dst, :] = kvg[src, :HD]
            vc[dst, :HD] = kvg[src, HD:]
            return carry

        lax.fori_loop(0, sources, copy_source, 0)
        tail = pl.ds(pl.multiple_of(total, BLK), KT)
        kc[tail, :] = jnp.zeros((KT, HD), bf16)
        vc[tail, :HD] = jnp.zeros((KT, HD), bf16)
        vc[:, HD:] = jnp.ones((vc.shape[0], HD), bf16)
        vw[:, HD:] = jnp.ones((vw.shape[0], HD), bf16)
        for k, y in enumerate((y0, y1, y2, y3)):
            chunk = zp[0] ^ k
            dst = pl.ds(pl.multiple_of(chunk * TOK, TOK), TOK)
            qs[dst, :] = y[:, :HD]
            dst = pl.ds(pl.multiple_of(PAD + chunk * TOK, PAD), TOK)
            kw[dst, :] = y[:, HD : 2 * HD]
            vw[dst, :HD] = y[:, 2 * HD :]
        end = PAD + 4 * TOK
        gap = PAD - HALO
        kw[:gap, :] = jnp.zeros((gap, HD), bf16)
        vw[:gap, :HD] = jnp.zeros((gap, HD), bf16)
        kw[gap:PAD, :] = left[:, :HD]
        vw[gap:PAD, :HD] = left[:, HD:]
        kw[end : end + HALO, :] = right[:, :HD]
        vw[end : end + HALO, :HD] = right[:, HD:]
        kw[end + HALO :, :] = jnp.zeros((gap, HD), bf16)
        vw[end + HALO :, :HD] = jnp.zeros((gap, HD), bf16)
        send[...] = jnp.zeros(send.shape, f32)

    q = qs[pl.ds(pl.multiple_of(i * TOK, TOK), TOK), :]
    ids = qid[...]

    def scores(keys):
        return lax.dot_general(q, keys, (((1,), (1,)), ((), ())), preferred_element_type=f32)

    def step(s, values, state):
        m, acc = state
        new = jnp.max(s, axis=1, keepdims=True)
        if m is not None:
            new = jnp.maximum(m, new)
        w = jnp.exp2(s * coef - new * coef).astype(bf16)
        part = jnp.dot(w, values, preferred_element_type=f32)
        if m is not None:
            part = acc * jnp.exp2((m - new) * coef) + part
        return new, part

    window = TOK + 2 * PAD
    base = pl.multiple_of(i * TOK, TOK)
    s = scores(kw[pl.ds(base, window), :])
    s = jnp.where(ids == kid[0], s, NEG)
    state = step(s, vw[pl.ds(base, window), :], (None, None))

    def body(j, state):
        rows = pl.ds(pl.multiple_of(j * KT, KT), KT)
        return step(scores(kc[rows, :]), vc[rows, :], state)

    full = total // KT
    state = lax.fori_loop(0, full, body, state)
    rows = pl.ds(pl.multiple_of(full * KT, KT), KT)
    s = scores(kc[rows, :])
    col = lax.broadcasted_iota(jnp.int32, s.shape, 1)
    s = jnp.where(col < total - full * KT, s, NEG)
    m, acc = step(s, vc[rows, :], state)
    ob[...] = acc[:, :HD] / acc[:, HD:]

    def place(r, carry):
        dst = tgt[i * (TOK // 4) + r] * 4
        send[pl.ds(pl.multiple_of(dst, 4), 4), :] = ob[pl.ds(pl.multiple_of(r * 4, 4), 4), :]
        return carry

    lax.fori_loop(0, TOK // 4, place, 0, unroll=8)

    @pl.when(i == pl.num_programs(0) - 1)
    def _():
        out[...] = send[...].astype(bf16)


def attend(off, tgt, zp, ys, left, right, kvg, qid, kid, slots):
    chunks = len(ys)
    sources = off.shape[0] - 1
    cache_most = sources * LIVE_MOST * BLK
    whole = pl.BlockSpec(memory_space=pltpu.VMEM)
    window = TOK + 2 * PAD
    return pl.pallas_call(
        attention_kernel,
        out_shape=jax.ShapeDtypeStruct((slots * 4, HD), bf16),
        grid_spec=pltpu.PrefetchScalarGridSpec(
            num_scalar_prefetch=3,
            grid=(chunks,),
            in_specs=[whole] * 7
            + [
                pl.BlockSpec((TOK, 1), lambda i, *_: (i, 0)),
                pl.BlockSpec((1, 1, window), lambda i, *_: (i, 0, 0)),
            ],
            out_specs=whole,
            scratch_shapes=[
                pltpu.VMEM((cache_most + KT, HD), bf16),
                pltpu.VMEM((cache_most + KT, 2 * HD), bf16),
                pltpu.VMEM((chunks * TOK, HD), bf16),
                pltpu.VMEM((chunks * TOK + 2 * PAD, HD), bf16),
                pltpu.VMEM((chunks * TOK + 2 * PAD, 2 * HD), bf16),
                pltpu.VMEM((TOK, HD), f32),
                pltpu.VMEM((slots * 4, HD), f32),
            ],
        ),
        compiler_params=pltpu.CompilerParams(
            dimension_semantics=("arbitrary",), vmem_limit_bytes=48 << 20
        ),
        cost_estimate=pl.CostEstimate(
            flops=4 * 2048 * 7168 * 128, bytes_accessed=8 << 20, transcendentals=2048 * 7168
        ),
    )(off, tgt, zp, *ys, left, right, kvg, qid, kid)


def project_kernel(a0, a1, a2, a3, w0, w1, w2, w3, res, scale, mix, out, att, res32, proj):
    b = pl.program_id(0)
    groups = att.shape[0] // 48

    @pl.when(b == 0)
    def _():
        res32[...] = res[...].astype(f32)
        for k, a in enumerate((a0, a1, a2, a3)):
            for p in range(4):
                col = (k * 4 + p) * HD

                def move(g, carry):
                    src = pl.ds(pl.multiple_of(g * 192 + p * 48, 16), 48)
                    att[pl.ds(pl.multiple_of(g * 48, 16), 48), col : col + HD] = a[src, :]
                    return carry

                lax.fori_loop(0, groups, move, 0, unroll=4)

    total = None
    width = w0.shape[0]
    for k, w in enumerate((w0, w1, w2, w3)):
        part = jnp.dot(att[:, k * width : (k + 1) * width], w[...], preferred_element_type=f32)
        total = part if total is None else total + part
    total = total * scale[...]
    slots = out.shape[0]
    per = w0.shape[1] // HD
    for d in range(per):
        proj[d * 4 * slots : (d + 1) * 4 * slots, :] = total[:, d * HD : (d + 1) * HD]
    for d in range(per):
        parts = []
        for t in range(4):
            new = proj[pl.ds(d * 4 * slots + t, slots, stride=4), :]
            old = res32[pl.ds(t * 8 + b * per + d, slots, stride=32), :]
            parts.append((old + new).astype(bf16))
        rows = jnp.concatenate(parts, axis=1)
        out[:, d * 4 * HD : (d + 1) * 4 * HD] = jnp.dot(
            rows, mix[...], preferred_element_type=f32
        ).astype(bf16)


def project(atts, weights, res, scale, slots):
    width = weights[0].shape[1]
    part = 256
    whole = pl.BlockSpec(memory_space=pltpu.VMEM)
    source = np.arange(4 * HD)
    mix = np.zeros((4 * HD, 4 * HD), np.float32)
    mix[source, (source % HD) * 4 + source // HD] = 1.0
    return pl.pallas_call(
        project_kernel,
        out_shape=jax.ShapeDtypeStruct((slots, 4 * width), bf16),
        grid_spec=pltpu.PrefetchScalarGridSpec(
            num_scalar_prefetch=0,
            grid=(width // part,),
            in_specs=[whole] * 4
            + [pl.BlockSpec((weights[0].shape[0], part), lambda b: (0, b))] * 4
            + [whole, pl.BlockSpec((1, part), lambda b: (0, b)), whole],
            out_specs=pl.BlockSpec((slots, 4 * part), lambda b: (0, b)),
            scratch_shapes=[
                pltpu.VMEM((slots * 4, 16 * HD), bf16),
                pltpu.VMEM((slots * 32, HD), f32),
                pltpu.VMEM((slots * 4 * part // HD, HD), f32),
            ],
        ),
        compiler_params=pltpu.CompilerParams(
            dimension_semantics=("arbitrary",), vmem_limit_bytes=48 << 20
        ),
        cost_estimate=pl.CostEstimate(
            flops=2 * 768 * 2048 * 1024, bytes_accessed=16 << 20, transcendentals=0
        ),
    )(*atts, *weights, res, scale, jnp.asarray(mix, bf16))


def swap(x, axis, k):
    n = lax.axis_size(axis)
    return lax.ppermute(x, axis, [(i, i ^ k) for i in range(n)])


def tie(x, *others):
    return lax.optimization_barrier((x, *others))[0]


def shards(
    queries,
    keys_new,
    values_new,
    residual,
    layer_scale,
    out_weight,
    segment_ids,
    cache_keys,
    cache_values,
    block_live,
    recompute_block,
    recompute_hidden,
    key_weight,
    owners,
):
    tokens, columns = queries.shape
    heads = columns // HD
    n_seq = lax.axis_size(SEQ)
    seq = lax.axis_index(SEQ)
    zp = lax.axis_index("zp")
    head = lax.axis_index(HEAD)
    merged_rows = tokens // 4

    meta = jnp.concatenate(
        [segment_ids, owners[:, 0], block_live, jnp.zeros((128 - block_live.shape[0],), jnp.int32)]
    )
    meta = jnp.broadcast_to(meta[None, None, :], (n_seq, 1, meta.shape[0]))
    meta = lax.all_to_all(meta, SEQ, split_axis=0, concat_axis=0, tiled=True)[:, 0, :]
    ids_all = meta[:, :tokens].reshape(-1)
    owners_all = meta[:, tokens : tokens + merged_rows]
    live_all = meta[:, tokens + merged_rows : tokens + merged_rows + block_live.shape[0]]

    cache_rows = cache_keys.shape[0]
    block = recompute_block[0]
    fresh = jnp.dot(recompute_hidden, key_weight, preferred_element_type=f32)
    fresh_rows = seq * cache_rows + block * BLK + jnp.arange(BLK, dtype=jnp.int32)
    fresh = rotate(fresh.reshape(BLK, heads, HD), *rope_parts(fresh_rows % SEG_MOST))
    fresh = fresh.reshape(BLK, columns).astype(bf16)
    refreshed = lax.dynamic_update_slice(cache_keys, fresh, (block * BLK, 0))

    live = block_live > 0
    rank = jnp.cumsum(live.astype(jnp.int32)) - 1
    blocks = jnp.arange(block_live.shape[0], dtype=jnp.int32)
    hit = live[None, :] & (rank[None, :] == jnp.arange(LIVE_MOST, dtype=jnp.int32)[:, None])
    order = jnp.sum(jnp.where(hit, blocks[None, :], 0), axis=1)
    kv = pl.pallas_call(
        pack_kernel,
        out_shape=jax.ShapeDtypeStruct((heads, LIVE_MOST * BLK, 2 * HD), bf16),
        grid_spec=pltpu.PrefetchScalarGridSpec(
            num_scalar_prefetch=1,
            grid=(),
            in_specs=[pl.BlockSpec(memory_space=pltpu.VMEM)] * 2,
            out_specs=pl.BlockSpec(memory_space=pltpu.VMEM),
        ),
    )(order, refreshed, cache_values)
    kv = lax.all_to_all(kv, "zp", split_axis=0, concat_axis=0, tiled=True)
    kv = kv.reshape(heads * LIVE_MOST * BLK, 2 * HD)
    kv = lax.all_gather(kv, "zh", axis=0, tiled=True)
    kv = lax.all_gather(kv, "xh", axis=0, tiled=True)
    kvg = lax.all_gather(kv, "y", axis=0, tiled=True)
    counts = jnp.sum((live_all > 0).astype(jnp.int32), axis=1)
    sizes = tuple(lax.axis_size(a) for a in SEQ)
    counts = jnp.transpose(counts.reshape(sizes), (1, 0, 2, 3)).reshape(-1)
    upto = jnp.sum(
        jnp.where(
            jnp.arange(n_seq)[None, :] < jnp.arange(n_seq + 1)[:, None], counts[None, :], 0
        ),
        axis=1,
    )
    off = (upto * BLK).astype(jnp.int32)

    padded_ids = jnp.pad(ids_all, (PAD, PAD), constant_values=-1)
    near_ids = lax.dynamic_slice(padded_ids, (seq * tokens,), (PAD + tokens,))
    near_index = jnp.arange(PAD + tokens, dtype=jnp.int32)
    same = segment_ids[:, None] == near_ids[None, :]
    first = jnp.min(jnp.where(same, near_index[None, :], PAD + tokens), axis=1)
    own_pos = PAD + jnp.arange(tokens, dtype=jnp.int32) - first
    cosine, sine = rope_parts(own_pos)
    q = rotate(queries.astype(f32).reshape(tokens, heads, HD), cosine, sine).astype(bf16)
    k = rotate(keys_new.astype(f32).reshape(tokens, heads, HD), cosine, sine).astype(bf16)
    v = values_new.reshape(tokens, heads, HD)
    qkv = jnp.transpose(jnp.concatenate([q, k, v], axis=2), (1, 0, 2))
    ys = []
    for j in range(heads):
        part = lax.dynamic_index_in_dim(qkv, zp ^ j, 0, keepdims=False)
        ys.append(part if j == 0 else swap(part, "zp", j))
    tails = jnp.stack([y[tokens - HALO :, HD:] for y in ys])
    starts = jnp.stack([y[:HALO, HD:] for y in ys])
    up = [(i, i + heads) for i in range(n_seq - heads)]
    down = [(j, i) for i, j in up]
    left = lax.ppermute(
        lax.dynamic_index_in_dim(tails, zp ^ (heads - 1), 0, keepdims=False), SEQ, up
    )
    right = lax.ppermute(lax.dynamic_index_in_dim(starts, zp, 0, keepdims=False), SEQ, down)
    group = seq // heads
    span = heads * tokens
    group_ids = lax.dynamic_slice(padded_ids, (group * span,), (span + 2 * PAD,))
    qid = group_ids[PAD : PAD + span, None]
    kid = jnp.stack(
        [group_ids[j * tokens : j * tokens + tokens + 2 * PAD] for j in range(heads)]
    )[:, None, :]

    group_owners = lax.dynamic_slice(owners_all, (group * heads, 0), (heads, merged_rows))
    r = jnp.arange(merged_rows, dtype=jnp.int32)
    equal = group_owners[:, :, None] == group_owners[:, None, :]
    slot = jnp.sum((equal & (r[None, None, :] < r[None, :, None])).astype(jnp.int32), axis=2)
    peer = jnp.arange(heads, dtype=jnp.int32)[:, None]
    tgt = (group_owners * (heads * CAP) + peer * CAP + slot).reshape(-1)

    own_target = lax.dynamic_index_in_dim(group_owners * CAP + slot, zp, 0, keepdims=False)
    choose = (jnp.arange(n_seq * CAP, dtype=jnp.int32)[:, None] == own_target[None, :]).astype(bf16)
    width = residual.shape[1]
    res = jnp.dot(
        choose, residual.reshape(merged_rows, 4 * width), preferred_element_type=f32
    ).astype(bf16)
    res = res.reshape(n_seq, CAP * 4 * width // HD, HD)
    res = lax.all_to_all(res, SEQ, split_axis=0, concat_axis=0, tiled=True)
    res = res.reshape(n_seq * CAP * 4 * width // HD, HD)

    weights = []
    for j in range(lax.axis_size(HEAD)):
        part = lax.dynamic_slice(out_weight, (0, (head ^ j) * width), (columns, width))
        weights.append(part if j == 0 else swap(part, HEAD, j))

    sent = attend(off, tgt, zp[None].astype(jnp.int32), ys, left, right, kvg, qid, kid, n_seq * heads * CAP)
    got = lax.all_to_all(
        sent.reshape(n_seq, heads * CAP * 4, HD), SEQ, split_axis=0, concat_axis=0, tiled=True
    ).reshape(n_seq * heads * CAP * 4, HD)
    got_c = swap(got, HEAD, 1)
    got_x = swap(got, HEAD, 2)
    got_xc = swap(got_x, HEAD, 1)
    delivered = project(
        (got, got_c, got_x, got_xc), weights, res, layer_scale[None, :], n_seq * CAP
    )
    return (delivered, refreshed)


def solution(mesh):
    devices = np.asarray(mesh.devices).reshape(2, 4, 2, 4, 2, 2)
    fine = Mesh(devices, SEQ + HEAD)
    in_specs = (
        P(SEQ, HEAD),
        P(SEQ, HEAD),
        P(SEQ, HEAD),
        P(SEQ, HEAD),
        P(HEAD),
        P(HEAD, None),
        P(SEQ),
        P(SEQ, HEAD),
        P(SEQ, HEAD),
        P(SEQ),
        P(SEQ),
        P(SEQ, None),
        P(None, HEAD),
        P(SEQ, None),
    )
    out_specs = (P(SEQ, HEAD), P(SEQ, HEAD))
    return jax.shard_map(shards, mesh=fine, in_specs=in_specs, out_specs=out_specs, check_vma=False)
```

```python
import math

import jax
import jax.numpy as jnp
import numpy as np
from jax import lax
from jax.experimental import pallas as pl
from jax.experimental.pallas import tpu as pltpu
from jax.sharding import Mesh, PartitionSpec as P

HD = 128
BLK = 16
SEG_MOST = 201
LIVE_MOST = 6
CAP = 3
HALO = 208
PAD = 256
TOK = 512
KT = 2048
NEG = -1e30
SEQ = ("xh", "y", "zh", "zp")
HEAD = ("xl", "c")
bf16 = jnp.bfloat16
f32 = jnp.float32


def rope_parts(positions):
    half = HD // 2
    freqs = 100.0 ** (-jnp.arange(half, dtype=f32) / half)
    angles = positions.astype(f32)[:, None] * freqs[None, :]
    return jnp.cos(angles), jnp.sin(angles)


def rotate(vectors, cosine, sine):
    half = HD // 2
    a, b = vectors[..., :half], vectors[..., half:]
    c, s = cosine[:, None, :], sine[:, None, :]
    return jnp.concatenate([a * c - b * s, b * c + a * s], axis=-1)


def pack_kernel(idx, k_ref, v_ref, out_ref):
    heads = out_ref.shape[0]
    for j in range(LIVE_MOST):
        rows = pl.ds(pl.multiple_of(idx[j] * BLK, BLK), BLK)
        k = k_ref[rows, :]
        v = v_ref[rows, :]
        for p in range(heads):
            out_ref[p, j * BLK : (j + 1) * BLK, :HD] = k[:, p * HD : (p + 1) * HD]
            out_ref[p, j * BLK : (j + 1) * BLK, HD:] = v[:, p * HD : (p + 1) * HD]


def rope_kernel(q_ref, k_ref, v_ref, c_ref, s_ref, out_ref):
    c = c_ref[...]
    s = s_ref[...]
    for h in range(out_ref.shape[0]):
        cols = slice(h * HD, (h + 1) * HD)
        for j, ref in enumerate((q_ref, k_ref)):
            x = ref[:, cols].astype(f32)
            turned = x * c + pltpu.roll(x, HD // 2, 1) * s
            out_ref[h, :, j * HD : (j + 1) * HD] = turned.astype(bf16)
        out_ref[h, :, 2 * HD :] = v_ref[:, cols]


def attention_kernel(off, tgt, zp, *refs):
    chunks = 4
    ys = refs[:chunks]
    left, right, ids = refs[chunks : chunks + 3]
    pieces = refs[chunks + 3 : -13]
    out, kc, vc, qs, kw, vw, ob, send, mx, ac, idcol, gathered, sems = refs[-13:]
    i = pl.program_id(0)
    sources = off.shape[0] - 1
    slot_rows = LIVE_MOST * BLK
    coef = math.log2(math.e) / math.sqrt(HD)
    total = off[sources]

    @pl.when(i == 0)
    def _():
        copies = []
        row = 0
        for n, piece in enumerate(pieces):
            to = gathered.at[pl.ds(row, piece.shape[0])]
            copies.append(pltpu.make_async_copy(piece, to, sems.at[n]))
            row += piece.shape[0]
        for copy in copies:
            copy.start()
        vc[:, HD:] = jnp.ones((vc.shape[0], HD), bf16)
        vw[:, HD:] = jnp.ones((vw.shape[0], HD), bf16)
        for k, y in enumerate(ys):
            chunk = zp[0] ^ k
            dst = pl.ds(pl.multiple_of(chunk * TOK, TOK), TOK)
            qs[dst, :] = y[:, :HD]
            dst = pl.ds(pl.multiple_of(PAD + chunk * TOK, PAD), TOK)
            kw[dst, :] = y[:, HD : 2 * HD]
            vw[dst, :HD] = y[:, 2 * HD :]
        end = PAD + chunks * TOK
        gap = PAD - HALO
        kw[:gap, :] = jnp.zeros((gap, HD), bf16)
        vw[:gap, :HD] = jnp.zeros((gap, HD), bf16)
        kw[gap:PAD, :] = left[:, :HD]
        vw[gap:PAD, :HD] = left[:, HD:]
        kw[end : end + HALO, :] = right[:, :HD]
        vw[end : end + HALO, :HD] = right[:, HD:]
        kw[end + HALO :, :] = jnp.zeros((gap, HD), bf16)
        vw[end + HALO :, :HD] = jnp.zeros((gap, HD), bf16)
        send[...] = jnp.zeros(send.shape, f32)
        for copy in copies:
            copy.wait()

        def copy_source(s, carry):
            dst = pl.ds(pl.multiple_of(off[s], BLK), slot_rows)
            src = pl.ds(pl.multiple_of(s * slot_rows, BLK), slot_rows)
            kc[dst, :] = gathered[src, :HD]
            vc[dst, :HD] = gathered[src, HD:]
            return carry

        lax.fori_loop(0, sources, copy_source, 0, unroll=2)
        tail = pl.ds(pl.multiple_of(total, BLK), KT)
        kc[tail, :] = jnp.zeros((KT, HD), bf16)
        vc[tail, :HD] = jnp.zeros((KT, HD), bf16)

    base = pl.multiple_of(i * TOK, TOK)
    sub = 128
    parts = TOK // sub
    wide = sub + 2 * PAD
    for b in range(parts):
        line = ids[:, pl.ds(pl.multiple_of(base + PAD + b * sub, sub), sub)]
        idcol[b * sub : (b + 1) * sub, :] = jnp.transpose(jnp.broadcast_to(line, (sub, sub)))

    def scores(b, keys):
        q = qs[pl.ds(pl.multiple_of(base + b * sub, sub), sub), :]
        return lax.dot_general(q, keys, (((1,), (1,)), ((), ())), preferred_element_type=f32)

    def weigh(s, m):
        new = jnp.max(s, axis=1, keepdims=True)
        if m is not None:
            new = jnp.maximum(m, new)
        return new, jnp.exp2(s * coef - new * coef).astype(bf16)

    for b in range(parts):
        rows = pl.ds(pl.multiple_of(base + b * sub, sub), wide)
        s = scores(b, kw[rows, :])
        near = ids[:, rows]
        s = jnp.where(idcol[b * sub : (b + 1) * sub, :1] == near, s, NEG)
        new, w = weigh(s, None)
        mx[b * sub : (b + 1) * sub, :] = new
        ac[b * sub : (b + 1) * sub, :] = jnp.dot(w, vw[rows, :], preferred_element_type=f32)

    def visit(start, size, masked):
        rows = pl.ds(pl.multiple_of(start, size // 2), size)
        keys, values = kc[rows, :], vc[rows, :]

        def rows_of(b, carry):
            s = scores(b, keys)
            if masked:
                col = lax.broadcasted_iota(jnp.int32, s.shape, 1)
                s = jnp.where(col < total - start, s, NEG)
            here = pl.ds(pl.multiple_of(b * sub, sub), sub)
            m = mx[here, :]
            new, w = weigh(s, m)
            mx[here, :] = new
            part = jnp.dot(w, values, preferred_element_type=f32)
            ac[here, :] = ac[here, :] * jnp.exp2((m - new) * coef) + part
            return carry

        lax.fori_loop(0, parts, rows_of, 0, unroll=2 if masked else True)

    def loop(j, carry):
        visit(j * KT, KT, False)
        return carry

    full = total // KT
    rest = total - full * KT
    lax.fori_loop(0, full, loop, 0)

    @pl.when(rest > KT // 2)
    def _():
        visit(full * KT, KT, True)

    @pl.when((rest > 0) & (rest <= KT // 2))
    def _():
        visit(full * KT, KT // 2, True)

    ob[...] = ac[:, :HD] / ac[:, HD:]

    def place(r, carry):
        dst = tgt[i * (TOK // 4) + r] * 4
        send[pl.ds(pl.multiple_of(dst, 4), 4), :] = ob[pl.ds(pl.multiple_of(r * 4, 4), 4), :]
        return carry

    lax.fori_loop(0, TOK // 4, place, 0, unroll=8)

    @pl.when(i == pl.num_programs(0) - 1)
    def _():
        out[...] = send[...].astype(bf16)


def attend(off, tgt, zp, ys, left, right, ids, pieces, slots):
    chunks = len(ys)
    sources = off.shape[0] - 1
    cache_most = sources * LIVE_MOST * BLK
    whole = pl.BlockSpec(memory_space=pltpu.VMEM)
    return pl.pallas_call(
        attention_kernel,
        out_shape=jax.ShapeDtypeStruct((slots * 4, HD), bf16),
        grid_spec=pltpu.PrefetchScalarGridSpec(
            num_scalar_prefetch=3,
            grid=(chunks,),
            in_specs=[whole] * (chunks + 3)
            + [pl.BlockSpec(memory_space=pl.ANY)] * len(pieces),
            out_specs=whole,
            scratch_shapes=[
                pltpu.VMEM((cache_most + KT, HD), bf16),
                pltpu.VMEM((cache_most + KT, 2 * HD), bf16),
                pltpu.VMEM((chunks * TOK, HD), bf16),
                pltpu.VMEM((chunks * TOK + 2 * PAD, HD), bf16),
                pltpu.VMEM((chunks * TOK + 2 * PAD, 2 * HD), bf16),
                pltpu.VMEM((TOK, HD), f32),
                pltpu.VMEM((slots * 4, HD), f32),
                pltpu.VMEM((TOK, 1), f32),
                pltpu.VMEM((TOK, 2 * HD), f32),
                pltpu.VMEM((TOK, 128), f32),
                pltpu.VMEM((cache_most, 2 * HD), bf16),
                pltpu.SemaphoreType.DMA((len(pieces),)),
            ],
        ),
        compiler_params=pltpu.CompilerParams(
            dimension_semantics=("arbitrary",), vmem_limit_bytes=48 << 20
        ),
        cost_estimate=pl.CostEstimate(
            flops=4 * 2048 * 7168 * 128, bytes_accessed=8 << 20, transcendentals=2048 * 7168
        ),
    )(off, tgt, zp, *ys, left, right, ids, *pieces)


def project_kernel(core, a0, a1, a2, a3, weights, res, scale, mix, out, att, pick):
    b = pl.program_id(0)
    c = core[1]
    groups = a0.shape[0] // (8 * 48)

    @pl.when(b == 0)
    def _():
        slot = lax.broadcasted_iota(jnp.int32, pick.shape, 0)
        row = lax.broadcasted_iota(jnp.int32, pick.shape, 1)
        slots = out.shape[0]
        pick[...] = (row == (slot % slots) * 4 + slot // slots).astype(bf16)
        for k, a in enumerate((a0, a1, a2, a3)):

            def move(g, carry):
                to = pl.ds(pl.multiple_of((g * 2 + (c ^ (k % 2))) * 48, 16), 48)
                for p in range(8):
                    block = (core[0] ^ (k // 2)) * 2 + p // 4
                    src = pl.ds(pl.multiple_of(g * 384 + p * 48, 16), 48)
                    att[block, to, (p % 4) * HD : (p % 4 + 1) * HD] = a[src, :]
                return carry

            lax.fori_loop(0, groups, move, 0)

    total = None
    for k in range(4):
        part = jnp.dot(att[k], weights[k], preferred_element_type=f32)
        total = part if total is None else total + part
    layer = (res[...].astype(f32) + total * scale[...]).astype(bf16)
    turns = jnp.dot(pick[...], layer, preferred_element_type=f32).astype(bf16)
    slots = out.shape[0]
    for d in range(weights.shape[2] // HD):
        cols = slice(d * HD, (d + 1) * HD)
        rows = jnp.concatenate([turns[t * slots : (t + 1) * slots, cols] for t in range(4)], axis=1)
        out[:, d * 4 * HD : (d + 1) * 4 * HD] = jnp.dot(
            rows, mix[...], preferred_element_type=f32
        ).astype(bf16)


def project(core, atts, weights, res, scale, slots):
    width = weights.shape[2]
    part = 256
    whole = pl.BlockSpec(memory_space=pltpu.VMEM)
    source = np.arange(4 * HD)
    mix = np.zeros((4 * HD, 4 * HD), np.float32)
    mix[source, (source % HD) * 4 + source // HD] = 1.0
    return pl.pallas_call(
        project_kernel,
        out_shape=jax.ShapeDtypeStruct((slots, 4 * width), bf16),
        grid_spec=pltpu.PrefetchScalarGridSpec(
            num_scalar_prefetch=1,
            grid=(width // part,),
            in_specs=[whole] * 4
            + [pl.BlockSpec((*weights.shape[:2], part), lambda b, *_: (0, 0, b))]
            + [pl.BlockSpec((slots * 4, part), lambda b, *_: (0, b)), pl.BlockSpec((1, part), lambda b, *_: (0, b)), whole],
            out_specs=pl.BlockSpec((slots, 4 * part), lambda b, *_: (0, b)),
            scratch_shapes=[
                pltpu.VMEM((4, slots * 4, 4 * HD), bf16),
                pltpu.VMEM((slots * 4, slots * 4), bf16),
            ],
        ),
        compiler_params=pltpu.CompilerParams(
            dimension_semantics=("arbitrary",), vmem_limit_bytes=48 << 20
        ),
        cost_estimate=pl.CostEstimate(
            flops=2 * 768 * 2048 * 1024, bytes_accessed=16 << 20, transcendentals=0
        ),
    )(core, *atts, weights, res, scale, jnp.asarray(mix, bf16))


def swap(x, axis, k):
    n = lax.axis_size(axis)
    return lax.ppermute(x, axis, [(i, i ^ k) for i in range(n)])


def tie(x, *others):
    return lax.optimization_barrier((x, *others))[0]


def shards(
    queries,
    keys_new,
    values_new,
    residual,
    layer_scale,
    out_weight,
    segment_ids,
    cache_keys,
    cache_values,
    block_live,
    recompute_block,
    recompute_hidden,
    key_weight,
    owners,
):
    tokens, columns = queries.shape
    heads = columns // HD
    n_head = lax.axis_size(HEAD)
    n_seq = lax.axis_size(SEQ)
    seq = lax.axis_index(SEQ)
    xh, y, zp, xl, c = (lax.axis_index(n) for n in ("xh", "y", "zp", "xl", "c"))
    head = lax.axis_index(HEAD)
    merged_rows = tokens // 4
    group = (xh * 4 + y) * 2 + c
    n_group = n_seq // heads
    whole = pl.BlockSpec(memory_space=pltpu.VMEM)

    marks = segment_ids + 1
    n_blocks = block_live.shape[0]
    meta = jnp.concatenate(
        [marks, owners[:, 0], block_live, jnp.zeros((128 - n_blocks,), jnp.int32)]
    )
    meta = jnp.broadcast_to(meta[None, None, :], (n_seq, 1, meta.shape[0]))
    meta = lax.all_to_all(meta, SEQ, split_axis=0, concat_axis=0, tiled=True)[:, 0, :]
    marks_all = jnp.pad(meta[:, :tokens].reshape(-1), (PAD, PAD))

    near = lax.dynamic_slice(marks_all, (seq * tokens,), (PAD + tokens,))
    same = marks[:, None] == near[None, :]
    index = jnp.arange(PAD + tokens, dtype=jnp.int32)
    first = jnp.min(jnp.where(same, index[None, :], PAD + tokens), axis=1)
    cosine, sine = rope_parts(PAD + jnp.arange(tokens, dtype=jnp.int32) - first)

    qkv = pl.pallas_call(
        rope_kernel,
        out_shape=jax.ShapeDtypeStruct((heads, tokens, 3 * HD), bf16),
        in_specs=[whole] * 5,
        out_specs=whole,
    )(
        queries,
        keys_new,
        values_new,
        jnp.concatenate([cosine, cosine], axis=1),
        jnp.concatenate([-sine, sine], axis=1),
    )

    cache_rows = cache_keys.shape[0]
    block = recompute_block[0]
    fresh = jnp.dot(recompute_hidden, key_weight, preferred_element_type=f32)
    fresh_rows = seq * cache_rows + block * BLK + jnp.arange(BLK, dtype=jnp.int32)
    fresh = rotate(fresh.reshape(BLK, heads, HD), *rope_parts(fresh_rows % SEG_MOST))
    fresh = fresh.reshape(BLK, columns).astype(bf16)
    refreshed = lax.dynamic_update_slice(cache_keys, fresh, (block * BLK, 0))

    live = block_live > 0
    blocks = jnp.arange(n_blocks, dtype=jnp.int32)
    rank = jnp.sum(jnp.where(blocks[None, :] < blocks[:, None], live[None, :], False), axis=1)
    hit = live[None, :] & (rank[None, :] == jnp.arange(LIVE_MOST, dtype=jnp.int32)[:, None])
    order = jnp.sum(jnp.where(hit, blocks[None, :], 0), axis=1)
    kv = pl.pallas_call(
        pack_kernel,
        out_shape=jax.ShapeDtypeStruct((heads, LIVE_MOST * BLK, 2 * HD), bf16),
        grid_spec=pltpu.PrefetchScalarGridSpec(
            num_scalar_prefetch=1, grid=(), in_specs=[whole] * 2, out_specs=whole
        ),
    )(order, refreshed, cache_values)

    def spread(x, j):
        pairs = []
        for a in range(2):
            for b in range(heads):
                for d in range(2):
                    pairs.append(((a * heads + b) * 2 + d, (d * heads + (b ^ j)) * 2 + a))
        part = lax.dynamic_index_in_dim(x, zp ^ j, 0, keepdims=False)
        return lax.ppermute(part, ("zh", "zp", "c"), pairs)

    kv4 = jnp.concatenate([spread(kv, j) for j in range(heads)], axis=0)
    ys = [spread(qkv, j) for j in range(heads)]

    kv4 = tie(kv4, qkv)
    kv8 = jnp.concatenate([kv4, swap(kv4, "xh", 1)], axis=0)
    kv32 = lax.all_gather(kv8, "y", axis=0, tiled=True)
    pieces = [kv32, swap(kv32, "c", 1)]

    owners_all = meta[:, tokens : tokens + merged_rows]
    live_all = meta[:, tokens + merged_rows : tokens + merged_rows + n_blocks]
    counts = jnp.sum((live_all > 0).astype(jnp.int32), axis=1)
    j4 = jnp.arange(heads, dtype=jnp.int32) ^ zp
    x2 = jnp.arange(2, dtype=jnp.int32) ^ xh
    y4 = jnp.arange(4, dtype=jnp.int32)
    c2 = jnp.arange(2, dtype=jnp.int32) ^ c
    arrival = (
        (x2[None, None, :, None] * 4 + y4[None, :, None, None]) * 2 + c2[:, None, None, None]
    ) * heads + j4[None, None, None, :]
    arrival = arrival.reshape(-1)
    every = jnp.arange(n_seq, dtype=jnp.int32)
    counts = jnp.sum(jnp.where(arrival[:, None] == every[None, :], counts[None, :], 0), axis=1)
    ends = jnp.arange(n_seq + 1, dtype=jnp.int32)
    off = jnp.sum(jnp.where(every[None, :] < ends[:, None], counts[None, :] * BLK, 0), axis=1)

    tails = jnp.stack([t[tokens - HALO :, HD:] for t in ys])
    starts = jnp.stack([t[:HALO, HD:] for t in ys])
    ahead = [(i, i + 1) for i in range(n_group - 1)]
    left = lax.ppermute(
        lax.dynamic_index_in_dim(tails, zp ^ (heads - 1), 0, keepdims=False),
        ("xh", "y", "c"),
        ahead,
    )
    right = lax.ppermute(
        lax.dynamic_index_in_dim(starts, zp, 0, keepdims=False),
        ("xh", "y", "c"),
        [(j, i) for i, j in ahead],
    )
    span = heads * tokens
    ids = lax.dynamic_slice(
        marks_all, (group * span,), (span + 2 * PAD,)
    )
    ids = ids.astype(f32)[None, :]

    def slots_of(owner_rows):
        r = jnp.arange(merged_rows, dtype=jnp.int32)
        equal = owner_rows[:, :, None] == owner_rows[:, None, :]
        return jnp.sum((equal & (r[None, None, :] < r[None, :, None])).astype(jnp.int32), axis=2)

    group_owners = lax.dynamic_slice(owners_all, (group * heads, 0), (heads, merged_rows))
    peer = jnp.arange(heads, dtype=jnp.int32)[:, None]
    tgt = (group_owners * (heads * CAP) + peer * CAP + slots_of(group_owners)).reshape(-1)

    width = residual.shape[1]
    weights = out_weight.reshape(columns, n_head, width).transpose(1, 0, 2)
    weights = lax.all_to_all(tie(weights, kv4), HEAD, split_axis=0, concat_axis=0, tiled=True)

    own_target = owners[:, 0] * CAP + slots_of(owners[:, 0][None, :])[0]
    choose = (jnp.arange(n_seq * CAP, dtype=jnp.int32)[:, None] == own_target[None, :]).astype(bf16)
    width = residual.shape[1]
    res = jnp.dot(
        choose, residual.reshape(merged_rows, 4 * width), preferred_element_type=f32
    ).astype(bf16)
    res = res.reshape(n_seq, CAP * 4 * width // HD, HD)
    res = lax.all_to_all(tie(res, kv32, weights, *ys), SEQ, split_axis=0, concat_axis=0, tiled=True)
    res = res.reshape(n_seq * CAP * 4, width)

    one = zp[None].astype(jnp.int32)
    sent = attend(off, tgt, one, ys, left, right, ids, pieces, n_seq * heads * CAP)
    sent, res, weights = lax.optimization_barrier((sent, res, weights))
    got = lax.all_to_all(
        sent.reshape(n_seq, heads * CAP * 4, HD), SEQ, split_axis=0, concat_axis=0, tiled=True
    ).reshape(n_seq * heads * CAP * 4, HD)
    got_c = swap(got, HEAD, 1)
    got_x = swap(got, HEAD, 2)
    got_xc = swap(got_x, HEAD, 1)
    delivered = project(
        jnp.stack([xl, c]).astype(jnp.int32),
        (got, got_c, got_x, got_xc),
        weights,
        res,
        layer_scale[None, :],
        n_seq * CAP,
    )
    return (delivered, refreshed)


def solution(mesh):
    devices = np.asarray(mesh.devices).reshape(2, 4, 2, 4, 2, 2)
    fine = Mesh(devices, SEQ + HEAD)
    in_specs = (
        P(SEQ, HEAD),
        P(SEQ, HEAD),
        P(SEQ, HEAD),
        P(SEQ, HEAD),
        P(HEAD),
        P(HEAD, None),
        P(SEQ),
        P(SEQ, HEAD),
        P(SEQ, HEAD),
        P(SEQ),
        P(SEQ),
        P(SEQ, None),
        P(None, HEAD),
        P(SEQ, None),
    )
    out_specs = (P(SEQ, HEAD), P(SEQ, HEAD))
    return jax.shard_map(shards, mesh=fine, in_specs=in_specs, out_specs=out_specs, check_vma=False)
```

```python
import math

import jax
import jax.numpy as jnp
import numpy as np
from jax import lax
from jax.experimental import pallas as pl
from jax.experimental.pallas import tpu as pltpu
from jax.sharding import Mesh, PartitionSpec as P

HD = 128
BLK = 16
SEG_MOST = 201
LIVE_MOST = 6
CAP = 3
HALO = 208
PAD = 256
TOK = 512
KT = 2048
NEG = -1e30
SEQ = ("xh", "y", "zh", "zp")
HEAD = ("xl", "c")
bf16 = jnp.bfloat16
f32 = jnp.float32


def rope_parts(positions):
    half = HD // 2
    freqs = 100.0 ** (-jnp.arange(half, dtype=f32) / half)
    angles = positions.astype(f32)[:, None] * freqs[None, :]
    return jnp.cos(angles), jnp.sin(angles)


def rotate(vectors, cosine, sine):
    half = HD // 2
    a, b = vectors[..., :half], vectors[..., half:]
    c, s = cosine[:, None, :], sine[:, None, :]
    return jnp.concatenate([a * c - b * s, b * c + a * s], axis=-1)


def pack_kernel(idx, k_ref, v_ref, out_ref):
    heads = out_ref.shape[0]
    for j in range(LIVE_MOST):
        rows = pl.ds(pl.multiple_of(idx[j] * BLK, BLK), BLK)
        k = k_ref[rows, :]
        v = v_ref[rows, :]
        for p in range(heads):
            out_ref[p, j * BLK : (j + 1) * BLK, :HD] = k[:, p * HD : (p + 1) * HD]
            out_ref[p, j * BLK : (j + 1) * BLK, HD:] = v[:, p * HD : (p + 1) * HD]


def rope_kernel(q_ref, k_ref, v_ref, c_ref, s_ref, out_ref):
    c = c_ref[...]
    s = s_ref[...]
    for h in range(out_ref.shape[0]):
        cols = slice(h * HD, (h + 1) * HD)
        for j, ref in enumerate((q_ref, k_ref)):
            x = ref[:, cols].astype(f32)
            turned = x * c + pltpu.roll(x, HD // 2, 1) * s
            out_ref[h, :, j * HD : (j + 1) * HD] = turned.astype(bf16)
        out_ref[h, :, 2 * HD :] = v_ref[:, cols]


def attention_kernel(off, tgt, zp, *refs):
    chunks = 4
    ys = refs[:chunks]
    left, right, ids = refs[chunks : chunks + 3]
    pieces = refs[chunks + 3 : -13]
    out, kc, vc, qs, kw, vw, ob, send, mx, ac, idcol, gathered, sems = refs[-13:]
    i = pl.program_id(0)
    sources = off.shape[0] - 1
    slot_rows = LIVE_MOST * BLK
    coef = math.log2(math.e) / math.sqrt(HD)
    total = off[sources]

    @pl.when(i == 0)
    def _():
        copies = []
        row = 0
        for n, piece in enumerate(pieces):
            to = gathered.at[pl.ds(row, piece.shape[0])]
            copies.append(pltpu.make_async_copy(piece, to, sems.at[n]))
            row += piece.shape[0]
        for copy in copies:
            copy.start()
        vc[:, HD:] = jnp.ones((vc.shape[0], HD), bf16)
        vw[:, HD:] = jnp.ones((vw.shape[0], HD), bf16)
        for k, y in enumerate(ys):
            chunk = zp[0] ^ k
            dst = pl.ds(pl.multiple_of(chunk * TOK, TOK), TOK)
            qs[dst, :] = y[:, :HD]
            dst = pl.ds(pl.multiple_of(PAD + chunk * TOK, PAD), TOK)
            kw[dst, :] = y[:, HD : 2 * HD]
            vw[dst, :HD] = y[:, 2 * HD :]
        end = PAD + chunks * TOK
        gap = PAD - HALO
        kw[:gap, :] = jnp.zeros((gap, HD), bf16)
        vw[:gap, :HD] = jnp.zeros((gap, HD), bf16)
        kw[gap:PAD, :] = left[:, :HD]
        vw[gap:PAD, :HD] = left[:, HD:]
        kw[end : end + HALO, :] = right[:, :HD]
        vw[end : end + HALO, :HD] = right[:, HD:]
        kw[end + HALO :, :] = jnp.zeros((gap, HD), bf16)
        vw[end + HALO :, :HD] = jnp.zeros((gap, HD), bf16)
        send[...] = jnp.zeros(send.shape, f32)
        for copy in copies:
            copy.wait()

        def copy_source(s, carry):
            dst = pl.ds(pl.multiple_of(off[s], BLK), slot_rows)
            src = pl.ds(pl.multiple_of(s * slot_rows, BLK), slot_rows)
            kc[dst, :] = gathered[src, :HD]
            vc[dst, :HD] = gathered[src, HD:]
            return carry

        lax.fori_loop(0, sources, copy_source, 0, unroll=2)
        tail = pl.ds(pl.multiple_of(total, BLK), KT)
        kc[tail, :] = jnp.zeros((KT, HD), bf16)
        vc[tail, :HD] = jnp.zeros((KT, HD), bf16)

    base = pl.multiple_of(i * TOK, TOK)
    sub = 128
    parts = TOK // sub
    wide = sub + 2 * PAD
    for b in range(parts):
        line = ids[:, pl.ds(pl.multiple_of(base + PAD + b * sub, sub), sub)]
        idcol[b * sub : (b + 1) * sub, :] = jnp.transpose(jnp.broadcast_to(line, (sub, sub)))

    def scores(b, keys):
        q = qs[pl.ds(pl.multiple_of(base + b * sub, sub), sub), :]
        return lax.dot_general(q, keys, (((1,), (1,)), ((), ())), preferred_element_type=f32)

    def weigh(s, m):
        new = jnp.max(s, axis=1, keepdims=True)
        if m is not None:
            new = jnp.maximum(m, new)
        return new, jnp.exp2(s * coef - new * coef).astype(bf16)

    for b in range(parts):
        rows = pl.ds(pl.multiple_of(base + b * sub, sub), wide)
        s = scores(b, kw[rows, :])
        near = ids[:, rows]
        s = jnp.where(idcol[b * sub : (b + 1) * sub, :1] == near, s, NEG)
        new, w = weigh(s, None)
        mx[b * sub : (b + 1) * sub, :] = new
        ac[b * sub : (b + 1) * sub, :] = jnp.dot(w, vw[rows, :], preferred_element_type=f32)

    def visit(start, size, masked):
        rows = pl.ds(pl.multiple_of(start, size // 2), size)
        keys, values = kc[rows, :], vc[rows, :]

        def rows_of(b, carry):
            s = scores(b, keys)
            if masked:
                col = lax.broadcasted_iota(jnp.int32, s.shape, 1)
                s = jnp.where(col < total - start, s, NEG)
            here = pl.ds(pl.multiple_of(b * sub, sub), sub)
            m = mx[here, :]
            new, w = weigh(s, m)
            mx[here, :] = new
            part = jnp.dot(w, values, preferred_element_type=f32)
            ac[here, :] = ac[here, :] * jnp.exp2((m - new) * coef) + part
            return carry

        lax.fori_loop(0, parts, rows_of, 0, unroll=2 if masked else True)

    def loop(j, carry):
        visit(j * KT, KT, False)
        return carry

    full = total // KT
    rest = total - full * KT
    lax.fori_loop(0, full, loop, 0)

    @pl.when(rest > KT // 2)
    def _():
        visit(full * KT, KT, True)

    @pl.when((rest > 0) & (rest <= KT // 2))
    def _():
        visit(full * KT, KT // 2, True)

    ob[...] = ac[:, :HD] / ac[:, HD:]

    def place(r, carry):
        dst = tgt[i * (TOK // 4) + r] * 4
        send[pl.ds(pl.multiple_of(dst, 4), 4), :] = ob[pl.ds(pl.multiple_of(r * 4, 4), 4), :]
        return carry

    lax.fori_loop(0, TOK // 4, place, 0, unroll=8)

    @pl.when(i == pl.num_programs(0) - 1)
    def _():
        out[...] = send[...].astype(bf16)


def attend(off, tgt, zp, ys, left, right, ids, pieces, slots):
    chunks = len(ys)
    sources = off.shape[0] - 1
    cache_most = sources * LIVE_MOST * BLK
    whole = pl.BlockSpec(memory_space=pltpu.VMEM)
    return pl.pallas_call(
        attention_kernel,
        out_shape=jax.ShapeDtypeStruct((slots * 4, HD), bf16),
        grid_spec=pltpu.PrefetchScalarGridSpec(
            num_scalar_prefetch=3,
            grid=(chunks,),
            in_specs=[whole] * (chunks + 3)
            + [pl.BlockSpec(memory_space=pl.ANY)] * len(pieces),
            out_specs=whole,
            scratch_shapes=[
                pltpu.VMEM((cache_most + KT, HD), bf16),
                pltpu.VMEM((cache_most + KT, 2 * HD), bf16),
                pltpu.VMEM((chunks * TOK, HD), bf16),
                pltpu.VMEM((chunks * TOK + 2 * PAD, HD), bf16),
                pltpu.VMEM((chunks * TOK + 2 * PAD, 2 * HD), bf16),
                pltpu.VMEM((TOK, HD), f32),
                pltpu.VMEM((slots * 4, HD), f32),
                pltpu.VMEM((TOK, 1), f32),
                pltpu.VMEM((TOK, 2 * HD), f32),
                pltpu.VMEM((TOK, 128), f32),
                pltpu.VMEM((cache_most, 2 * HD), bf16),
                pltpu.SemaphoreType.DMA((len(pieces),)),
            ],
        ),
        compiler_params=pltpu.CompilerParams(
            dimension_semantics=("arbitrary",), vmem_limit_bytes=48 << 20
        ),
        cost_estimate=pl.CostEstimate(
            flops=4 * 2048 * 7168 * 128, bytes_accessed=8 << 20, transcendentals=2048 * 7168
        ),
    )(off, tgt, zp, *ys, left, right, ids, *pieces)


def project_kernel(core, a0, a1, a2, a3, w0, w1, w2, w3, res, scale, mix, out, att, res32, proj):
    b = pl.program_id(0)
    c = core[0]
    groups = a0.shape[0] // (8 * 48)

    @pl.when(b == 0)
    def _():
        res32[...] = res[...].astype(f32)
        for k, a in enumerate((a0, a1, a2, a3)):

            def move(g, carry):
                to = pl.ds(pl.multiple_of((g * 2 + (c ^ (k % 2))) * 48, 16), 48)
                for p in range(8):
                    block = (k // 2) * 2 + (c ^ (p // 4))
                    src = pl.ds(pl.multiple_of(g * 384 + p * 48, 16), 48)
                    att[block, to, (p % 4) * HD : (p % 4 + 1) * HD] = a[src, :]
                return carry

            lax.fori_loop(0, groups, move, 0)

    total = None
    for k, w in enumerate((w0, w1, w2, w3)):
        part = jnp.dot(att[k], w[...], preferred_element_type=f32)
        total = part if total is None else total + part
    total = total * scale[...]
    slots = out.shape[0]
    per = w0.shape[1] // HD
    for d in range(per):
        proj[d * 4 * slots : (d + 1) * 4 * slots, :] = total[:, d * HD : (d + 1) * HD]
    for d in range(per):
        parts = []
        for t in range(4):
            new = proj[pl.ds(d * 4 * slots + t, slots, stride=4), :]
            old = res32[pl.ds(t * 8 + b * per + d, slots, stride=32), :]
            parts.append((old + new).astype(bf16))
        rows = jnp.concatenate(parts, axis=1)
        out[:, d * 4 * HD : (d + 1) * 4 * HD] = jnp.dot(
            rows, mix[...], preferred_element_type=f32
        ).astype(bf16)


def project(core, atts, weights, res, scale, slots):
    width = weights[0].shape[1]
    part = 256
    whole = pl.BlockSpec(memory_space=pltpu.VMEM)
    source = np.arange(4 * HD)
    mix = np.zeros((4 * HD, 4 * HD), np.float32)
    mix[source, (source % HD) * 4 + source // HD] = 1.0
    return pl.pallas_call(
        project_kernel,
        out_shape=jax.ShapeDtypeStruct((slots, 4 * width), bf16),
        grid_spec=pltpu.PrefetchScalarGridSpec(
            num_scalar_prefetch=1,
            grid=(width // part,),
            in_specs=[whole] * 4
            + [pl.BlockSpec((weights[0].shape[0], part), lambda b, *_: (0, b))] * 4
            + [whole, pl.BlockSpec((1, part), lambda b, *_: (0, b)), whole],
            out_specs=pl.BlockSpec((slots, 4 * part), lambda b, *_: (0, b)),
            scratch_shapes=[
                pltpu.VMEM((4, slots * 4, 4 * HD), bf16),
                pltpu.VMEM((slots * 32, HD), f32),
                pltpu.VMEM((slots * 4 * part // HD, HD), f32),
            ],
        ),
        compiler_params=pltpu.CompilerParams(
            dimension_semantics=("arbitrary",), vmem_limit_bytes=48 << 20
        ),
        cost_estimate=pl.CostEstimate(
            flops=2 * 768 * 2048 * 1024, bytes_accessed=16 << 20, transcendentals=0
        ),
    )(core, *atts, *weights, res, scale, jnp.asarray(mix, bf16))


def swap(x, axis, k):
    n = lax.axis_size(axis)
    return lax.ppermute(x, axis, [(i, i ^ k) for i in range(n)])


def tie(x, *others):
    return lax.optimization_barrier((x, *others))[0]


def shards(
    queries,
    keys_new,
    values_new,
    residual,
    layer_scale,
    out_weight,
    segment_ids,
    cache_keys,
    cache_values,
    block_live,
    recompute_block,
    recompute_hidden,
    key_weight,
    owners,
):
    tokens, columns = queries.shape
    heads = columns // HD
    n_seq = lax.axis_size(SEQ)
    seq = lax.axis_index(SEQ)
    xh, y, zp, c = (lax.axis_index(n) for n in ("xh", "y", "zp", "c"))
    head = lax.axis_index(HEAD)
    merged_rows = tokens // 4
    group = (xh * 4 + y) * 2 + c
    n_group = n_seq // heads
    whole = pl.BlockSpec(memory_space=pltpu.VMEM)

    marks = segment_ids + 1
    n_blocks = block_live.shape[0]
    meta = jnp.concatenate(
        [marks, owners[:, 0], block_live, jnp.zeros((128 - n_blocks,), jnp.int32)]
    )
    meta = jnp.broadcast_to(meta[None, None, :], (n_seq, 1, meta.shape[0]))
    meta = lax.all_to_all(meta, SEQ, split_axis=0, concat_axis=0, tiled=True)[:, 0, :]
    marks_all = jnp.pad(meta[:, :tokens].reshape(-1), (PAD, PAD))

    near = lax.dynamic_slice(marks_all, (seq * tokens,), (PAD + tokens,))
    same = marks[:, None] == near[None, :]
    index = jnp.arange(PAD + tokens, dtype=jnp.int32)
    first = jnp.min(jnp.where(same, index[None, :], PAD + tokens), axis=1)
    cosine, sine = rope_parts(PAD + jnp.arange(tokens, dtype=jnp.int32) - first)

    qkv = pl.pallas_call(
        rope_kernel,
        out_shape=jax.ShapeDtypeStruct((heads, tokens, 3 * HD), bf16),
        in_specs=[whole] * 5,
        out_specs=whole,
    )(
        queries,
        keys_new,
        values_new,
        jnp.concatenate([cosine, cosine], axis=1),
        jnp.concatenate([-sine, sine], axis=1),
    )

    cache_rows = cache_keys.shape[0]
    block = recompute_block[0]
    fresh = jnp.dot(recompute_hidden, key_weight, preferred_element_type=f32)
    fresh_rows = seq * cache_rows + block * BLK + jnp.arange(BLK, dtype=jnp.int32)
    fresh = rotate(fresh.reshape(BLK, heads, HD), *rope_parts(fresh_rows % SEG_MOST))
    fresh = fresh.reshape(BLK, columns).astype(bf16)
    refreshed = lax.dynamic_update_slice(cache_keys, fresh, (block * BLK, 0))

    live = block_live > 0
    blocks = jnp.arange(n_blocks, dtype=jnp.int32)
    rank = jnp.sum(jnp.where(blocks[None, :] < blocks[:, None], live[None, :], False), axis=1)
    hit = live[None, :] & (rank[None, :] == jnp.arange(LIVE_MOST, dtype=jnp.int32)[:, None])
    order = jnp.sum(jnp.where(hit, blocks[None, :], 0), axis=1)
    kv = pl.pallas_call(
        pack_kernel,
        out_shape=jax.ShapeDtypeStruct((heads, LIVE_MOST * BLK, 2 * HD), bf16),
        grid_spec=pltpu.PrefetchScalarGridSpec(
            num_scalar_prefetch=1, grid=(), in_specs=[whole] * 2, out_specs=whole
        ),
    )(order, refreshed, cache_values)

    def spread(x, j):
        pairs = []
        for a in range(2):
            for b in range(heads):
                for d in range(2):
                    pairs.append(((a * heads + b) * 2 + d, (d * heads + (b ^ j)) * 2 + a))
        part = lax.dynamic_index_in_dim(x, zp ^ j, 0, keepdims=False)
        return lax.ppermute(part, ("zh", "zp", "c"), pairs)

    kv4 = jnp.concatenate([spread(kv, j) for j in range(heads)], axis=0)
    ys = [spread(qkv, j) for j in range(heads)]

    kv4 = tie(kv4, qkv)
    kv8 = jnp.concatenate([kv4, swap(kv4, "xh", 1)], axis=0)
    kv32 = lax.all_gather(kv8, "y", axis=0, tiled=True)
    pieces = [kv32, swap(kv32, "c", 1)]

    owners_all = meta[:, tokens : tokens + merged_rows]
    live_all = meta[:, tokens + merged_rows : tokens + merged_rows + n_blocks]
    counts = jnp.sum((live_all > 0).astype(jnp.int32), axis=1)
    j4 = jnp.arange(heads, dtype=jnp.int32) ^ zp
    x2 = jnp.arange(2, dtype=jnp.int32) ^ xh
    y4 = jnp.arange(4, dtype=jnp.int32)
    c2 = jnp.arange(2, dtype=jnp.int32) ^ c
    arrival = (
        (x2[None, None, :, None] * 4 + y4[None, :, None, None]) * 2 + c2[:, None, None, None]
    ) * heads + j4[None, None, None, :]
    arrival = arrival.reshape(-1)
    every = jnp.arange(n_seq, dtype=jnp.int32)
    counts = jnp.sum(jnp.where(arrival[:, None] == every[None, :], counts[None, :], 0), axis=1)
    ends = jnp.arange(n_seq + 1, dtype=jnp.int32)
    off = jnp.sum(jnp.where(every[None, :] < ends[:, None], counts[None, :] * BLK, 0), axis=1)

    tails = jnp.stack([t[tokens - HALO :, HD:] for t in ys])
    starts = jnp.stack([t[:HALO, HD:] for t in ys])
    ahead = [(i, i + 1) for i in range(n_group - 1)]
    left = lax.ppermute(
        lax.dynamic_index_in_dim(tails, zp ^ (heads - 1), 0, keepdims=False),
        ("xh", "y", "c"),
        ahead,
    )
    right = lax.ppermute(
        lax.dynamic_index_in_dim(starts, zp, 0, keepdims=False),
        ("xh", "y", "c"),
        [(j, i) for i, j in ahead],
    )
    span = heads * tokens
    ids = lax.dynamic_slice(
        marks_all, (group * span,), (span + 2 * PAD,)
    )
    ids = ids.astype(f32)[None, :]

    def slots_of(owner_rows):
        r = jnp.arange(merged_rows, dtype=jnp.int32)
        equal = owner_rows[:, :, None] == owner_rows[:, None, :]
        return jnp.sum((equal & (r[None, None, :] < r[None, :, None])).astype(jnp.int32), axis=2)

    group_owners = lax.dynamic_slice(owners_all, (group * heads, 0), (heads, merged_rows))
    peer = jnp.arange(heads, dtype=jnp.int32)[:, None]
    tgt = (group_owners * (heads * CAP) + peer * CAP + slots_of(group_owners)).reshape(-1)

    width = residual.shape[1]
    out_weight = tie(out_weight, kv8)
    weights = []
    for j in range(lax.axis_size(HEAD)):
        part = lax.dynamic_slice(out_weight, (0, (head ^ j) * width), (columns, width))
        weights.append(part if j == 0 else swap(part, HEAD, j))

    own_target = owners[:, 0] * CAP + slots_of(owners[:, 0][None, :])[0]
    choose = (jnp.arange(n_seq * CAP, dtype=jnp.int32)[:, None] == own_target[None, :]).astype(bf16)
    width = residual.shape[1]
    res = jnp.dot(
        choose, residual.reshape(merged_rows, 4 * width), preferred_element_type=f32
    ).astype(bf16)
    res = res.reshape(n_seq, CAP * 4 * width // HD, HD)
    res = lax.all_to_all(tie(res, kv32, weights[2], *ys), SEQ, split_axis=0, concat_axis=0, tiled=True)

    one = zp[None].astype(jnp.int32)
    sent = attend(off, tgt, one, ys, left, right, ids, pieces, n_seq * heads * CAP)
    sent, res, *weights = lax.optimization_barrier((sent, res, *weights))
    got = lax.all_to_all(
        sent.reshape(n_seq, heads * CAP * 4, HD), SEQ, split_axis=0, concat_axis=0, tiled=True
    ).reshape(n_seq * heads * CAP * 4, HD)
    res = res.reshape(n_seq * CAP * 4 * width // HD, HD)
    got_c = swap(got, HEAD, 1)
    got_x = swap(got, HEAD, 2)
    got_xc = swap(got_x, HEAD, 1)
    delivered = project(
        c[None].astype(jnp.int32),
        (got, got_c, got_x, got_xc),
        weights,
        res,
        layer_scale[None, :],
        n_seq * CAP,
    )
    return (delivered, refreshed)


def solution(mesh):
    devices = np.asarray(mesh.devices).reshape(2, 4, 2, 4, 2, 2)
    fine = Mesh(devices, SEQ + HEAD)
    in_specs = (
        P(SEQ, HEAD),
        P(SEQ, HEAD),
        P(SEQ, HEAD),
        P(SEQ, HEAD),
        P(HEAD),
        P(HEAD, None),
        P(SEQ),
        P(SEQ, HEAD),
        P(SEQ, HEAD),
        P(SEQ),
        P(SEQ),
        P(SEQ, None),
        P(None, HEAD),
        P(SEQ, None),
    )
    out_specs = (P(SEQ, HEAD), P(SEQ, HEAD))
    return jax.shard_map(shards, mesh=fine, in_specs=in_specs, out_specs=out_specs, check_vma=False)
```

```python
import math

import jax
import jax.numpy as jnp
import numpy as np
from jax import lax
from jax.experimental import pallas as pl
from jax.experimental.pallas import tpu as pltpu
from jax.sharding import Mesh, PartitionSpec as P

HD = 128
BLK = 16
SEG_MOST = 201
LIVE_MOST = 6
CAP = 3
HALO = 208
PAD = 256
TOK = 512
KT = 2048
NEG = -1e30
SEQ = ("xh", "y", "zh", "zp")
HEAD = ("xl", "c")
bf16 = jnp.bfloat16
f32 = jnp.float32


def rope_parts(positions):
    half = HD // 2
    freqs = 100.0 ** (-jnp.arange(half, dtype=f32) / half)
    angles = positions.astype(f32)[:, None] * freqs[None, :]
    return jnp.cos(angles), jnp.sin(angles)


def rotate(vectors, cosine, sine):
    half = HD // 2
    a, b = vectors[..., :half], vectors[..., half:]
    c, s = cosine[:, None, :], sine[:, None, :]
    return jnp.concatenate([a * c - b * s, b * c + a * s], axis=-1)


def pack_kernel(idx, k_ref, v_ref, out_ref):
    heads = out_ref.shape[0]
    for j in range(LIVE_MOST):
        rows = pl.ds(pl.multiple_of(idx[j] * BLK, BLK), BLK)
        k = k_ref[rows, :]
        v = v_ref[rows, :]
        for p in range(heads):
            out_ref[p, j * BLK : (j + 1) * BLK, :HD] = k[:, p * HD : (p + 1) * HD]
            out_ref[p, j * BLK : (j + 1) * BLK, HD:] = v[:, p * HD : (p + 1) * HD]


def rope_kernel(q_ref, k_ref, v_ref, c_ref, s_ref, out_ref):
    c = c_ref[...]
    s = s_ref[...]
    for h in range(out_ref.shape[0]):
        cols = slice(h * HD, (h + 1) * HD)
        for j, ref in enumerate((q_ref, k_ref)):
            x = ref[:, cols].astype(f32)
            turned = x * c + pltpu.roll(x, HD // 2, 1) * s
            out_ref[h, :, j * HD : (j + 1) * HD] = turned.astype(bf16)
        out_ref[h, :, 2 * HD :] = v_ref[:, cols]


def attention_kernel(off, tgt, zp, *refs):
    chunks = 4
    ys = refs[:chunks]
    left, right, ids = refs[chunks : chunks + 3]
    pieces = refs[chunks + 3 : -13]
    out, kc, vc, qs, kw, vw, ob, send, mx, ac, idcol, gathered, sems = refs[-13:]
    i = pl.program_id(0)
    sources = off.shape[0] - 1
    slot_rows = LIVE_MOST * BLK
    coef = math.log2(math.e) / math.sqrt(HD)
    total = off[sources]

    @pl.when(i == 0)
    def _():
        copies = []
        row = 0
        for n, piece in enumerate(pieces):
            to = gathered.at[pl.ds(row, piece.shape[0])]
            copies.append(pltpu.make_async_copy(piece, to, sems.at[n]))
            row += piece.shape[0]
        for copy in copies:
            copy.start()
        vc[:, HD:] = jnp.ones((vc.shape[0], HD), bf16)
        vw[:, HD:] = jnp.ones((vw.shape[0], HD), bf16)
        for k, y in enumerate(ys):
            chunk = zp[0] ^ k
            dst = pl.ds(pl.multiple_of(chunk * TOK, TOK), TOK)
            qs[dst, :] = y[:, :HD]
            dst = pl.ds(pl.multiple_of(PAD + chunk * TOK, PAD), TOK)
            kw[dst, :] = y[:, HD : 2 * HD]
            vw[dst, :HD] = y[:, 2 * HD :]
        end = PAD + chunks * TOK
        gap = PAD - HALO
        kw[:gap, :] = jnp.zeros((gap, HD), bf16)
        vw[:gap, :HD] = jnp.zeros((gap, HD), bf16)
        kw[gap:PAD, :] = left[:, :HD]
        vw[gap:PAD, :HD] = left[:, HD:]
        kw[end : end + HALO, :] = right[:, :HD]
        vw[end : end + HALO, :HD] = right[:, HD:]
        kw[end + HALO :, :] = jnp.zeros((gap, HD), bf16)
        vw[end + HALO :, :HD] = jnp.zeros((gap, HD), bf16)
        send[...] = jnp.zeros(send.shape, f32)
        for copy in copies:
            copy.wait()

        def copy_source(s, carry):
            dst = pl.ds(pl.multiple_of(off[s], BLK), slot_rows)
            src = pl.ds(pl.multiple_of(s * slot_rows, BLK), slot_rows)
            kc[dst, :] = gathered[src, :HD]
            vc[dst, :HD] = gathered[src, HD:]
            return carry

        lax.fori_loop(0, sources, copy_source, 0, unroll=2)
        tail = pl.ds(pl.multiple_of(total, BLK), KT)
        kc[tail, :] = jnp.zeros((KT, HD), bf16)
        vc[tail, :HD] = jnp.zeros((KT, HD), bf16)

    base = pl.multiple_of(i * TOK, TOK)
    sub = 128
    parts = TOK // sub
    wide = sub + 2 * PAD
    for b in range(parts):
        line = ids[:, pl.ds(pl.multiple_of(base + PAD + b * sub, sub), sub)]
        idcol[b * sub : (b + 1) * sub, :] = jnp.transpose(jnp.broadcast_to(line, (sub, sub)))

    def scores(b, keys):
        q = qs[pl.ds(pl.multiple_of(base + b * sub, sub), sub), :]
        return lax.dot_general(q, keys, (((1,), (1,)), ((), ())), preferred_element_type=f32)

    def weigh(s, m):
        new = jnp.max(s, axis=1, keepdims=True)
        if m is not None:
            new = jnp.maximum(m, new)
        return new, jnp.exp2(s * coef - new * coef).astype(bf16)

    for b in range(parts):
        rows = pl.ds(pl.multiple_of(base + b * sub, sub), wide)
        s = scores(b, kw[rows, :])
        near = ids[:, rows]
        s = jnp.where(idcol[b * sub : (b + 1) * sub, :1] == near, s, NEG)
        new, w = weigh(s, None)
        mx[b * sub : (b + 1) * sub, :] = new
        ac[b * sub : (b + 1) * sub, :] = jnp.dot(w, vw[rows, :], preferred_element_type=f32)

    def visit(start, size, masked):
        rows = pl.ds(pl.multiple_of(start, size // 2), size)
        keys, values = kc[rows, :], vc[rows, :]

        def rows_of(b, carry):
            s = scores(b, keys)
            if masked:
                col = lax.broadcasted_iota(jnp.int32, s.shape, 1)
                s = jnp.where(col < total - start, s, NEG)
            here = pl.ds(pl.multiple_of(b * sub, sub), sub)
            m = mx[here, :]
            new, w = weigh(s, m)
            mx[here, :] = new
            part = jnp.dot(w, values, preferred_element_type=f32)
            ac[here, :] = ac[here, :] * jnp.exp2((m - new) * coef) + part
            return carry

        lax.fori_loop(0, parts, rows_of, 0, unroll=2 if masked else True)

    def loop(j, carry):
        visit(j * KT, KT, False)
        return carry

    full = total // KT
    rest = total - full * KT
    lax.fori_loop(0, full, loop, 0)

    @pl.when(rest > KT // 2)
    def _():
        visit(full * KT, KT, True)

    @pl.when((rest > 0) & (rest <= KT // 2))
    def _():
        visit(full * KT, KT // 2, True)

    ob[...] = ac[:, :HD] / ac[:, HD:]

    def place(r, carry):
        dst = tgt[i * (TOK // 4) + r] * 4
        send[pl.ds(pl.multiple_of(dst, 4), 4), :] = ob[pl.ds(pl.multiple_of(r * 4, 4), 4), :]
        return carry

    lax.fori_loop(0, TOK // 4, place, 0, unroll=8)

    @pl.when(i == pl.num_programs(0) - 1)
    def _():
        out[...] = send[...].astype(bf16)


def attend(off, tgt, zp, ys, left, right, ids, pieces, slots):
    chunks = len(ys)
    sources = off.shape[0] - 1
    cache_most = sources * LIVE_MOST * BLK
    whole = pl.BlockSpec(memory_space=pltpu.VMEM)
    return pl.pallas_call(
        attention_kernel,
        out_shape=jax.ShapeDtypeStruct((slots * 4, HD), bf16),
        grid_spec=pltpu.PrefetchScalarGridSpec(
            num_scalar_prefetch=3,
            grid=(chunks,),
            in_specs=[whole] * (chunks + 3)
            + [pl.BlockSpec(memory_space=pl.ANY)] * len(pieces),
            out_specs=whole,
            scratch_shapes=[
                pltpu.VMEM((cache_most + KT, HD), bf16),
                pltpu.VMEM((cache_most + KT, 2 * HD), bf16),
                pltpu.VMEM((chunks * TOK, HD), bf16),
                pltpu.VMEM((chunks * TOK + 2 * PAD, HD), bf16),
                pltpu.VMEM((chunks * TOK + 2 * PAD, 2 * HD), bf16),
                pltpu.VMEM((TOK, HD), f32),
                pltpu.VMEM((slots * 4, HD), f32),
                pltpu.VMEM((TOK, 1), f32),
                pltpu.VMEM((TOK, 2 * HD), f32),
                pltpu.VMEM((TOK, 128), f32),
                pltpu.VMEM((cache_most, 2 * HD), bf16),
                pltpu.SemaphoreType.DMA((len(pieces),)),
            ],
        ),
        compiler_params=pltpu.CompilerParams(
            dimension_semantics=("arbitrary",), vmem_limit_bytes=48 << 20
        ),
        cost_estimate=pl.CostEstimate(
            flops=4 * 2048 * 7168 * 128, bytes_accessed=8 << 20, transcendentals=2048 * 7168
        ),
    )(off, tgt, zp, *ys, left, right, ids, *pieces)


def project_kernel(core, a0, a1, a2, a3, w0, w1, w2, w3, res, scale, mix, out, att, res32, proj):
    b = pl.program_id(0)
    c = core[0]
    groups = a0.shape[0] // (8 * 48)

    @pl.when(b == 0)
    def _():
        res32[...] = res[...].astype(f32)
        for k, a in enumerate((a0, a1, a2, a3)):

            def move(g, carry):
                to = pl.ds(pl.multiple_of((g * 2 + (c ^ (k % 2))) * 48, 16), 48)
                for p in range(8):
                    block = (k // 2) * 2 + (c ^ (p // 4))
                    src = pl.ds(pl.multiple_of(g * 384 + p * 48, 16), 48)
                    att[block, to, (p % 4) * HD : (p % 4 + 1) * HD] = a[src, :]
                return carry

            lax.fori_loop(0, groups, move, 0)

    total = None
    for k, w in enumerate((w0, w1, w2, w3)):
        part = jnp.dot(att[k], w[...], preferred_element_type=f32)
        total = part if total is None else total + part
    total = total * scale[...]
    slots = out.shape[0]
    per = w0.shape[1] // HD
    for d in range(per):
        proj[d * 4 * slots : (d + 1) * 4 * slots, :] = total[:, d * HD : (d + 1) * HD]
    for d in range(per):
        parts = []
        for t in range(4):
            new = proj[pl.ds(d * 4 * slots + t, slots, stride=4), :]
            old = res32[pl.ds(t * 8 + b * per + d, slots, stride=32), :]
            parts.append((old + new).astype(bf16))
        rows = jnp.concatenate(parts, axis=1)
        out[:, d * 4 * HD : (d + 1) * 4 * HD] = jnp.dot(
            rows, mix[...], preferred_element_type=f32
        ).astype(bf16)


def project(core, atts, weights, res, scale, slots):
    width = weights[0].shape[1]
    part = 256
    whole = pl.BlockSpec(memory_space=pltpu.VMEM)
    source = np.arange(4 * HD)
    mix = np.zeros((4 * HD, 4 * HD), np.float32)
    mix[source, (source % HD) * 4 + source // HD] = 1.0
    return pl.pallas_call(
        project_kernel,
        out_shape=jax.ShapeDtypeStruct((slots, 4 * width), bf16),
        grid_spec=pltpu.PrefetchScalarGridSpec(
            num_scalar_prefetch=1,
            grid=(width // part,),
            in_specs=[whole] * 4
            + [pl.BlockSpec((weights[0].shape[0], part), lambda b, *_: (0, b))] * 4
            + [whole, pl.BlockSpec((1, part), lambda b, *_: (0, b)), whole],
            out_specs=pl.BlockSpec((slots, 4 * part), lambda b, *_: (0, b)),
            scratch_shapes=[
                pltpu.VMEM((4, slots * 4, 4 * HD), bf16),
                pltpu.VMEM((slots * 32, HD), f32),
                pltpu.VMEM((slots * 4 * part // HD, HD), f32),
            ],
        ),
        compiler_params=pltpu.CompilerParams(
            dimension_semantics=("arbitrary",), vmem_limit_bytes=48 << 20
        ),
        cost_estimate=pl.CostEstimate(
            flops=2 * 768 * 2048 * 1024, bytes_accessed=16 << 20, transcendentals=0
        ),
    )(core, *atts, *weights, res, scale, jnp.asarray(mix, bf16))


def swap(x, axis, k):
    n = lax.axis_size(axis)
    return lax.ppermute(x, axis, [(i, i ^ k) for i in range(n)])


def tie(x, *others):
    return lax.optimization_barrier((x, *others))[0]


def shards(
    queries,
    keys_new,
    values_new,
    residual,
    layer_scale,
    out_weight,
    segment_ids,
    cache_keys,
    cache_values,
    block_live,
    recompute_block,
    recompute_hidden,
    key_weight,
    owners,
):
    tokens, columns = queries.shape
    heads = columns // HD
    n_head = lax.axis_size(HEAD)
    n_seq = lax.axis_size(SEQ)
    seq = lax.axis_index(SEQ)
    xh, y, zp, c = (lax.axis_index(n) for n in ("xh", "y", "zp", "c"))
    head = lax.axis_index(HEAD)
    merged_rows = tokens // 4
    group = (xh * 4 + y) * 2 + c
    n_group = n_seq // heads
    whole = pl.BlockSpec(memory_space=pltpu.VMEM)

    marks = segment_ids + 1
    before = lax.ppermute(marks[tokens - PAD :], SEQ, [(i, i + 1) for i in range(n_seq - 1)])
    near = jnp.concatenate([before, marks])
    same = marks[:, None] == near[None, :]
    index = jnp.arange(PAD + tokens, dtype=jnp.int32)
    first = jnp.min(jnp.where(same, index[None, :], PAD + tokens), axis=1)
    cosine, sine = rope_parts(PAD + jnp.arange(tokens, dtype=jnp.int32) - first)

    qkv = pl.pallas_call(
        rope_kernel,
        out_shape=jax.ShapeDtypeStruct((heads, tokens, 3 * HD), bf16),
        in_specs=[whole] * 5,
        out_specs=whole,
    )(
        queries,
        keys_new,
        values_new,
        jnp.concatenate([cosine, cosine], axis=1),
        jnp.concatenate([-sine, sine], axis=1),
    )

    cache_rows = cache_keys.shape[0]
    block = recompute_block[0]
    fresh = jnp.dot(recompute_hidden, key_weight, preferred_element_type=f32)
    fresh_rows = seq * cache_rows + block * BLK + jnp.arange(BLK, dtype=jnp.int32)
    fresh = rotate(fresh.reshape(BLK, heads, HD), *rope_parts(fresh_rows % SEG_MOST))
    fresh = fresh.reshape(BLK, columns).astype(bf16)
    refreshed = lax.dynamic_update_slice(cache_keys, fresh, (block * BLK, 0))

    live = block_live > 0
    n_blocks = block_live.shape[0]
    blocks = jnp.arange(n_blocks, dtype=jnp.int32)
    rank = jnp.sum(jnp.where(blocks[None, :] < blocks[:, None], live[None, :], False), axis=1)
    hit = live[None, :] & (rank[None, :] == jnp.arange(LIVE_MOST, dtype=jnp.int32)[:, None])
    order = jnp.sum(jnp.where(hit, blocks[None, :], 0), axis=1)
    kv = pl.pallas_call(
        pack_kernel,
        out_shape=jax.ShapeDtypeStruct((heads, LIVE_MOST * BLK, 2 * HD), bf16),
        grid_spec=pltpu.PrefetchScalarGridSpec(
            num_scalar_prefetch=1, grid=(), in_specs=[whole] * 2, out_specs=whole
        ),
    )(order, refreshed, cache_values)

    def spread(x, j):
        pairs = []
        for a in range(2):
            for b in range(heads):
                for d in range(2):
                    pairs.append(((a * heads + b) * 2 + d, (d * heads + (b ^ j)) * 2 + a))
        part = lax.dynamic_index_in_dim(x, zp ^ j, 0, keepdims=False)
        return lax.ppermute(part, ("zh", "zp", "c"), pairs)

    kv = tie(kv, before)
    cached = [spread(kv, j) for j in range(heads)]
    kv4 = jnp.concatenate(cached, axis=0)

    ys = [spread(qkv, j) for j in range(heads)]

    kv4 = tie(kv4, qkv)
    kv8 = jnp.concatenate([kv4, swap(kv4, "xh", 1)], axis=0)
    kv32 = lax.all_gather(kv8, "y", axis=0, tiled=True)
    pieces = [kv32, swap(tie(kv32, *ys), "c", 1)]

    meta = jnp.concatenate(
        [marks, owners[:, 0], block_live, jnp.zeros((128 - n_blocks,), jnp.int32)]
    )
    meta = jnp.broadcast_to(tie(meta, kv8, qkv)[None, None, :], (n_seq, 1, meta.shape[0]))
    meta = lax.all_to_all(meta, SEQ, split_axis=0, concat_axis=0, tiled=True)[:, 0, :]
    marks_all = jnp.pad(meta[:, :tokens].reshape(-1), (PAD, PAD))

    owners_all = meta[:, tokens : tokens + merged_rows]
    live_all = meta[:, tokens + merged_rows : tokens + merged_rows + n_blocks]
    counts = jnp.sum((live_all > 0).astype(jnp.int32), axis=1)
    j4 = jnp.arange(heads, dtype=jnp.int32) ^ zp
    x2 = jnp.arange(2, dtype=jnp.int32) ^ xh
    y4 = jnp.arange(4, dtype=jnp.int32)
    c2 = jnp.arange(2, dtype=jnp.int32) ^ c
    arrival = (
        (x2[None, None, :, None] * 4 + y4[None, :, None, None]) * 2 + c2[:, None, None, None]
    ) * heads + j4[None, None, None, :]
    arrival = arrival.reshape(-1)
    every = jnp.arange(n_seq, dtype=jnp.int32)
    counts = jnp.sum(jnp.where(arrival[:, None] == every[None, :], counts[None, :], 0), axis=1)
    ends = jnp.arange(n_seq + 1, dtype=jnp.int32)
    off = jnp.sum(jnp.where(every[None, :] < ends[:, None], counts[None, :] * BLK, 0), axis=1)

    width = residual.shape[1]
    out_weight = tie(out_weight, kv8)
    blocks_w = [
        lax.dynamic_slice(out_weight, (0, (head ^ j) * width), (columns, width))
        for j in range(n_head)
    ]
    weight_x = swap(blocks_w[2], HEAD, 2)

    ends_of = tie(tuple(ys), weight_x, meta)
    tails = jnp.stack([t[tokens - HALO :, HD:] for t in ends_of])
    starts = jnp.stack([t[:HALO, HD:] for t in ends_of])
    ahead = [(i, i + 1) for i in range(n_group - 1)]
    left = lax.ppermute(
        lax.dynamic_index_in_dim(tails, zp ^ (heads - 1), 0, keepdims=False),
        ("xh", "y", "c"),
        ahead,
    )
    right = lax.ppermute(
        lax.dynamic_index_in_dim(starts, zp, 0, keepdims=False),
        ("xh", "y", "c"),
        [(j, i) for i, j in ahead],
    )
    span = heads * tokens
    ids = lax.dynamic_slice(
        marks_all, (group * span,), (span + 2 * PAD,)
    )
    ids = ids.astype(f32)[None, :]

    def slots_of(owner_rows):
        r = jnp.arange(merged_rows, dtype=jnp.int32)
        equal = owner_rows[:, :, None] == owner_rows[:, None, :]
        return jnp.sum((equal & (r[None, None, :] < r[None, :, None])).astype(jnp.int32), axis=2)

    group_owners = lax.dynamic_slice(owners_all, (group * heads, 0), (heads, merged_rows))
    peer = jnp.arange(heads, dtype=jnp.int32)[:, None]
    tgt = (group_owners * (heads * CAP) + peer * CAP + slots_of(group_owners)).reshape(-1)

    weights = [
        blocks_w[0],
        swap(tie(blocks_w[1], left, right), HEAD, 1),
        weight_x,
        swap(tie(blocks_w[3], left, right), HEAD, 3),
    ]

    own_target = owners[:, 0] * CAP + slots_of(owners[:, 0][None, :])[0]
    choose = (jnp.arange(n_seq * CAP, dtype=jnp.int32)[:, None] == own_target[None, :]).astype(bf16)
    width = residual.shape[1]
    residual = tie(residual, kv32)
    res = jnp.dot(
        choose, residual.reshape(merged_rows, 4 * width), preferred_element_type=f32
    ).astype(bf16)
    res = res.reshape(n_seq, CAP * 4 * width // HD, HD)
    res = lax.all_to_all(tie(res, pieces[1], left, right), SEQ, split_axis=0, concat_axis=0, tiled=True)

    one = zp[None].astype(jnp.int32)
    sent = attend(off, tgt, one, ys, left, right, ids, pieces, n_seq * heads * CAP)
    sent, res, *weights = lax.optimization_barrier((sent, res, *weights))
    got = lax.all_to_all(
        sent.reshape(n_seq, heads * CAP * 4, HD), SEQ, split_axis=0, concat_axis=0, tiled=True
    ).reshape(n_seq * heads * CAP * 4, HD)
    res = res.reshape(n_seq * CAP * 4 * width // HD, HD)
    got_c = swap(got, HEAD, 1)
    got_x = swap(got, HEAD, 2)
    got_xc = swap(got_x, HEAD, 1)
    delivered = project(
        c[None].astype(jnp.int32),
        (got, got_c, got_x, got_xc),
        weights,
        res,
        layer_scale[None, :],
        n_seq * CAP,
    )
    return (delivered, refreshed)


def solution(mesh):
    devices = np.asarray(mesh.devices).reshape(2, 4, 2, 4, 2, 2)
    fine = Mesh(devices, SEQ + HEAD)
    in_specs = (
        P(SEQ, HEAD),
        P(SEQ, HEAD),
        P(SEQ, HEAD),
        P(SEQ, HEAD),
        P(HEAD),
        P(HEAD, None),
        P(SEQ),
        P(SEQ, HEAD),
        P(SEQ, HEAD),
        P(SEQ),
        P(SEQ),
        P(SEQ, None),
        P(None, HEAD),
        P(SEQ, None),
    )
    out_specs = (P(SEQ, HEAD), P(SEQ, HEAD))
    return jax.shard_map(shards, mesh=fine, in_specs=in_specs, out_specs=out_specs, check_vma=False)
```

```python
import math

import jax
import jax.numpy as jnp
import numpy as np
from jax import lax
from jax.experimental import pallas as pl
from jax.experimental.pallas import tpu as pltpu
from jax.sharding import Mesh, PartitionSpec as P

HD = 128
BLK = 16
SEG_MOST = 201
LIVE_MOST = 6
CAP = 3
HALO = 208
PAD = 256
TOK = 512
KT = 2048
NEG = -1e30
SEQ = ("xh", "y", "zh", "zp")
HEAD = ("xl", "c")
bf16 = jnp.bfloat16
f32 = jnp.float32


def rope_parts(positions):
    half = HD // 2
    freqs = 100.0 ** (-jnp.arange(half, dtype=f32) / half)
    angles = positions.astype(f32)[:, None] * freqs[None, :]
    return jnp.cos(angles), jnp.sin(angles)


def rotate(vectors, cosine, sine):
    half = HD // 2
    a, b = vectors[..., :half], vectors[..., half:]
    c, s = cosine[:, None, :], sine[:, None, :]
    return jnp.concatenate([a * c - b * s, b * c + a * s], axis=-1)


def pack_kernel(idx, k_ref, v_ref, out_ref):
    heads = out_ref.shape[0]
    for j in range(LIVE_MOST):
        rows = pl.ds(pl.multiple_of(idx[j] * BLK, BLK), BLK)
        k = jnp.where(j < idx[LIVE_MOST], k_ref[rows, :], jnp.inf).astype(bf16)
        v = v_ref[rows, :]
        for p in range(heads):
            out_ref[p, j * BLK : (j + 1) * BLK, :HD] = k[:, p * HD : (p + 1) * HD]
            out_ref[p, j * BLK : (j + 1) * BLK, HD:] = v[:, p * HD : (p + 1) * HD]


def rope_kernel(q_ref, k_ref, v_ref, c_ref, s_ref, extra_ref, out_ref):
    tokens = q_ref.shape[0]
    c = c_ref[...]
    s = s_ref[...]
    for h in range(out_ref.shape[0]):
        cols = slice(h * HD, (h + 1) * HD)
        for j, ref in enumerate((q_ref, k_ref)):
            x = ref[:, cols].astype(f32)
            turned = x * c + pltpu.roll(x, HD // 2, 1) * s
            out_ref[h, :tokens, j * HD : (j + 1) * HD] = turned.astype(bf16)
        out_ref[h, :tokens, 2 * HD :] = v_ref[:, cols]
        out_ref[h, tokens:, :] = extra_ref[...]


def attention_kernel(off, tgt, zp, *refs):
    chunks = 4
    ys = refs[:chunks]
    left, right = refs[chunks : chunks + 2]
    pieces = refs[chunks + 2 : -14]
    out, kc, vc, qs, kw, vw, ob, send, mx, ac, idcol, gathered, ids, sems = refs[-14:]
    i = pl.program_id(0)
    sources = off.shape[0] - 1
    slot_rows = LIVE_MOST * BLK
    coef = math.log2(math.e) / math.sqrt(HD)
    total = off[sources]

    @pl.when(i == 0)
    def _():
        copies = []
        row = 0
        for n, piece in enumerate(pieces):
            to = gathered.at[pl.ds(row, piece.shape[0])]
            copies.append(pltpu.make_async_copy(piece, to, sems.at[n]))
            row += piece.shape[0]
        for copy in copies:
            copy.start()
        vc[:, HD:] = jnp.ones((vc.shape[0], HD), bf16)
        vw[:, HD:] = jnp.ones((vw.shape[0], HD), bf16)
        for k, y in enumerate(ys):
            chunk = zp[0] ^ k
            dst = pl.ds(pl.multiple_of(chunk * TOK, TOK), TOK)
            qs[dst, :] = y[:TOK, :HD]
            dst = pl.ds(pl.multiple_of(PAD + chunk * TOK, PAD), TOK)
            kw[dst, :] = y[:TOK, HD : 2 * HD]
            vw[dst, :HD] = y[:TOK, 2 * HD :]
            line = y[TOK:, :].astype(f32)
            at = pl.multiple_of(PAD + chunk * TOK, PAD)
            ids[:, pl.ds(at, 3 * HD)] = line[0:1, :]
            at = pl.multiple_of(PAD + chunk * TOK + 3 * HD, HD)
            ids[:, pl.ds(at, HD)] = line[1:2, :HD]
        end = PAD + chunks * TOK
        gap = PAD - HALO
        kw[:gap, :] = jnp.zeros((gap, HD), bf16)
        vw[:gap, :HD] = jnp.zeros((gap, HD), bf16)
        kw[gap:PAD, :] = left[:HALO, :HD]
        vw[gap:PAD, :HD] = left[:HALO, HD:]
        kw[end : end + HALO, :] = right[:HALO, :HD]
        vw[end : end + HALO, :HD] = right[:HALO, HD:]
        ids[:, :PAD] = left[HALO:, :].astype(f32)[0:1, :]
        ids[:, end:] = right[HALO:, :].astype(f32)[0:1, :]
        kw[end + HALO :, :] = jnp.zeros((gap, HD), bf16)
        vw[end + HALO :, :HD] = jnp.zeros((gap, HD), bf16)
        send[...] = jnp.zeros(send.shape, f32)
        for copy in copies:
            copy.wait()

        def copy_source(s, carry):
            dst = pl.ds(pl.multiple_of(off[s], BLK), slot_rows)
            src = pl.ds(pl.multiple_of(s * slot_rows, BLK), slot_rows)
            kc[dst, :] = gathered[src, :HD]
            vc[dst, :HD] = gathered[src, HD:]
            return carry

        lax.fori_loop(0, sources, copy_source, 0, unroll=2)
        tail = pl.ds(pl.multiple_of(total, BLK), KT)
        kc[tail, :] = jnp.zeros((KT, HD), bf16)
        vc[tail, :HD] = jnp.zeros((KT, HD), bf16)

    base = pl.multiple_of(i * TOK, TOK)
    sub = 128
    parts = TOK // sub
    wide = sub + 2 * PAD
    for b in range(parts):
        line = ids[:, pl.ds(pl.multiple_of(base + PAD + b * sub, sub), sub)]
        idcol[b * sub : (b + 1) * sub, :] = jnp.transpose(jnp.broadcast_to(line, (sub, sub)))

    def scores(b, keys):
        q = qs[pl.ds(pl.multiple_of(base + b * sub, sub), sub), :]
        return lax.dot_general(q, keys, (((1,), (1,)), ((), ())), preferred_element_type=f32)

    def weigh(s, m):
        new = jnp.max(s, axis=1, keepdims=True)
        if m is not None:
            new = jnp.maximum(m, new)
        return new, jnp.exp2(s * coef - new * coef).astype(bf16)

    for b in range(parts):
        rows = pl.ds(pl.multiple_of(base + b * sub, sub), wide)
        s = scores(b, kw[rows, :])
        near = ids[:, rows]
        s = jnp.where(idcol[b * sub : (b + 1) * sub, :1] == near, s, NEG)
        new, w = weigh(s, None)
        mx[b * sub : (b + 1) * sub, :] = new
        ac[b * sub : (b + 1) * sub, :] = jnp.dot(w, vw[rows, :], preferred_element_type=f32)

    def visit(start, size, masked):
        rows = pl.ds(pl.multiple_of(start, size // 2), size)
        keys, values = kc[rows, :], vc[rows, :]

        def rows_of(b, carry):
            s = scores(b, keys)
            if masked:
                col = lax.broadcasted_iota(jnp.int32, s.shape, 1)
                s = jnp.where(col < total - start, s, NEG)
            here = pl.ds(pl.multiple_of(b * sub, sub), sub)
            m = mx[here, :]
            new, w = weigh(s, m)
            mx[here, :] = new
            part = jnp.dot(w, values, preferred_element_type=f32)
            ac[here, :] = ac[here, :] * jnp.exp2((m - new) * coef) + part
            return carry

        lax.fori_loop(0, parts, rows_of, 0, unroll=2 if masked else True)

    def loop(j, carry):
        visit(j * KT, KT, False)
        return carry

    full = total // KT
    rest = total - full * KT
    lax.fori_loop(0, full, loop, 0)

    @pl.when(rest > KT // 2)
    def _():
        visit(full * KT, KT, True)

    @pl.when((rest > 0) & (rest <= KT // 2))
    def _():
        visit(full * KT, KT // 2, True)

    ob[...] = ac[:, :HD] / ac[:, HD:]

    def place(r, carry):
        dst = tgt[(i ^ zp[0]) * (TOK // 4) + r] * 4
        send[pl.ds(pl.multiple_of(dst, 4), 4), :] = ob[pl.ds(pl.multiple_of(r * 4, 4), 4), :]
        return carry

    lax.fori_loop(0, TOK // 4, place, 0, unroll=8)

    @pl.when(i == pl.num_programs(0) - 1)
    def _():
        out[...] = send[...].astype(bf16)


def attend(off, tgt, zp, ys, left, right, pieces, slots):
    chunks = len(ys)
    sources = off.shape[0] - 1
    cache_most = sources * LIVE_MOST * BLK
    whole = pl.BlockSpec(memory_space=pltpu.VMEM)
    return pl.pallas_call(
        attention_kernel,
        out_shape=jax.ShapeDtypeStruct((slots * 4, HD), bf16),
        grid_spec=pltpu.PrefetchScalarGridSpec(
            num_scalar_prefetch=3,
            grid=(chunks,),
            in_specs=[whole] * (chunks + 2)
            + [pl.BlockSpec(memory_space=pl.ANY)] * len(pieces),
            out_specs=whole,
            scratch_shapes=[
                pltpu.VMEM((cache_most + KT, HD), bf16),
                pltpu.VMEM((cache_most + KT, 2 * HD), bf16),
                pltpu.VMEM((chunks * TOK, HD), bf16),
                pltpu.VMEM((chunks * TOK + 2 * PAD, HD), bf16),
                pltpu.VMEM((chunks * TOK + 2 * PAD, 2 * HD), bf16),
                pltpu.VMEM((TOK, HD), f32),
                pltpu.VMEM((slots * 4, HD), f32),
                pltpu.VMEM((TOK, 1), f32),
                pltpu.VMEM((TOK, 2 * HD), f32),
                pltpu.VMEM((TOK, 128), f32),
                pltpu.VMEM((cache_most, 2 * HD), bf16),
                pltpu.VMEM((1, chunks * TOK + 2 * PAD), f32),
                pltpu.SemaphoreType.DMA((len(pieces),)),
            ],
        ),
        compiler_params=pltpu.CompilerParams(
            dimension_semantics=("arbitrary",), vmem_limit_bytes=48 << 20
        ),
        cost_estimate=pl.CostEstimate(
            flops=4 * 2048 * 7168 * 128, bytes_accessed=8 << 20, transcendentals=2048 * 7168
        ),
    )(off, tgt, zp, *ys, left, right, *pieces)


def project_kernel(core, a0, a1, a2, a3, w0, w1, w2, w3, res, scale, mix, out, att, res32, proj):
    b = pl.program_id(0)
    c = core[0]
    groups = a0.shape[0] // (8 * 48)

    @pl.when(b == 0)
    def _():
        res32[...] = res[...].astype(f32)
        for k, a in enumerate((a0, a1, a2, a3)):

            def move(g, carry):
                to = pl.ds(pl.multiple_of((g * 2 + (c ^ (k % 2))) * 48, 16), 48)
                for p in range(8):
                    block = (k // 2) * 2 + (c ^ (p // 4))
                    src = pl.ds(pl.multiple_of(g * 384 + p * 48, 16), 48)
                    att[block, to, (p % 4) * HD : (p % 4 + 1) * HD] = a[src, :]
                return carry

            lax.fori_loop(0, groups, move, 0)

    total = None
    for k, w in enumerate((w0, w1, w2, w3)):
        part = jnp.dot(att[k], w[...], preferred_element_type=f32)
        total = part if total is None else total + part
    total = total * scale[...]
    slots = out.shape[0]
    per = w0.shape[1] // HD
    for d in range(per):
        proj[d * 4 * slots : (d + 1) * 4 * slots, :] = total[:, d * HD : (d + 1) * HD]
    for d in range(per):
        parts = []
        for t in range(4):
            new = proj[pl.ds(d * 4 * slots + t, slots, stride=4), :]
            old = res32[pl.ds(t * 8 + b * per + d, slots, stride=32), :]
            parts.append((old + new).astype(bf16))
        rows = jnp.concatenate(parts, axis=1)
        out[:, d * 4 * HD : (d + 1) * 4 * HD] = jnp.dot(
            rows, mix[...], preferred_element_type=f32
        ).astype(bf16)


def project(core, atts, weights, res, scale, slots):
    width = weights[0].shape[1]
    part = 256
    whole = pl.BlockSpec(memory_space=pltpu.VMEM)
    source = np.arange(4 * HD)
    mix = np.zeros((4 * HD, 4 * HD), np.float32)
    mix[source, (source % HD) * 4 + source // HD] = 1.0
    return pl.pallas_call(
        project_kernel,
        out_shape=jax.ShapeDtypeStruct((slots, 4 * width), bf16),
        grid_spec=pltpu.PrefetchScalarGridSpec(
            num_scalar_prefetch=1,
            grid=(width // part,),
            in_specs=[whole] * 4
            + [pl.BlockSpec((weights[0].shape[0], part), lambda b, *_: (0, b))] * 4
            + [whole, pl.BlockSpec((1, part), lambda b, *_: (0, b)), whole],
            out_specs=pl.BlockSpec((slots, 4 * part), lambda b, *_: (0, b)),
            scratch_shapes=[
                pltpu.VMEM((4, slots * 4, 4 * HD), bf16),
                pltpu.VMEM((slots * 32, HD), f32),
                pltpu.VMEM((slots * 4 * part // HD, HD), f32),
            ],
        ),
        compiler_params=pltpu.CompilerParams(
            dimension_semantics=("arbitrary",), vmem_limit_bytes=48 << 20
        ),
        cost_estimate=pl.CostEstimate(
            flops=2 * 768 * 2048 * 1024, bytes_accessed=16 << 20, transcendentals=0
        ),
    )(core, *atts, *weights, res, scale, jnp.asarray(mix, bf16))


def swap(x, axis, k):
    n = lax.axis_size(axis)
    return lax.ppermute(x, axis, [(i, i ^ k) for i in range(n)])


def tie(x, *others):
    return lax.optimization_barrier((x, *others))[0]


def shards(
    queries,
    keys_new,
    values_new,
    residual,
    layer_scale,
    out_weight,
    segment_ids,
    cache_keys,
    cache_values,
    block_live,
    recompute_block,
    recompute_hidden,
    key_weight,
    owners,
):
    tokens, columns = queries.shape
    heads = columns // HD
    n_head = lax.axis_size(HEAD)
    n_seq = lax.axis_size(SEQ)
    seq = lax.axis_index(SEQ)
    zp, c = (lax.axis_index(n) for n in ("zp", "c"))
    head = lax.axis_index(HEAD)
    merged_rows = tokens // 4
    n_group = n_seq // heads
    whole = pl.BlockSpec(memory_space=pltpu.VMEM)

    marks = segment_ids + 1
    before = lax.ppermute(marks[tokens - PAD :], SEQ, [(i, i + 1) for i in range(n_seq - 1)])
    near = jnp.concatenate([before, marks])
    same = marks[:, None] == near[None, :]
    index = jnp.arange(PAD + tokens, dtype=jnp.int32)
    first = jnp.min(jnp.where(same, index[None, :], PAD + tokens), axis=1)
    cosine, sine = rope_parts(PAD + jnp.arange(tokens, dtype=jnp.int32) - first)

    extra = jnp.concatenate([marks, owners[:, 0]])
    extra = jnp.pad(extra, (0, BLK * 3 * HD - extra.shape[0])).astype(bf16).reshape(BLK, 3 * HD)
    qkv = pl.pallas_call(
        rope_kernel,
        out_shape=jax.ShapeDtypeStruct((heads, tokens + BLK, 3 * HD), bf16),
        in_specs=[whole] * 6,
        out_specs=whole,
    )(
        queries,
        keys_new,
        values_new,
        jnp.concatenate([cosine, cosine], axis=1),
        jnp.concatenate([-sine, sine], axis=1),
        extra,
    )

    cache_rows = cache_keys.shape[0]
    block = recompute_block[0]
    fresh = jnp.dot(recompute_hidden, key_weight, preferred_element_type=f32)
    fresh_rows = seq * cache_rows + block * BLK + jnp.arange(BLK, dtype=jnp.int32)
    fresh = rotate(fresh.reshape(BLK, heads, HD), *rope_parts(fresh_rows % SEG_MOST))
    fresh = fresh.reshape(BLK, columns).astype(bf16)
    refreshed = lax.dynamic_update_slice(cache_keys, fresh, (block * BLK, 0))

    live = block_live > 0
    n_blocks = block_live.shape[0]
    blocks = jnp.arange(n_blocks, dtype=jnp.int32)
    rank = jnp.sum(jnp.where(blocks[None, :] < blocks[:, None], live[None, :], False), axis=1)
    hit = live[None, :] & (rank[None, :] == jnp.arange(LIVE_MOST, dtype=jnp.int32)[:, None])
    order = jnp.sum(jnp.where(hit, blocks[None, :], 0), axis=1)
    order = jnp.concatenate([order, jnp.sum(live.astype(jnp.int32), keepdims=True)])
    kv = pl.pallas_call(
        pack_kernel,
        out_shape=jax.ShapeDtypeStruct((heads, LIVE_MOST * BLK, 2 * HD), bf16),
        grid_spec=pltpu.PrefetchScalarGridSpec(
            num_scalar_prefetch=1, grid=(), in_specs=[whole] * 2, out_specs=whole
        ),
    )(order, refreshed, cache_values)

    def spread(x, j):
        pairs = []
        for a in range(2):
            for b in range(heads):
                for d in range(2):
                    pairs.append(((a * heads + b) * 2 + d, (d * heads + (b ^ j)) * 2 + a))
        part = lax.dynamic_index_in_dim(x, zp ^ j, 0, keepdims=False)
        return lax.ppermute(part, ("zh", "zp", "c"), pairs)

    kv = tie(kv, before)
    cached = [spread(kv, j) for j in range(heads)]
    kv4 = jnp.concatenate(cached, axis=0)

    ys = [spread(qkv, j) for j in range(heads)]

    kv4 = tie(kv4, qkv)
    kv8 = jnp.concatenate([kv4, swap(kv4, "xh", 1)], axis=0)
    kv32 = lax.all_gather(kv8, "y", axis=0, tiled=True)

    width = residual.shape[1]
    out_weight = tie(out_weight, kv8)
    blocks_w = [
        lax.dynamic_slice(out_weight, (0, (head ^ j) * width), (columns, width))
        for j in range(n_head)
    ]
    weight_x = swap(blocks_w[2], HEAD, 2)

    def slots_of(owner_rows):
        r = jnp.arange(merged_rows, dtype=jnp.int32)
        equal = owner_rows[:, :, None] == owner_rows[:, None, :]
        return jnp.sum((equal & (r[None, None, :] < r[None, :, None])).astype(jnp.int32), axis=2)

    own_target = owners[:, 0] * CAP + slots_of(owners[:, 0][None, :])[0]
    choose = (jnp.arange(n_seq * CAP, dtype=jnp.int32)[:, None] == own_target[None, :]).astype(bf16)
    residual = tie(residual, kv8, qkv)
    res = jnp.dot(
        choose, residual.reshape(merged_rows, 4 * width), preferred_element_type=f32
    ).astype(bf16)
    res = res.reshape(n_seq, CAP * 4 * width // HD, HD)

    edges = tie(tuple(ys), weight_x, res)

    def edge(low, j, line, pairs):
        part = jnp.stack([t[low : low + HALO, HD:] for t in edges])
        part = lax.dynamic_index_in_dim(part, j, 0, keepdims=False)
        line = lax.dynamic_index_in_dim(jnp.stack([line(t[tokens : tokens + 2]) for t in edges]), j, 0)
        part = jnp.concatenate([part, jnp.pad(line, ((0, BLK - 1), (0, 0)))], axis=0)
        return lax.ppermute(part, ("xh", "y", "c"), pairs)

    ahead = [(i, i + 1) for i in range(n_group - 1)]
    none = jnp.zeros((PAD - HALO,), bf16)
    lead = tokens - HALO
    left = edge(
        lead,
        zp ^ (heads - 1),
        lambda t: jnp.concatenate([none, t[0, lead:], t[1, : tokens - 3 * HD]]),
        ahead,
    )
    right = edge(
        0, zp, lambda t: jnp.concatenate([t[0, :HALO], none]), [(j, i) for i, j in ahead]
    )

    pieces = [kv32, swap(tie(kv32, left, right), "c", 1)]

    firsts = jnp.stack([p.reshape(-1, LIVE_MOST, BLK, 2 * HD)[:, :, 0, 0] for p in pieces])
    counts = jnp.sum(jnp.isfinite(firsts).astype(jnp.int32), axis=2).reshape(-1)
    every = jnp.arange(n_seq, dtype=jnp.int32)
    ends = jnp.arange(n_seq + 1, dtype=jnp.int32)
    off = jnp.sum(jnp.where(every[None, :] < ends[:, None], counts[None, :] * BLK, 0), axis=1)

    group_owners = jnp.stack([t[tokens + 1, HD : HD + merged_rows] for t in ys]).astype(jnp.int32)
    peer = (jnp.arange(heads, dtype=jnp.int32) ^ zp)[:, None]
    tgt = (group_owners * (heads * CAP) + peer * CAP + slots_of(group_owners)).reshape(-1)

    weights = [
        blocks_w[0],
        swap(tie(blocks_w[1], left, right), HEAD, 1),
        weight_x,
        swap(tie(blocks_w[3], left, right), HEAD, 3),
    ]

    res = lax.all_to_all(tie(res, pieces[1], weight_x, left, right), SEQ, split_axis=0, concat_axis=0, tiled=True)

    one = zp[None].astype(jnp.int32)
    sent = attend(off, tgt, one, ys, left, right, pieces, n_seq * heads * CAP)
    sent, res, *weights = lax.optimization_barrier((sent, res, *weights))
    got = lax.all_to_all(
        sent.reshape(n_seq, heads * CAP * 4, HD), SEQ, split_axis=0, concat_axis=0, tiled=True
    ).reshape(n_seq * heads * CAP * 4, HD)
    res = res.reshape(n_seq * CAP * 4 * width // HD, HD)
    got_c = swap(got, HEAD, 1)
    got_x = swap(got, HEAD, 2)
    got_xc = swap(got_x, HEAD, 1)
    delivered = project(
        c[None].astype(jnp.int32),
        (got, got_c, got_x, got_xc),
        weights,
        res,
        layer_scale[None, :],
        n_seq * CAP,
    )
    return (delivered, refreshed)


def solution(mesh):
    devices = np.asarray(mesh.devices).reshape(2, 4, 2, 4, 2, 2)
    fine = Mesh(devices, SEQ + HEAD)
    in_specs = (
        P(SEQ, HEAD),
        P(SEQ, HEAD),
        P(SEQ, HEAD),
        P(SEQ, HEAD),
        P(HEAD),
        P(HEAD, None),
        P(SEQ),
        P(SEQ, HEAD),
        P(SEQ, HEAD),
        P(SEQ),
        P(SEQ),
        P(SEQ, None),
        P(None, HEAD),
        P(SEQ, None),
    )
    out_specs = (P(SEQ, HEAD), P(SEQ, HEAD))
    return jax.shard_map(shards, mesh=fine, in_specs=in_specs, out_specs=out_specs, check_vma=False)
```

```python
import math

import jax
import jax.numpy as jnp
import numpy as np
from jax import lax
from jax.experimental import pallas as pl
from jax.experimental.pallas import tpu as pltpu
from jax.sharding import Mesh, PartitionSpec as P

HD = 128
BLK = 16
SEG_MOST = 201
LIVE_MOST = 6
CAP = 3
HALO = 208
PAD = 256
TOK = 512
KT = 2048
NEG = -1e30
SEQ = ("xh", "y", "zh", "zp")
HEAD = ("xl", "c")
bf16 = jnp.bfloat16
f32 = jnp.float32


def rope_parts(positions):
    half = HD // 2
    freqs = 100.0 ** (-jnp.arange(half, dtype=f32) / half)
    angles = positions.astype(f32)[:, None] * freqs[None, :]
    return jnp.cos(angles), jnp.sin(angles)


def rotate(vectors, cosine, sine):
    half = HD // 2
    a, b = vectors[..., :half], vectors[..., half:]
    c, s = cosine[:, None, :], sine[:, None, :]
    return jnp.concatenate([a * c - b * s, b * c + a * s], axis=-1)


def pack_kernel(idx, k_ref, v_ref, out_ref):
    heads = out_ref.shape[0]
    for j in range(LIVE_MOST):
        rows = pl.ds(pl.multiple_of(idx[j] * BLK, BLK), BLK)
        k = jnp.where(j < idx[LIVE_MOST], k_ref[rows, :], jnp.inf).astype(bf16)
        v = v_ref[rows, :]
        for p in range(heads):
            out_ref[p, j * BLK : (j + 1) * BLK, :HD] = k[:, p * HD : (p + 1) * HD]
            out_ref[p, j * BLK : (j + 1) * BLK, HD:] = v[:, p * HD : (p + 1) * HD]


def rope_kernel(q_ref, k_ref, v_ref, c_ref, s_ref, extra_ref, out_ref):
    tokens = q_ref.shape[0]
    c = c_ref[...]
    s = s_ref[...]
    for h in range(out_ref.shape[0]):
        cols = slice(h * HD, (h + 1) * HD)
        for j, ref in enumerate((q_ref, k_ref)):
            x = ref[:, cols].astype(f32)
            turned = x * c + pltpu.roll(x, HD // 2, 1) * s
            out_ref[h, :tokens, j * HD : (j + 1) * HD] = turned.astype(bf16)
        out_ref[h, :tokens, 2 * HD :] = v_ref[:, cols]
        out_ref[h, tokens:, :] = extra_ref[...]


def attention_kernel(off, tgt, zp, *refs):
    chunks = 4
    ys = refs[:chunks]
    left, right = refs[chunks : chunks + 2]
    pieces = refs[chunks + 2 : -14]
    out, kc, vc, qs, kw, vw, ob, send, mx, ac, idcol, gathered, ids, sems = refs[-14:]
    i = pl.program_id(0)
    sources = off.shape[0] - 1
    slot_rows = LIVE_MOST * BLK
    coef = math.log2(math.e) / math.sqrt(HD)
    total = off[sources]

    @pl.when(i == 0)
    def _():
        copies = []
        row = 0
        for n, piece in enumerate(pieces):
            to = gathered.at[pl.ds(row, piece.shape[0])]
            copies.append(pltpu.make_async_copy(piece, to, sems.at[n]))
            row += piece.shape[0]
        for copy in copies:
            copy.start()
        vc[:, HD:] = jnp.ones((vc.shape[0], HD), bf16)
        vw[:, HD:] = jnp.ones((vw.shape[0], HD), bf16)
        for k, y in enumerate(ys):
            chunk = zp[0] ^ k
            dst = pl.ds(pl.multiple_of(chunk * TOK, TOK), TOK)
            qs[dst, :] = y[:TOK, :HD]
            dst = pl.ds(pl.multiple_of(PAD + chunk * TOK, PAD), TOK)
            kw[dst, :] = y[:TOK, HD : 2 * HD]
            vw[dst, :HD] = y[:TOK, 2 * HD :]
            line = y[TOK:, :].astype(f32)
            at = pl.multiple_of(PAD + chunk * TOK, PAD)
            ids[:, pl.ds(at, 3 * HD)] = line[0:1, :]
            at = pl.multiple_of(PAD + chunk * TOK + 3 * HD, HD)
            ids[:, pl.ds(at, HD)] = line[1:2, :HD]
        end = PAD + chunks * TOK
        gap = PAD - HALO
        kw[:gap, :] = jnp.zeros((gap, HD), bf16)
        vw[:gap, :HD] = jnp.zeros((gap, HD), bf16)
        kw[gap:PAD, :] = left[:HALO, :HD]
        vw[gap:PAD, :HD] = left[:HALO, HD:]
        kw[end : end + HALO, :] = right[:HALO, :HD]
        vw[end : end + HALO, :HD] = right[:HALO, HD:]
        ids[:, :PAD] = left[HALO:, :].astype(f32)[0:1, :]
        ids[:, end:] = right[HALO:, :].astype(f32)[0:1, :]
        kw[end + HALO :, :] = jnp.zeros((gap, HD), bf16)
        vw[end + HALO :, :HD] = jnp.zeros((gap, HD), bf16)
        send[...] = jnp.zeros(send.shape, f32)
        for copy in copies:
            copy.wait()

        def copy_source(s, carry):
            dst = pl.ds(pl.multiple_of(off[s], BLK), slot_rows)
            src = pl.ds(pl.multiple_of(s * slot_rows, BLK), slot_rows)
            kc[dst, :] = gathered[src, :HD]
            vc[dst, :HD] = gathered[src, HD:]
            return carry

        lax.fori_loop(0, sources, copy_source, 0, unroll=2)
        tail = pl.ds(pl.multiple_of(total, BLK), KT)
        kc[tail, :] = jnp.zeros((KT, HD), bf16)
        vc[tail, :HD] = jnp.zeros((KT, HD), bf16)

    base = pl.multiple_of(i * TOK, TOK)
    sub = 128
    parts = TOK // sub
    wide = sub + 2 * PAD
    for b in range(parts):
        line = ids[:, pl.ds(pl.multiple_of(base + PAD + b * sub, sub), sub)]
        idcol[b * sub : (b + 1) * sub, :] = jnp.transpose(jnp.broadcast_to(line, (sub, sub)))

    def scores(b, keys):
        q = qs[pl.ds(pl.multiple_of(base + b * sub, sub), sub), :]
        return lax.dot_general(q, keys, (((1,), (1,)), ((), ())), preferred_element_type=f32)

    def weigh(s, m):
        new = jnp.max(s, axis=1, keepdims=True)
        if m is not None:
            new = jnp.maximum(m, new)
        return new, jnp.exp2(s * coef - new * coef).astype(bf16)

    for b in range(parts):
        rows = pl.ds(pl.multiple_of(base + b * sub, sub), wide)
        s = scores(b, kw[rows, :])
        near = ids[:, rows]
        s = jnp.where(idcol[b * sub : (b + 1) * sub, :1] == near, s, NEG)
        new, w = weigh(s, None)
        mx[b * sub : (b + 1) * sub, :] = new
        ac[b * sub : (b + 1) * sub, :] = jnp.dot(w, vw[rows, :], preferred_element_type=f32)

    def visit(start, size, masked):
        rows = pl.ds(pl.multiple_of(start, size // 2), size)
        keys, values = kc[rows, :], vc[rows, :]

        def rows_of(b, carry):
            s = scores(b, keys)
            if masked:
                col = lax.broadcasted_iota(jnp.int32, s.shape, 1)
                s = jnp.where(col < total - start, s, NEG)
            here = pl.ds(pl.multiple_of(b * sub, sub), sub)
            m = mx[here, :]
            new, w = weigh(s, m)
            mx[here, :] = new
            part = jnp.dot(w, values, preferred_element_type=f32)
            ac[here, :] = ac[here, :] * jnp.exp2((m - new) * coef) + part
            return carry

        lax.fori_loop(0, parts, rows_of, 0, unroll=2 if masked else True)

    def loop(j, carry):
        visit(j * KT, KT, False)
        return carry

    full = total // KT
    rest = total - full * KT
    lax.fori_loop(0, full, loop, 0)

    for size in (KT, KT // 2, KT // 4):
        least = size // 2 if size > KT // 4 else 0

        @pl.when((rest > least) & (rest <= size))
        def _():
            visit(full * KT, size, True)

    ob[...] = ac[:, :HD] / ac[:, HD:]

    def place(r, carry):
        dst = tgt[(i ^ zp[0]) * (TOK // 4) + r] * 4
        send[pl.ds(pl.multiple_of(dst, 4), 4), :] = ob[pl.ds(pl.multiple_of(r * 4, 4), 4), :]
        return carry

    lax.fori_loop(0, TOK // 4, place, 0, unroll=8)

    @pl.when(i == pl.num_programs(0) - 1)
    def _():
        out[...] = send[...].astype(bf16)


def attend(off, tgt, zp, ys, left, right, pieces, slots):
    chunks = len(ys)
    sources = off.shape[0] - 1
    cache_most = sources * LIVE_MOST * BLK
    whole = pl.BlockSpec(memory_space=pltpu.VMEM)
    return pl.pallas_call(
        attention_kernel,
        out_shape=jax.ShapeDtypeStruct((slots * 4, HD), bf16),
        grid_spec=pltpu.PrefetchScalarGridSpec(
            num_scalar_prefetch=3,
            grid=(chunks,),
            in_specs=[whole] * (chunks + 2)
            + [pl.BlockSpec(memory_space=pl.ANY)] * len(pieces),
            out_specs=whole,
            scratch_shapes=[
                pltpu.VMEM((cache_most + KT, HD), bf16),
                pltpu.VMEM((cache_most + KT, 2 * HD), bf16),
                pltpu.VMEM((chunks * TOK, HD), bf16),
                pltpu.VMEM((chunks * TOK + 2 * PAD, HD), bf16),
                pltpu.VMEM((chunks * TOK + 2 * PAD, 2 * HD), bf16),
                pltpu.VMEM((TOK, HD), f32),
                pltpu.VMEM((slots * 4, HD), f32),
                pltpu.VMEM((TOK, 1), f32),
                pltpu.VMEM((TOK, 2 * HD), f32),
                pltpu.VMEM((TOK, 128), f32),
                pltpu.VMEM((cache_most, 2 * HD), bf16),
                pltpu.VMEM((1, chunks * TOK + 2 * PAD), f32),
                pltpu.SemaphoreType.DMA((len(pieces),)),
            ],
        ),
        compiler_params=pltpu.CompilerParams(
            dimension_semantics=("arbitrary",), vmem_limit_bytes=48 << 20
        ),
        cost_estimate=pl.CostEstimate(
            flops=4 * 2048 * 7168 * 128, bytes_accessed=8 << 20, transcendentals=2048 * 7168
        ),
    )(off, tgt, zp, *ys, left, right, *pieces)


def project_kernel(core, a0, a1, a2, a3, w0, w1, w2, w3, res, scale, mix, out, att, res32, proj):
    b = pl.program_id(0)
    c = core[0]
    groups = a0.shape[0] // (8 * 48)

    @pl.when(b == 0)
    def _():
        res32[...] = res[...].astype(f32)
        for k, a in enumerate((a0, a1, a2, a3)):

            def move(g, carry):
                to = pl.ds(pl.multiple_of((g * 2 + (c ^ (k % 2))) * 48, 16), 48)
                for p in range(8):
                    block = (k // 2) * 2 + (c ^ (p // 4))
                    src = pl.ds(pl.multiple_of(g * 384 + p * 48, 16), 48)
                    att[block, to, (p % 4) * HD : (p % 4 + 1) * HD] = a[src, :]
                return carry

            lax.fori_loop(0, groups, move, 0)

    total = None
    for k, w in enumerate((w0, w1, w2, w3)):
        part = jnp.dot(att[k], w[...], preferred_element_type=f32)
        total = part if total is None else total + part
    total = total * scale[...]
    slots = out.shape[0]
    per = w0.shape[1] // HD
    for d in range(per):
        proj[d * 4 * slots : (d + 1) * 4 * slots, :] = total[:, d * HD : (d + 1) * HD]
    for d in range(per):
        parts = []
        for t in range(4):
            new = proj[pl.ds(d * 4 * slots + t, slots, stride=4), :]
            old = res32[pl.ds(t * 8 + b * per + d, slots, stride=32), :]
            parts.append((old + new).astype(bf16))
        rows = jnp.concatenate(parts, axis=1)
        out[:, d * 4 * HD : (d + 1) * 4 * HD] = jnp.dot(
            rows, mix[...], preferred_element_type=f32
        ).astype(bf16)


def project(core, atts, weights, res, scale, slots):
    width = weights[0].shape[1]
    part = 256
    whole = pl.BlockSpec(memory_space=pltpu.VMEM)
    source = np.arange(4 * HD)
    mix = np.zeros((4 * HD, 4 * HD), np.float32)
    mix[source, (source % HD) * 4 + source // HD] = 1.0
    return pl.pallas_call(
        project_kernel,
        out_shape=jax.ShapeDtypeStruct((slots, 4 * width), bf16),
        grid_spec=pltpu.PrefetchScalarGridSpec(
            num_scalar_prefetch=1,
            grid=(width // part,),
            in_specs=[whole] * 4
            + [pl.BlockSpec((weights[0].shape[0], part), lambda b, *_: (0, b))] * 4
            + [whole, pl.BlockSpec((1, part), lambda b, *_: (0, b)), whole],
            out_specs=pl.BlockSpec((slots, 4 * part), lambda b, *_: (0, b)),
            scratch_shapes=[
                pltpu.VMEM((4, slots * 4, 4 * HD), bf16),
                pltpu.VMEM((slots * 32, HD), f32),
                pltpu.VMEM((slots * 4 * part // HD, HD), f32),
            ],
        ),
        compiler_params=pltpu.CompilerParams(
            dimension_semantics=("arbitrary",), vmem_limit_bytes=48 << 20
        ),
        cost_estimate=pl.CostEstimate(
            flops=2 * 768 * 2048 * 1024, bytes_accessed=16 << 20, transcendentals=0
        ),
    )(core, *atts, *weights, res, scale, jnp.asarray(mix, bf16))


def swap(x, axis, k):
    n = lax.axis_size(axis)
    return lax.ppermute(x, axis, [(i, i ^ k) for i in range(n)])


def tie(x, *others):
    return lax.optimization_barrier((x, *others))[0]


def shards(
    queries,
    keys_new,
    values_new,
    residual,
    layer_scale,
    out_weight,
    segment_ids,
    cache_keys,
    cache_values,
    block_live,
    recompute_block,
    recompute_hidden,
    key_weight,
    owners,
):
    tokens, columns = queries.shape
    heads = columns // HD
    n_head = lax.axis_size(HEAD)
    n_seq = lax.axis_size(SEQ)
    seq = lax.axis_index(SEQ)
    zp, c = (lax.axis_index(n) for n in ("zp", "c"))
    head = lax.axis_index(HEAD)
    merged_rows = tokens // 4
    n_group = n_seq // heads
    whole = pl.BlockSpec(memory_space=pltpu.VMEM)

    width = residual.shape[1]

    def weight_rows(j):
        return lax.dynamic_slice(out_weight, (0, (head ^ j) * width), (columns, width))

    weight_x = swap(weight_rows(2), HEAD, 2)

    marks = segment_ids + 1
    before = lax.ppermute(marks[tokens - PAD :], SEQ, [(i, i + 1) for i in range(n_seq - 1)])
    near = jnp.concatenate([before, marks])
    same = marks[:, None] == near[None, :]
    index = jnp.arange(PAD + tokens, dtype=jnp.int32)
    first = jnp.min(jnp.where(same, index[None, :], PAD + tokens), axis=1)
    cosine, sine = rope_parts(PAD + jnp.arange(tokens, dtype=jnp.int32) - first)

    extra = jnp.concatenate([marks, owners[:, 0]])
    extra = jnp.pad(extra, (0, BLK * 3 * HD - extra.shape[0])).astype(bf16).reshape(BLK, 3 * HD)
    qkv = pl.pallas_call(
        rope_kernel,
        out_shape=jax.ShapeDtypeStruct((heads, tokens + BLK, 3 * HD), bf16),
        in_specs=[whole] * 6,
        out_specs=whole,
    )(
        queries,
        keys_new,
        values_new,
        jnp.concatenate([cosine, cosine], axis=1),
        jnp.concatenate([-sine, sine], axis=1),
        extra,
    )

    cache_rows = cache_keys.shape[0]
    block = recompute_block[0]
    fresh = jnp.dot(recompute_hidden, key_weight, preferred_element_type=f32)
    fresh_rows = seq * cache_rows + block * BLK + jnp.arange(BLK, dtype=jnp.int32)
    fresh = rotate(fresh.reshape(BLK, heads, HD), *rope_parts(fresh_rows % SEG_MOST))
    fresh = fresh.reshape(BLK, columns).astype(bf16)
    refreshed = lax.dynamic_update_slice(cache_keys, fresh, (block * BLK, 0))

    live = block_live > 0
    n_blocks = block_live.shape[0]
    blocks = jnp.arange(n_blocks, dtype=jnp.int32)
    rank = jnp.sum(jnp.where(blocks[None, :] < blocks[:, None], live[None, :], False), axis=1)
    hit = live[None, :] & (rank[None, :] == jnp.arange(LIVE_MOST, dtype=jnp.int32)[:, None])
    order = jnp.sum(jnp.where(hit, blocks[None, :], 0), axis=1)
    order = jnp.concatenate([order, jnp.sum(live.astype(jnp.int32), keepdims=True)])
    kv = pl.pallas_call(
        pack_kernel,
        out_shape=jax.ShapeDtypeStruct((heads, LIVE_MOST * BLK, 2 * HD), bf16),
        grid_spec=pltpu.PrefetchScalarGridSpec(
            num_scalar_prefetch=1, grid=(), in_specs=[whole] * 2, out_specs=whole
        ),
    )(order, refreshed, cache_values)

    def spread(x, j):
        pairs = []
        for a in range(2):
            for b in range(heads):
                for d in range(2):
                    pairs.append(((a * heads + b) * 2 + d, (d * heads + (b ^ j)) * 2 + a))
        part = lax.dynamic_index_in_dim(x, zp ^ j, 0, keepdims=False)
        return lax.ppermute(part, ("zh", "zp", "c"), pairs)

    kv = tie(kv, before)
    cached = [spread(kv, j) for j in range(heads)]
    kv4 = jnp.concatenate(cached, axis=0)

    ys = [spread(qkv, j) for j in range(heads)]

    kv4 = tie(kv4, qkv, weight_x)
    kv8 = jnp.concatenate([kv4, swap(kv4, "xh", 1)], axis=0)
    kv32 = lax.all_gather(kv8, "y", axis=0, tiled=True)

    def slots_of(owner_rows):
        r = jnp.arange(merged_rows, dtype=jnp.int32)
        equal = owner_rows[:, :, None] == owner_rows[:, None, :]
        return jnp.sum((equal & (r[None, None, :] < r[None, :, None])).astype(jnp.int32), axis=2)

    own_target = owners[:, 0] * CAP + slots_of(owners[:, 0][None, :])[0]
    choose = (jnp.arange(n_seq * CAP, dtype=jnp.int32)[:, None] == own_target[None, :]).astype(bf16)
    residual = tie(residual, kv8, qkv)
    res = jnp.dot(
        choose, residual.reshape(merged_rows, 4 * width), preferred_element_type=f32
    ).astype(bf16)
    res = res.reshape(n_seq, CAP * 4 * width // HD, HD)

    edges = tie(tuple(ys), res)

    def edge(low, j, line, pairs):
        part = jnp.stack([t[low : low + HALO, HD:] for t in edges])
        part = lax.dynamic_index_in_dim(part, j, 0, keepdims=False)
        line = lax.dynamic_index_in_dim(jnp.stack([line(t[tokens : tokens + 2]) for t in edges]), j, 0)
        part = jnp.concatenate([part, jnp.pad(line, ((0, BLK - 1), (0, 0)))], axis=0)
        return lax.ppermute(part, ("xh", "y", "c"), pairs)

    ahead = [(i, i + 1) for i in range(n_group - 1)]
    none = jnp.zeros((PAD - HALO,), bf16)
    lead = tokens - HALO
    left = edge(
        lead,
        zp ^ (heads - 1),
        lambda t: jnp.concatenate([none, t[0, lead:], t[1, : tokens - 3 * HD]]),
        ahead,
    )
    right = edge(
        0, zp, lambda t: jnp.concatenate([t[0, :HALO], none]), [(j, i) for i, j in ahead]
    )

    pieces = [kv32, swap(tie(kv32, left, right), "c", 1)]

    def live_blocks(piece):
        firsts = piece.reshape(-1, LIVE_MOST, BLK, 2 * HD)[:, :, 0, 0]
        return jnp.sum(jnp.isfinite(firsts).astype(jnp.int32), axis=1)

    live_near = live_blocks(pieces[0])
    counts = jnp.concatenate([live_near, live_blocks(pieces[1])])
    every = jnp.arange(n_seq, dtype=jnp.int32)
    ends = jnp.arange(n_seq + 1, dtype=jnp.int32)
    off = jnp.sum(jnp.where(every[None, :] < ends[:, None], counts[None, :] * BLK, 0), axis=1)

    group_owners = jnp.stack([t[tokens + 1, HD : HD + merged_rows] for t in ys]).astype(jnp.int32)
    peer = (jnp.arange(heads, dtype=jnp.int32) ^ zp)[:, None]
    tgt = (group_owners * (heads * CAP) + peer * CAP + slots_of(group_owners)).reshape(-1)

    out_weight = tie(out_weight, left, right)
    weights = [
        weight_rows(0),
        swap(weight_rows(1), HEAD, 1),
        weight_x,
        swap(weight_rows(3), HEAD, 3),
    ]

    res = lax.all_to_all(tie(res, pieces[1], live_near), SEQ, split_axis=0, concat_axis=0, tiled=True)

    one = zp[None].astype(jnp.int32)
    sent = attend(off, tgt, one, ys, left, right, pieces, n_seq * heads * CAP)
    sent, res, *weights = lax.optimization_barrier((sent, res, *weights))
    got = lax.all_to_all(
        sent.reshape(n_seq, heads * CAP * 4, HD), SEQ, split_axis=0, concat_axis=0, tiled=True
    ).reshape(n_seq * heads * CAP * 4, HD)
    res = res.reshape(n_seq * CAP * 4 * width // HD, HD)
    got_c = swap(got, HEAD, 1)
    got_x = swap(got, HEAD, 2)
    got_xc = swap(got_x, HEAD, 1)
    delivered = project(
        c[None].astype(jnp.int32),
        (got, got_c, got_x, got_xc),
        weights,
        res,
        layer_scale[None, :],
        n_seq * CAP,
    )
    return (delivered, refreshed)


def solution(mesh):
    devices = np.asarray(mesh.devices).reshape(2, 4, 2, 4, 2, 2)
    fine = Mesh(devices, SEQ + HEAD)
    in_specs = (
        P(SEQ, HEAD),
        P(SEQ, HEAD),
        P(SEQ, HEAD),
        P(SEQ, HEAD),
        P(HEAD),
        P(HEAD, None),
        P(SEQ),
        P(SEQ, HEAD),
        P(SEQ, HEAD),
        P(SEQ),
        P(SEQ),
        P(SEQ, None),
        P(None, HEAD),
        P(SEQ, None),
    )
    out_specs = (P(SEQ, HEAD), P(SEQ, HEAD))
    return jax.shard_map(shards, mesh=fine, in_specs=in_specs, out_specs=out_specs, check_vma=False)
```

```python
import math

import jax
import jax.numpy as jnp
import numpy as np
from jax import lax
from jax.experimental import pallas as pl
from jax.experimental.pallas import tpu as pltpu
from jax.sharding import Mesh, PartitionSpec as P

HD = 128
BLK = 16
SEG_MOST = 201
LIVE_MOST = 6
CAP = 3
HALO = 208
PAD = 256
TOK = 512
KT = 2048
NEG = -1e30
SEQ = ("xh", "y", "zh", "zp")
HEAD = ("xl", "c")
bf16 = jnp.bfloat16
f32 = jnp.float32


def rope_parts(positions):
    half = HD // 2
    freqs = 100.0 ** (-jnp.arange(half, dtype=f32) / half)
    angles = positions.astype(f32)[:, None] * freqs[None, :]
    return jnp.cos(angles), jnp.sin(angles)


def rotate(vectors, cosine, sine):
    half = HD // 2
    a, b = vectors[..., :half], vectors[..., half:]
    c, s = cosine[:, None, :], sine[:, None, :]
    return jnp.concatenate([a * c - b * s, b * c + a * s], axis=-1)


def pack_kernel(idx, k_ref, v_ref, out_ref):
    heads = out_ref.shape[0]
    for j in range(LIVE_MOST):
        rows = pl.ds(pl.multiple_of(idx[j] * BLK, BLK), BLK)
        k = jnp.where(j < idx[LIVE_MOST], k_ref[rows, :], jnp.inf).astype(bf16)
        v = v_ref[rows, :]
        for p in range(heads):
            out_ref[p, j * BLK : (j + 1) * BLK, :HD] = k[:, p * HD : (p + 1) * HD]
            out_ref[p, j * BLK : (j + 1) * BLK, HD:] = v[:, p * HD : (p + 1) * HD]


def rope_kernel(q_ref, k_ref, v_ref, c_ref, s_ref, extra_ref, out_ref):
    tokens = q_ref.shape[0]
    c = c_ref[...]
    s = s_ref[...]
    for h in range(out_ref.shape[0]):
        cols = slice(h * HD, (h + 1) * HD)
        for j, ref in enumerate((q_ref, k_ref)):
            x = ref[:, cols].astype(f32)
            turned = x * c + pltpu.roll(x, HD // 2, 1) * s
            out_ref[h, :tokens, j * HD : (j + 1) * HD] = turned.astype(bf16)
        out_ref[h, :tokens, 2 * HD :] = v_ref[:, cols]
        out_ref[h, tokens:, :] = extra_ref[...]


def attention_kernel(off, tgt, zp, *refs):
    chunks = 4
    ys = refs[:chunks]
    left, right = refs[chunks : chunks + 2]
    pieces = refs[chunks + 2 : -14]
    out, kc, vc, qs, kw, vw, ob, send, mx, ac, idcol, gathered, ids, sems = refs[-14:]
    i = pl.program_id(0)
    sources = off.shape[0] - 1
    slot_rows = LIVE_MOST * BLK
    coef = math.log2(math.e) / math.sqrt(HD)
    total = off[sources]

    @pl.when(i == 0)
    def _():
        copies = []
        row = 0
        for n, piece in enumerate(pieces):
            to = gathered.at[pl.ds(row, piece.shape[0])]
            copies.append(pltpu.make_async_copy(piece, to, sems.at[n]))
            row += piece.shape[0]
        for copy in copies:
            copy.start()
        vc[:, HD:] = jnp.ones((vc.shape[0], HD), bf16)
        vw[:, HD:] = jnp.ones((vw.shape[0], HD), bf16)
        for k, y in enumerate(ys):
            chunk = zp[0] ^ k
            dst = pl.ds(pl.multiple_of(chunk * TOK, TOK), TOK)
            qs[dst, :] = y[:TOK, :HD]
            dst = pl.ds(pl.multiple_of(PAD + chunk * TOK, PAD), TOK)
            kw[dst, :] = y[:TOK, HD : 2 * HD]
            vw[dst, :HD] = y[:TOK, 2 * HD :]
            line = y[TOK:, :].astype(f32)
            at = pl.multiple_of(PAD + chunk * TOK, PAD)
            ids[:, pl.ds(at, 3 * HD)] = line[0:1, :]
            at = pl.multiple_of(PAD + chunk * TOK + 3 * HD, HD)
            ids[:, pl.ds(at, HD)] = line[1:2, :HD]
        end = PAD + chunks * TOK
        gap = PAD - HALO
        kw[:gap, :] = jnp.zeros((gap, HD), bf16)
        vw[:gap, :HD] = jnp.zeros((gap, HD), bf16)
        kw[gap:PAD, :] = left[:HALO, :HD]
        vw[gap:PAD, :HD] = left[:HALO, HD:]
        kw[end : end + HALO, :] = right[:HALO, :HD]
        vw[end : end + HALO, :HD] = right[:HALO, HD:]
        ids[:, :PAD] = left[HALO:, :].astype(f32)[0:1, :]
        ids[:, end:] = right[HALO:, :].astype(f32)[0:1, :]
        kw[end + HALO :, :] = jnp.zeros((gap, HD), bf16)
        vw[end + HALO :, :HD] = jnp.zeros((gap, HD), bf16)
        send[...] = jnp.zeros(send.shape, f32)
        for copy in copies:
            copy.wait()

        def copy_source(s, carry):
            dst = pl.ds(pl.multiple_of(off[s], BLK), slot_rows)
            src = pl.ds(pl.multiple_of(s * slot_rows, BLK), slot_rows)
            kc[dst, :] = gathered[src, :HD]
            vc[dst, :HD] = gathered[src, HD:]
            return carry

        lax.fori_loop(0, sources, copy_source, 0, unroll=2)
        tail = pl.ds(pl.multiple_of(total, BLK), KT)
        kc[tail, :] = jnp.zeros((KT, HD), bf16)
        vc[tail, :HD] = jnp.zeros((KT, HD), bf16)

    base = pl.multiple_of(i * TOK, TOK)
    sub = 256
    parts = TOK // sub
    wide = sub + 2 * PAD
    for b in range(parts):
        line = ids[:, pl.ds(pl.multiple_of(base + PAD + b * sub, sub), sub)]
        idcol[b * sub : (b + 1) * sub, :] = jnp.transpose(jnp.broadcast_to(line, (128, sub)))

    def scores(b, keys):
        q = qs[pl.ds(pl.multiple_of(base + b * sub, sub), sub), :]
        return lax.dot_general(q, keys, (((1,), (1,)), ((), ())), preferred_element_type=f32)

    def weigh(s, m):
        new = jnp.max(s, axis=1, keepdims=True)
        if m is not None:
            new = jnp.maximum(m, new)
        return new, jnp.exp2(s * coef - new * coef).astype(bf16)

    for b in range(parts):
        rows = pl.ds(pl.multiple_of(base + b * sub, sub), wide)
        s = scores(b, kw[rows, :])
        near = ids[:, rows]
        s = jnp.where(idcol[b * sub : (b + 1) * sub, :1] == near, s, NEG)
        new, w = weigh(s, None)
        mx[b * sub : (b + 1) * sub, :] = new
        ac[b * sub : (b + 1) * sub, :] = jnp.dot(w, vw[rows, :], preferred_element_type=f32)

    def visit(start, size, masked):
        rows = pl.ds(pl.multiple_of(start, size // 2), size)
        keys, values = kc[rows, :], vc[rows, :]

        def mask(s):
            if not masked:
                return s
            col = lax.broadcasted_iota(jnp.int32, s.shape, 1)
            return jnp.where(col < total - start, s, NEG)

        def absorb(b, s):
            here = pl.ds(pl.multiple_of(b * sub, sub), sub)
            m = mx[here, :]
            new, w = weigh(s, m)
            mx[here, :] = new
            part = jnp.dot(w, values, preferred_element_type=f32)
            ac[here, :] = ac[here, :] * jnp.exp2((m - new) * coef) + part

        if masked:

            def rows_of(b, carry):
                absorb(b, mask(scores(b, keys)))
                return carry

            lax.fori_loop(0, parts, rows_of, 0)
        else:
            ahead = scores(0, keys)
            for b in range(parts):
                s = ahead
                if b + 1 < parts:
                    ahead = scores(b + 1, keys)
                absorb(b, s)

    def loop(j, carry):
        visit(j * KT, KT, False)
        return carry

    full = total // KT
    rest = total - full * KT
    lax.fori_loop(0, full, loop, 0)

    for size in (KT, KT // 2, KT // 4):
        least = size // 2 if size > KT // 4 else 0

        @pl.when((rest > least) & (rest <= size))
        def _():
            visit(full * KT, size, True)

    ob[...] = ac[:, :HD] / ac[:, HD:]

    def place(r, carry):
        dst = tgt[(i ^ zp[0]) * (TOK // 4) + r] * 4
        send[pl.ds(pl.multiple_of(dst, 4), 4), :] = ob[pl.ds(pl.multiple_of(r * 4, 4), 4), :]
        return carry

    lax.fori_loop(0, TOK // 4, place, 0, unroll=8)

    @pl.when(i == pl.num_programs(0) - 1)
    def _():
        out[...] = send[...].astype(bf16)


def attend(off, tgt, zp, ys, left, right, pieces, slots):
    chunks = len(ys)
    sources = off.shape[0] - 1
    cache_most = sources * LIVE_MOST * BLK
    whole = pl.BlockSpec(memory_space=pltpu.VMEM)
    return pl.pallas_call(
        attention_kernel,
        out_shape=jax.ShapeDtypeStruct((slots * 4, HD), bf16),
        grid_spec=pltpu.PrefetchScalarGridSpec(
            num_scalar_prefetch=3,
            grid=(chunks,),
            in_specs=[whole] * (chunks + 2)
            + [pl.BlockSpec(memory_space=pl.ANY)] * len(pieces),
            out_specs=whole,
            scratch_shapes=[
                pltpu.VMEM((cache_most + KT, HD), bf16),
                pltpu.VMEM((cache_most + KT, 2 * HD), bf16),
                pltpu.VMEM((chunks * TOK, HD), bf16),
                pltpu.VMEM((chunks * TOK + 2 * PAD, HD), bf16),
                pltpu.VMEM((chunks * TOK + 2 * PAD, 2 * HD), bf16),
                pltpu.VMEM((TOK, HD), f32),
                pltpu.VMEM((slots * 4, HD), f32),
                pltpu.VMEM((TOK, 1), f32),
                pltpu.VMEM((TOK, 2 * HD), f32),
                pltpu.VMEM((TOK, 128), f32),
                pltpu.VMEM((cache_most, 2 * HD), bf16),
                pltpu.VMEM((1, chunks * TOK + 2 * PAD), f32),
                pltpu.SemaphoreType.DMA((len(pieces),)),
            ],
        ),
        compiler_params=pltpu.CompilerParams(
            dimension_semantics=("arbitrary",), vmem_limit_bytes=48 << 20
        ),
        cost_estimate=pl.CostEstimate(
            flops=4 * 2048 * 7168 * 128, bytes_accessed=8 << 20, transcendentals=2048 * 7168
        ),
    )(off, tgt, zp, *ys, left, right, *pieces)


def project_kernel(core, a0, a1, a2, a3, w0, w1, w2, w3, res, scale, mix, out, att, res32, proj):
    b = pl.program_id(0)
    c = core[0]
    groups = a0.shape[0] // (8 * 48)

    @pl.when(b == 0)
    def _():
        res32[...] = res[...].astype(f32)
        for k, a in enumerate((a0, a1, a2, a3)):

            def move(g, carry):
                to = pl.ds(pl.multiple_of((g * 2 + (c ^ (k % 2))) * 48, 16), 48)
                for p in range(8):
                    block = (k // 2) * 2 + (c ^ (p // 4))
                    src = pl.ds(pl.multiple_of(g * 384 + p * 48, 16), 48)
                    att[block, to, (p % 4) * HD : (p % 4 + 1) * HD] = a[src, :]
                return carry

            lax.fori_loop(0, groups, move, 0)

    total = None
    for k, w in enumerate((w0, w1, w2, w3)):
        part = jnp.dot(att[k], w[...], preferred_element_type=f32)
        total = part if total is None else total + part
    total = total * scale[...]
    slots = out.shape[0]
    per = w0.shape[1] // HD
    for d in range(per):
        proj[d * 4 * slots : (d + 1) * 4 * slots, :] = total[:, d * HD : (d + 1) * HD]
    for d in range(per):
        parts = []
        for t in range(4):
            new = proj[pl.ds(d * 4 * slots + t, slots, stride=4), :]
            old = res32[pl.ds(t * 8 + b * per + d, slots, stride=32), :]
            parts.append((old + new).astype(bf16))
        rows = jnp.concatenate(parts, axis=1)
        out[:, d * 4 * HD : (d + 1) * 4 * HD] = jnp.dot(
            rows, mix[...], preferred_element_type=f32
        ).astype(bf16)


def project(core, atts, weights, res, scale, slots):
    width = weights[0].shape[1]
    part = 256
    whole = pl.BlockSpec(memory_space=pltpu.VMEM)
    source = np.arange(4 * HD)
    mix = np.zeros((4 * HD, 4 * HD), np.float32)
    mix[source, (source % HD) * 4 + source // HD] = 1.0
    return pl.pallas_call(
        project_kernel,
        out_shape=jax.ShapeDtypeStruct((slots, 4 * width), bf16),
        grid_spec=pltpu.PrefetchScalarGridSpec(
            num_scalar_prefetch=1,
            grid=(width // part,),
            in_specs=[whole] * 4
            + [pl.BlockSpec((weights[0].shape[0], part), lambda b, *_: (0, b))] * 4
            + [whole, pl.BlockSpec((1, part), lambda b, *_: (0, b)), whole],
            out_specs=pl.BlockSpec((slots, 4 * part), lambda b, *_: (0, b)),
            scratch_shapes=[
                pltpu.VMEM((4, slots * 4, 4 * HD), bf16),
                pltpu.VMEM((slots * 32, HD), f32),
                pltpu.VMEM((slots * 4 * part // HD, HD), f32),
            ],
        ),
        compiler_params=pltpu.CompilerParams(
            dimension_semantics=("arbitrary",), vmem_limit_bytes=48 << 20
        ),
        cost_estimate=pl.CostEstimate(
            flops=2 * 768 * 2048 * 1024, bytes_accessed=16 << 20, transcendentals=0
        ),
    )(core, *atts, *weights, res, scale, jnp.asarray(mix, bf16))


def swap(x, axis, k):
    n = lax.axis_size(axis)
    return lax.ppermute(x, axis, [(i, i ^ k) for i in range(n)])


def tie(x, *others):
    return lax.optimization_barrier((x, *others))[0]


def shards(
    queries,
    keys_new,
    values_new,
    residual,
    layer_scale,
    out_weight,
    segment_ids,
    cache_keys,
    cache_values,
    block_live,
    recompute_block,
    recompute_hidden,
    key_weight,
    owners,
):
    tokens, columns = queries.shape
    heads = columns // HD
    n_head = lax.axis_size(HEAD)
    n_seq = lax.axis_size(SEQ)
    seq = lax.axis_index(SEQ)
    zp, c = (lax.axis_index(n) for n in ("zp", "c"))
    head = lax.axis_index(HEAD)
    merged_rows = tokens // 4
    n_group = n_seq // heads
    whole = pl.BlockSpec(memory_space=pltpu.VMEM)

    width = residual.shape[1]

    def weight_rows(j):
        return lax.dynamic_slice(out_weight, (0, (head ^ j) * width), (columns, width))

    weight_x = swap(weight_rows(2), HEAD, 2)

    marks = segment_ids + 1
    before = lax.ppermute(marks[tokens - PAD :], SEQ, [(i, i + 1) for i in range(n_seq - 1)])
    near = jnp.concatenate([before, marks])
    same = marks[:, None] == near[None, :]
    index = jnp.arange(PAD + tokens, dtype=jnp.int32)
    first = jnp.min(jnp.where(same, index[None, :], PAD + tokens), axis=1)
    cosine, sine = rope_parts(PAD + jnp.arange(tokens, dtype=jnp.int32) - first)

    extra = jnp.concatenate([marks, owners[:, 0]])
    extra = jnp.pad(extra, (0, BLK * 3 * HD - extra.shape[0])).astype(bf16).reshape(BLK, 3 * HD)
    qkv = pl.pallas_call(
        rope_kernel,
        out_shape=jax.ShapeDtypeStruct((heads, tokens + BLK, 3 * HD), bf16),
        in_specs=[whole] * 6,
        out_specs=whole,
    )(
        queries,
        keys_new,
        values_new,
        jnp.concatenate([cosine, cosine], axis=1),
        jnp.concatenate([-sine, sine], axis=1),
        extra,
    )

    cache_rows = cache_keys.shape[0]
    block = recompute_block[0]
    fresh = jnp.dot(recompute_hidden, key_weight, preferred_element_type=f32)
    fresh_rows = seq * cache_rows + block * BLK + jnp.arange(BLK, dtype=jnp.int32)
    fresh = rotate(fresh.reshape(BLK, heads, HD), *rope_parts(fresh_rows % SEG_MOST))
    fresh = fresh.reshape(BLK, columns).astype(bf16)
    refreshed = lax.dynamic_update_slice(cache_keys, fresh, (block * BLK, 0))

    live = block_live > 0
    n_blocks = block_live.shape[0]
    blocks = jnp.arange(n_blocks, dtype=jnp.int32)
    rank = jnp.sum(jnp.where(blocks[None, :] < blocks[:, None], live[None, :], False), axis=1)
    hit = live[None, :] & (rank[None, :] == jnp.arange(LIVE_MOST, dtype=jnp.int32)[:, None])
    order = jnp.sum(jnp.where(hit, blocks[None, :], 0), axis=1)
    order = jnp.concatenate([order, jnp.sum(live.astype(jnp.int32), keepdims=True)])
    kv = pl.pallas_call(
        pack_kernel,
        out_shape=jax.ShapeDtypeStruct((heads, LIVE_MOST * BLK, 2 * HD), bf16),
        grid_spec=pltpu.PrefetchScalarGridSpec(
            num_scalar_prefetch=1, grid=(), in_specs=[whole] * 2, out_specs=whole
        ),
    )(order, refreshed, cache_values)

    def spread(x, j):
        pairs = []
        for a in range(2):
            for b in range(heads):
                for d in range(2):
                    pairs.append(((a * heads + b) * 2 + d, (d * heads + (b ^ j)) * 2 + a))
        part = lax.dynamic_index_in_dim(x, zp ^ j, 0, keepdims=False)
        return lax.ppermute(part, ("zh", "zp", "c"), pairs)

    kv = tie(kv, before)
    cached = [spread(kv, j) for j in range(heads)]
    kv4 = jnp.concatenate(cached, axis=0)

    ys = [spread(qkv, j) for j in range(heads)]

    kv4 = tie(kv4, qkv, weight_x)
    kv8 = jnp.concatenate([kv4, swap(kv4, "xh", 1)], axis=0)
    kv32 = lax.all_gather(kv8, "y", axis=0, tiled=True)

    def slots_of(owner_rows):
        r = jnp.arange(merged_rows, dtype=jnp.int32)
        equal = owner_rows[:, :, None] == owner_rows[:, None, :]
        return jnp.sum((equal & (r[None, None, :] < r[None, :, None])).astype(jnp.int32), axis=2)

    own_target = owners[:, 0] * CAP + slots_of(owners[:, 0][None, :])[0]
    choose = (jnp.arange(n_seq * CAP, dtype=jnp.int32)[:, None] == own_target[None, :]).astype(bf16)
    residual = tie(residual, kv8, qkv)
    res = jnp.dot(
        choose, residual.reshape(merged_rows, 4 * width), preferred_element_type=f32
    ).astype(bf16)
    res = res.reshape(n_seq, CAP * 4 * width // HD, HD)

    edges = tie(tuple(ys), res)

    def edge(low, j, line, pairs):
        part = jnp.stack([t[low : low + HALO, HD:] for t in edges])
        part = lax.dynamic_index_in_dim(part, j, 0, keepdims=False)
        line = lax.dynamic_index_in_dim(jnp.stack([line(t[tokens : tokens + 2]) for t in edges]), j, 0)
        part = jnp.concatenate([part, jnp.pad(line, ((0, BLK - 1), (0, 0)))], axis=0)
        return lax.ppermute(part, ("xh", "y", "c"), pairs)

    ahead = [(i, i + 1) for i in range(n_group - 1)]
    none = jnp.zeros((PAD - HALO,), bf16)
    lead = tokens - HALO
    left = edge(
        lead,
        zp ^ (heads - 1),
        lambda t: jnp.concatenate([none, t[0, lead:], t[1, : tokens - 3 * HD]]),
        ahead,
    )
    right = edge(
        0, zp, lambda t: jnp.concatenate([t[0, :HALO], none]), [(j, i) for i, j in ahead]
    )

    pieces = [kv32, swap(tie(kv32, left, right), "c", 1)]

    def live_blocks(piece):
        firsts = piece.reshape(-1, LIVE_MOST, BLK, 2 * HD)[:, :, 0, 0]
        return jnp.sum(jnp.isfinite(firsts).astype(jnp.int32), axis=1)

    live_near = live_blocks(pieces[0])
    counts = jnp.concatenate([live_near, live_blocks(pieces[1])])
    every = jnp.arange(n_seq, dtype=jnp.int32)
    ends = jnp.arange(n_seq + 1, dtype=jnp.int32)
    off = jnp.sum(jnp.where(every[None, :] < ends[:, None], counts[None, :] * BLK, 0), axis=1)

    group_owners = jnp.stack([t[tokens + 1, HD : HD + merged_rows] for t in ys]).astype(jnp.int32)
    peer = (jnp.arange(heads, dtype=jnp.int32) ^ zp)[:, None]
    tgt = (group_owners * (heads * CAP) + peer * CAP + slots_of(group_owners)).reshape(-1)

    out_weight = tie(out_weight, left, right)
    weights = [
        weight_rows(0),
        swap(weight_rows(1), HEAD, 1),
        weight_x,
        swap(weight_rows(3), HEAD, 3),
    ]

    res = lax.all_to_all(tie(res, left, right), SEQ, split_axis=0, concat_axis=0, tiled=True)

    one = zp[None].astype(jnp.int32)
    sent = attend(off, tgt, one, ys, left, right, pieces, n_seq * heads * CAP)
    sent, res, *weights = lax.optimization_barrier((sent, res, *weights))
    got = lax.all_to_all(
        sent.reshape(n_seq, heads * CAP * 4, HD), SEQ, split_axis=0, concat_axis=0, tiled=True
    ).reshape(n_seq * heads * CAP * 4, HD)
    res = res.reshape(n_seq * CAP * 4 * width // HD, HD)
    got_c = swap(got, HEAD, 1)
    got_x = swap(got, HEAD, 2)
    got_xc = swap(got_x, HEAD, 1)
    delivered = project(
        c[None].astype(jnp.int32),
        (got, got_c, got_x, got_xc),
        weights,
        res,
        layer_scale[None, :],
        n_seq * CAP,
    )
    return (delivered, refreshed)


def solution(mesh):
    devices = np.asarray(mesh.devices).reshape(2, 4, 2, 4, 2, 2)
    fine = Mesh(devices, SEQ + HEAD)
    in_specs = (
        P(SEQ, HEAD),
        P(SEQ, HEAD),
        P(SEQ, HEAD),
        P(SEQ, HEAD),
        P(HEAD),
        P(HEAD, None),
        P(SEQ),
        P(SEQ, HEAD),
        P(SEQ, HEAD),
        P(SEQ),
        P(SEQ),
        P(SEQ, None),
        P(None, HEAD),
        P(SEQ, None),
    )
    out_specs = (P(SEQ, HEAD), P(SEQ, HEAD))
    return jax.shard_map(shards, mesh=fine, in_specs=in_specs, out_specs=out_specs, check_vma=False)
```

```python
import math

import jax
import jax.numpy as jnp
import numpy as np
from jax import lax
from jax.experimental import pallas as pl
from jax.experimental.pallas import tpu as pltpu
from jax.sharding import Mesh, PartitionSpec as P

HD = 128
BLK = 16
SEG_MOST = 201
LIVE_MOST = 6
CAP = 3
HALO = 208
PAD = 256
TOK = 512
KT = 2048
NEG = -1e30
SEQ = ("xh", "y", "zh", "zp")
HEAD = ("xl", "c")
bf16 = jnp.bfloat16
f32 = jnp.float32


def rope_parts(positions):
    half = HD // 2
    freqs = 100.0 ** (-jnp.arange(half, dtype=f32) / half)
    angles = positions.astype(f32)[:, None] * freqs[None, :]
    return jnp.cos(angles), jnp.sin(angles)


def rotate(vectors, cosine, sine):
    half = HD // 2
    a, b = vectors[..., :half], vectors[..., half:]
    c, s = cosine[:, None, :], sine[:, None, :]
    return jnp.concatenate([a * c - b * s, b * c + a * s], axis=-1)


def pack_kernel(idx, k_ref, v_ref, out_ref):
    heads = out_ref.shape[0]
    for j in range(LIVE_MOST):
        rows = pl.ds(pl.multiple_of(idx[j] * BLK, BLK), BLK)
        k = jnp.where(j < idx[LIVE_MOST], k_ref[rows, :], jnp.inf).astype(bf16)
        v = v_ref[rows, :]
        for p in range(heads):
            out_ref[p, j * BLK : (j + 1) * BLK, :HD] = k[:, p * HD : (p + 1) * HD]
            out_ref[p, j * BLK : (j + 1) * BLK, HD:] = v[:, p * HD : (p + 1) * HD]


def rope_kernel(q_ref, k_ref, v_ref, c_ref, s_ref, extra_ref, out_ref):
    tokens = q_ref.shape[0]
    c = c_ref[...]
    s = s_ref[...]
    for h in range(out_ref.shape[0]):
        cols = slice(h * HD, (h + 1) * HD)
        for j, ref in enumerate((q_ref, k_ref)):
            x = ref[:, cols].astype(f32)
            turned = x * c + pltpu.roll(x, HD // 2, 1) * s
            out_ref[h, :tokens, j * HD : (j + 1) * HD] = turned.astype(bf16)
        out_ref[h, :tokens, 2 * HD :] = v_ref[:, cols]
        out_ref[h, tokens:, :] = extra_ref[...]


def attention_kernel(off, tgt, zp, *refs):
    chunks = 4
    ys = refs[:chunks]
    left, right = refs[chunks : chunks + 2]
    pieces = refs[chunks + 2 : -14]
    out, kc, vc, qs, kw, vw, ob, send, mx, ac, idcol, gathered, ids, sems = refs[-14:]
    i = pl.program_id(0)
    sources = off.shape[0] - 1
    slot_rows = LIVE_MOST * BLK
    coef = math.log2(math.e) / math.sqrt(HD)
    total = off[sources]

    @pl.when(i == 0)
    def _():
        copies = []
        row = 0
        for n, piece in enumerate(pieces):
            to = gathered.at[pl.ds(row, piece.shape[0])]
            copies.append(pltpu.make_async_copy(piece, to, sems.at[n]))
            row += piece.shape[0]
        for copy in copies:
            copy.start()
        vc[:, HD:] = jnp.ones((vc.shape[0], HD), bf16)
        vw[:, HD:] = jnp.ones((vw.shape[0], HD), bf16)
        for k, y in enumerate(ys):
            chunk = zp[0] ^ k
            dst = pl.ds(pl.multiple_of(chunk * TOK, TOK), TOK)
            qs[dst, :] = y[:TOK, :HD]
            dst = pl.ds(pl.multiple_of(PAD + chunk * TOK, PAD), TOK)
            kw[dst, :] = y[:TOK, HD : 2 * HD]
            vw[dst, :HD] = y[:TOK, 2 * HD :]
            line = y[TOK:, :].astype(f32)
            at = pl.multiple_of(PAD + chunk * TOK, PAD)
            ids[:, pl.ds(at, 3 * HD)] = line[0:1, :]
            at = pl.multiple_of(PAD + chunk * TOK + 3 * HD, HD)
            ids[:, pl.ds(at, HD)] = line[1:2, :HD]
        end = PAD + chunks * TOK
        gap = PAD - HALO
        kw[:gap, :] = jnp.zeros((gap, HD), bf16)
        vw[:gap, :HD] = jnp.zeros((gap, HD), bf16)
        kw[gap:PAD, :] = left[:HALO, :HD]
        vw[gap:PAD, :HD] = left[:HALO, HD:]
        kw[end : end + HALO, :] = right[:HALO, :HD]
        vw[end : end + HALO, :HD] = right[:HALO, HD:]
        ids[:, :PAD] = left[HALO:, :].astype(f32)[0:1, :]
        ids[:, end:] = right[HALO:, :].astype(f32)[0:1, :]
        kw[end + HALO :, :] = jnp.zeros((gap, HD), bf16)
        vw[end + HALO :, :HD] = jnp.zeros((gap, HD), bf16)
        send[...] = jnp.zeros(send.shape, f32)
        for copy in copies:
            copy.wait()

        def copy_source(s, carry):
            dst = pl.ds(pl.multiple_of(off[s], BLK), slot_rows)
            src = pl.ds(pl.multiple_of(s * slot_rows, BLK), slot_rows)
            kc[dst, :] = gathered[src, :HD]
            vc[dst, :HD] = gathered[src, HD:]
            return carry

        lax.fori_loop(0, sources, copy_source, 0, unroll=2)
        tail = pl.ds(pl.multiple_of(total, BLK), KT)
        kc[tail, :] = jnp.zeros((KT, HD), bf16)
        vc[tail, :HD] = jnp.zeros((KT, HD), bf16)

    base = pl.multiple_of(i * TOK, TOK)
    sub = 256
    parts = TOK // sub
    wide = sub + 2 * PAD
    for b in range(parts):
        line = ids[:, pl.ds(pl.multiple_of(base + PAD + b * sub, sub), sub)]
        idcol[b * sub : (b + 1) * sub, :] = jnp.transpose(jnp.broadcast_to(line, (128, sub)))

    def scores(b, keys):
        q = qs[pl.ds(pl.multiple_of(base + b * sub, sub), sub), :]
        return lax.dot_general(q, keys, (((1,), (1,)), ((), ())), preferred_element_type=f32)

    def weigh(s, m):
        new = jnp.max(s, axis=1, keepdims=True)
        if m is not None:
            new = jnp.maximum(m, new)
        return new, jnp.exp2(s * coef - new * coef).astype(bf16)

    for b in range(parts):
        rows = pl.ds(pl.multiple_of(base + b * sub, sub), wide)
        s = scores(b, kw[rows, :])
        near = ids[:, rows]
        s = jnp.where(idcol[b * sub : (b + 1) * sub, :1] == near, s, NEG)
        new, w = weigh(s, None)
        mx[b * sub : (b + 1) * sub, :] = new
        ac[b * sub : (b + 1) * sub, :] = jnp.dot(w, vw[rows, :], preferred_element_type=f32)

    def visit(start, size, masked):
        rows = pl.ds(pl.multiple_of(start, size // 2), size)
        keys, values = kc[rows, :], vc[rows, :]

        def mask(s):
            if not masked:
                return s
            col = lax.broadcasted_iota(jnp.int32, s.shape, 1)
            return jnp.where(col < total - start, s, NEG)

        def absorb(b, s):
            here = pl.ds(pl.multiple_of(b * sub, sub), sub)
            m = mx[here, :]
            new, w = weigh(s, m)
            mx[here, :] = new
            part = jnp.dot(w, values, preferred_element_type=f32)
            ac[here, :] = ac[here, :] * jnp.exp2((m - new) * coef) + part

        if masked:

            def rows_of(b, carry):
                absorb(b, mask(scores(b, keys)))
                return carry

            lax.fori_loop(0, parts, rows_of, 0)
        else:
            ahead = scores(0, keys)
            for b in range(parts):
                s = ahead
                if b + 1 < parts:
                    ahead = scores(b + 1, keys)
                absorb(b, s)

    def loop(j, carry):
        visit(j * KT, KT, False)
        return carry

    full = total // KT
    rest = total - full * KT
    lax.fori_loop(0, full, loop, 0)

    for least, size in ((0, KT // 4), (KT // 4, KT)):

        @pl.when((rest > least) & (rest <= size))
        def _():
            visit(full * KT, size, True)

    ob[...] = ac[:, :HD] / ac[:, HD:]

    def place(r, carry):
        dst = tgt[(i ^ zp[0]) * (TOK // 4) + r] * 4
        send[pl.ds(pl.multiple_of(dst, 4), 4), :] = ob[pl.ds(pl.multiple_of(r * 4, 4), 4), :]
        return carry

    lax.fori_loop(0, TOK // 4, place, 0, unroll=8)

    @pl.when(i == pl.num_programs(0) - 1)
    def _():
        out[...] = send[...].astype(bf16)


def attend(off, tgt, zp, ys, left, right, pieces, slots):
    chunks = len(ys)
    sources = off.shape[0] - 1
    cache_most = sources * LIVE_MOST * BLK
    whole = pl.BlockSpec(memory_space=pltpu.VMEM)
    return pl.pallas_call(
        attention_kernel,
        out_shape=jax.ShapeDtypeStruct((slots * 4, HD), bf16),
        grid_spec=pltpu.PrefetchScalarGridSpec(
            num_scalar_prefetch=3,
            grid=(chunks,),
            in_specs=[whole] * (chunks + 2)
            + [pl.BlockSpec(memory_space=pl.ANY)] * len(pieces),
            out_specs=whole,
            scratch_shapes=[
                pltpu.VMEM((cache_most + KT, HD), bf16),
                pltpu.VMEM((cache_most + KT, 2 * HD), bf16),
                pltpu.VMEM((chunks * TOK, HD), bf16),
                pltpu.VMEM((chunks * TOK + 2 * PAD, HD), bf16),
                pltpu.VMEM((chunks * TOK + 2 * PAD, 2 * HD), bf16),
                pltpu.VMEM((TOK, HD), f32),
                pltpu.VMEM((slots * 4, HD), f32),
                pltpu.VMEM((TOK, 1), f32),
                pltpu.VMEM((TOK, 2 * HD), f32),
                pltpu.VMEM((TOK, 128), f32),
                pltpu.VMEM((cache_most, 2 * HD), bf16),
                pltpu.VMEM((1, chunks * TOK + 2 * PAD), f32),
                pltpu.SemaphoreType.DMA((len(pieces),)),
            ],
        ),
        compiler_params=pltpu.CompilerParams(
            dimension_semantics=("arbitrary",), vmem_limit_bytes=48 << 20
        ),
        cost_estimate=pl.CostEstimate(
            flops=4 * 2048 * 7168 * 128, bytes_accessed=8 << 20, transcendentals=2048 * 7168
        ),
    )(off, tgt, zp, *ys, left, right, *pieces)


def project_half(core, halves, weights, scale, att, proj):
    c = core[0]
    groups = halves[0].shape[0] // (8 * 48)

    @pl.when(pl.program_id(0) == 0)
    def _():
        for k, a in enumerate(halves):

            def move(g, carry):
                to = pl.ds(pl.multiple_of((g * 2 + (c ^ k)) * 48, 16), 48)
                for p in range(8):
                    src = pl.ds(pl.multiple_of(g * 384 + p * 48, 16), 48)
                    att[c ^ (p // 4), to, (p % 4) * HD : (p % 4 + 1) * HD] = a[src, :]
                return carry

            lax.fori_loop(0, groups, move, 0)

    total = jnp.dot(att[0], weights[0][...], preferred_element_type=f32)
    total = total + jnp.dot(att[1], weights[1][...], preferred_element_type=f32)
    total = total * scale[...]
    rows = total.shape[0]
    for d in range(total.shape[1] // HD):
        proj[d * rows : (d + 1) * rows, :] = total[:, d * HD : (d + 1) * HD]


def near_kernel(core, a0, a1, w0, w1, res, scale, out, att, proj, res32):
    b = pl.program_id(0)

    @pl.when(b == 0)
    def _():
        res32[...] = res[...].astype(f32)

    project_half(core, (a0, a1), (w0, w1), scale, att, proj)
    slots = out.shape[0] // 4
    per = out.shape[1] // HD
    for d in range(per):
        for t in range(4):
            new = proj[pl.ds(d * 4 * slots + t, slots, stride=4), :]
            old = res32[pl.ds(t * 8 + b * per + d, slots, stride=32), :]
            out[t * slots : (t + 1) * slots, d * HD : (d + 1) * HD] = old + new


def far_kernel(core, a0, a1, w0, w1, base, scale, mix, out, att, proj):
    project_half(core, (a0, a1), (w0, w1), scale, att, proj)
    slots = out.shape[0]
    for d in range(base.shape[1] // HD):
        parts = []
        for t in range(4):
            new = proj[pl.ds(d * 4 * slots + t, slots, stride=4), :]
            old = base[t * slots : (t + 1) * slots, d * HD : (d + 1) * HD]
            parts.append((old + new).astype(bf16))
        rows = jnp.concatenate(parts, axis=1)
        out[:, d * 4 * HD : (d + 1) * 4 * HD] = jnp.dot(
            rows, mix[...], preferred_element_type=f32
        ).astype(bf16)


def project(core, atts, weights, rest, scale, slots, near):
    width = weights[0].shape[1]
    part = 256
    whole = pl.BlockSpec(memory_space=pltpu.VMEM)
    blocks = lambda rows, columns: pl.BlockSpec((rows, columns), lambda b, *_: (0, b))
    specs = [whole] * 2 + [blocks(weights[0].shape[0], part)] * 2
    scratch = [
        pltpu.VMEM((2, slots * 4, 4 * HD), bf16),
        pltpu.VMEM((slots * 4 * part // HD, HD), f32),
    ]
    if near:
        specs += [whole, blocks(1, part)]
        scratch.append(pltpu.VMEM((slots * 32, HD), f32))
        out_shape = jax.ShapeDtypeStruct((slots * 4, width), f32)
        out_specs = blocks(slots * 4, part)
        given = (rest, scale)
    else:
        source = np.arange(4 * HD)
        mix = np.zeros((4 * HD, 4 * HD), np.float32)
        mix[source, (source % HD) * 4 + source // HD] = 1.0
        specs += [blocks(slots * 4, part), blocks(1, part), whole]
        out_shape = jax.ShapeDtypeStruct((slots, 4 * width), bf16)
        out_specs = blocks(slots, 4 * part)
        given = (rest, scale, jnp.asarray(mix, bf16))
    return pl.pallas_call(
        near_kernel if near else far_kernel,
        out_shape=out_shape,
        grid_spec=pltpu.PrefetchScalarGridSpec(
            num_scalar_prefetch=1,
            grid=(width // part,),
            in_specs=specs,
            out_specs=out_specs,
            scratch_shapes=scratch,
        ),
        compiler_params=pltpu.CompilerParams(
            dimension_semantics=("arbitrary",), vmem_limit_bytes=40 << 20
        ),
        cost_estimate=pl.CostEstimate(
            flops=2 * 768 * 1024 * 1024, bytes_accessed=10 << 20, transcendentals=0
        ),
    )(core, *atts, *weights, *given)


def swap(x, axis, k):
    n = lax.axis_size(axis)
    return lax.ppermute(x, axis, [(i, i ^ k) for i in range(n)])


def tie(x, *others):
    return lax.optimization_barrier((x, *others))[0]


def shards(
    queries,
    keys_new,
    values_new,
    residual,
    layer_scale,
    out_weight,
    segment_ids,
    cache_keys,
    cache_values,
    block_live,
    recompute_block,
    recompute_hidden,
    key_weight,
    owners,
):
    tokens, columns = queries.shape
    heads = columns // HD
    n_head = lax.axis_size(HEAD)
    n_seq = lax.axis_size(SEQ)
    seq = lax.axis_index(SEQ)
    zp, c = (lax.axis_index(n) for n in ("zp", "c"))
    head = lax.axis_index(HEAD)
    merged_rows = tokens // 4
    n_group = n_seq // heads
    whole = pl.BlockSpec(memory_space=pltpu.VMEM)

    width = residual.shape[1]

    def weight_rows(j):
        return lax.dynamic_slice(out_weight, (0, (head ^ j) * width), (columns, width))

    weight_x = swap(weight_rows(2), HEAD, 2)

    marks = segment_ids + 1
    before = lax.ppermute(marks[tokens - PAD :], SEQ, [(i, i + 1) for i in range(n_seq - 1)])
    near = jnp.concatenate([before, marks])
    same = marks[:, None] == near[None, :]
    index = jnp.arange(PAD + tokens, dtype=jnp.int32)
    first = jnp.min(jnp.where(same, index[None, :], PAD + tokens), axis=1)
    cosine, sine = rope_parts(PAD + jnp.arange(tokens, dtype=jnp.int32) - first)

    extra = jnp.concatenate([marks, owners[:, 0]])
    extra = jnp.pad(extra, (0, BLK * 3 * HD - extra.shape[0])).astype(bf16).reshape(BLK, 3 * HD)
    qkv = pl.pallas_call(
        rope_kernel,
        out_shape=jax.ShapeDtypeStruct((heads, tokens + BLK, 3 * HD), bf16),
        in_specs=[whole] * 6,
        out_specs=whole,
    )(
        queries,
        keys_new,
        values_new,
        jnp.concatenate([cosine, cosine], axis=1),
        jnp.concatenate([-sine, sine], axis=1),
        extra,
    )

    cache_rows = cache_keys.shape[0]
    block = recompute_block[0]
    fresh = jnp.dot(recompute_hidden, key_weight, preferred_element_type=f32)
    fresh_rows = seq * cache_rows + block * BLK + jnp.arange(BLK, dtype=jnp.int32)
    fresh = rotate(fresh.reshape(BLK, heads, HD), *rope_parts(fresh_rows % SEG_MOST))
    fresh = fresh.reshape(BLK, columns).astype(bf16)
    refreshed = lax.dynamic_update_slice(cache_keys, fresh, (block * BLK, 0))

    live = block_live > 0
    n_blocks = block_live.shape[0]
    blocks = jnp.arange(n_blocks, dtype=jnp.int32)
    rank = jnp.sum(jnp.where(blocks[None, :] < blocks[:, None], live[None, :], False), axis=1)
    hit = live[None, :] & (rank[None, :] == jnp.arange(LIVE_MOST, dtype=jnp.int32)[:, None])
    order = jnp.sum(jnp.where(hit, blocks[None, :], 0), axis=1)
    order = jnp.concatenate([order, jnp.sum(live.astype(jnp.int32), keepdims=True)])
    kv = pl.pallas_call(
        pack_kernel,
        out_shape=jax.ShapeDtypeStruct((heads, LIVE_MOST * BLK, 2 * HD), bf16),
        grid_spec=pltpu.PrefetchScalarGridSpec(
            num_scalar_prefetch=1, grid=(), in_specs=[whole] * 2, out_specs=whole
        ),
    )(order, refreshed, cache_values)

    def spread(x, j):
        pairs = []
        for a in range(2):
            for b in range(heads):
                for d in range(2):
                    pairs.append(((a * heads + b) * 2 + d, (d * heads + (b ^ j)) * 2 + a))
        part = lax.dynamic_index_in_dim(x, zp ^ j, 0, keepdims=False)
        return lax.ppermute(part, ("zh", "zp", "c"), pairs)

    kv = tie(kv, before)
    cached = [spread(kv, j) for j in range(heads)]
    kv4 = jnp.concatenate(cached, axis=0)

    ys = [spread(qkv, j) for j in range(heads)]

    kv4 = tie(kv4, qkv, weight_x)
    kv8 = jnp.concatenate([kv4, swap(kv4, "xh", 1)], axis=0)
    kv32 = lax.all_gather(kv8, "y", axis=0, tiled=True)

    def slots_of(owner_rows):
        r = jnp.arange(merged_rows, dtype=jnp.int32)
        equal = owner_rows[:, :, None] == owner_rows[:, None, :]
        return jnp.sum((equal & (r[None, None, :] < r[None, :, None])).astype(jnp.int32), axis=2)

    own_target = owners[:, 0] * CAP + slots_of(owners[:, 0][None, :])[0]
    choose = (jnp.arange(n_seq * CAP, dtype=jnp.int32)[:, None] == own_target[None, :]).astype(bf16)
    residual = tie(residual, kv8, qkv)
    res = jnp.dot(
        choose, residual.reshape(merged_rows, 4 * width), preferred_element_type=f32
    ).astype(bf16)
    res = res.reshape(n_seq, CAP * 4 * width // HD, HD)

    edges = tie(tuple(ys), res)

    def edge(low, j, line, pairs):
        part = jnp.stack([t[low : low + HALO, HD:] for t in edges])
        part = lax.dynamic_index_in_dim(part, j, 0, keepdims=False)
        line = lax.dynamic_index_in_dim(jnp.stack([line(t[tokens : tokens + 2]) for t in edges]), j, 0)
        part = jnp.concatenate([part, jnp.pad(line, ((0, BLK - 1), (0, 0)))], axis=0)
        return lax.ppermute(part, ("xh", "y", "c"), pairs)

    ahead = [(i, i + 1) for i in range(n_group - 1)]
    none = jnp.zeros((PAD - HALO,), bf16)
    lead = tokens - HALO
    left = edge(
        lead,
        zp ^ (heads - 1),
        lambda t: jnp.concatenate([none, t[0, lead:], t[1, : tokens - 3 * HD]]),
        ahead,
    )
    right = edge(
        0, zp, lambda t: jnp.concatenate([t[0, :HALO], none]), [(j, i) for i, j in ahead]
    )

    pieces = [kv32, swap(tie(kv32, left, right), "c", 1)]

    def live_blocks(piece):
        firsts = piece.reshape(-1, LIVE_MOST, BLK, 2 * HD)[:, :, 0, 0]
        return jnp.sum(jnp.isfinite(firsts).astype(jnp.int32), axis=1)

    live_near = live_blocks(pieces[0])
    counts = jnp.concatenate([live_near, live_blocks(pieces[1])])
    every = jnp.arange(n_seq, dtype=jnp.int32)
    ends = jnp.arange(n_seq + 1, dtype=jnp.int32)
    off = jnp.sum(jnp.where(every[None, :] < ends[:, None], counts[None, :] * BLK, 0), axis=1)

    group_owners = jnp.stack([t[tokens + 1, HD : HD + merged_rows] for t in ys]).astype(jnp.int32)
    peer = (jnp.arange(heads, dtype=jnp.int32) ^ zp)[:, None]
    tgt = (group_owners * (heads * CAP) + peer * CAP + slots_of(group_owners)).reshape(-1)

    out_weight = tie(out_weight, left, right)
    weights = [
        weight_rows(0),
        swap(weight_rows(1), HEAD, 1),
        weight_x,
        swap(weight_rows(3), HEAD, 3),
    ]

    res = lax.all_to_all(tie(res, left, right), SEQ, split_axis=0, concat_axis=0, tiled=True)

    one = zp[None].astype(jnp.int32)
    sent = attend(off, tgt, one, ys, left, right, pieces, n_seq * heads * CAP)
    sent, res, *weights = lax.optimization_barrier((sent, res, *weights))
    got = lax.all_to_all(
        sent.reshape(n_seq, heads * CAP * 4, HD), SEQ, split_axis=0, concat_axis=0, tiled=True
    ).reshape(n_seq * heads * CAP * 4, HD)
    res = res.reshape(n_seq * CAP * 4 * width // HD, HD)
    got_c = swap(got, HEAD, 1)
    got_x = swap(got, HEAD, 2)
    core = c[None].astype(jnp.int32)
    gain = layer_scale[None, :]
    slots = n_seq * CAP
    base = project(core, (got, got_c), weights[:2], res, gain, slots, True)
    got_xc = swap(tie(got_x, base), HEAD, 1)
    delivered = project(core, (got_x, got_xc), weights[2:], base, gain, slots, False)
    return (delivered, refreshed)


def solution(mesh):
    devices = np.asarray(mesh.devices).reshape(2, 4, 2, 4, 2, 2)
    fine = Mesh(devices, SEQ + HEAD)
    in_specs = (
        P(SEQ, HEAD),
        P(SEQ, HEAD),
        P(SEQ, HEAD),
        P(SEQ, HEAD),
        P(HEAD),
        P(HEAD, None),
        P(SEQ),
        P(SEQ, HEAD),
        P(SEQ, HEAD),
        P(SEQ),
        P(SEQ),
        P(SEQ, None),
        P(None, HEAD),
        P(SEQ, None),
    )
    out_specs = (P(SEQ, HEAD), P(SEQ, HEAD))
    return jax.shard_map(shards, mesh=fine, in_specs=in_specs, out_specs=out_specs, check_vma=False)
```

```python
import math

import jax
import jax.numpy as jnp
import numpy as np
from jax import lax
from jax.experimental import pallas as pl
from jax.experimental.pallas import tpu as pltpu
from jax.sharding import Mesh, PartitionSpec as P

HD = 128
BLK = 16
SEG_MOST = 201
LIVE_MOST = 6
CAP = 3
HALO = 208
PAD = 256
TOK = 512
KT = 2048
NEG = -1e30
SEQ = ("xh", "y", "zh", "zp")
HEAD = ("xl", "c")
bf16 = jnp.bfloat16
f32 = jnp.float32


def rope_parts(positions):
    half = HD // 2
    freqs = 100.0 ** (-jnp.arange(half, dtype=f32) / half)
    angles = positions.astype(f32)[:, None] * freqs[None, :]
    return jnp.cos(angles), jnp.sin(angles)


def rotate(vectors, cosine, sine):
    half = HD // 2
    a, b = vectors[..., :half], vectors[..., half:]
    c, s = cosine[:, None, :], sine[:, None, :]
    return jnp.concatenate([a * c - b * s, b * c + a * s], axis=-1)


def pack_kernel(idx, k_ref, v_ref, out_ref):
    heads = out_ref.shape[0]
    for j in range(LIVE_MOST):
        rows = pl.ds(pl.multiple_of(idx[j] * BLK, BLK), BLK)
        k = jnp.where(j < idx[LIVE_MOST], k_ref[rows, :], jnp.inf).astype(bf16)
        v = v_ref[rows, :]
        for p in range(heads):
            out_ref[p, j * BLK : (j + 1) * BLK, :HD] = k[:, p * HD : (p + 1) * HD]
            out_ref[p, j * BLK : (j + 1) * BLK, HD:] = v[:, p * HD : (p + 1) * HD]


def rope_kernel(q_ref, k_ref, v_ref, c_ref, s_ref, extra_ref, out_ref):
    tokens = q_ref.shape[0]
    c = c_ref[...]
    s = s_ref[...]
    for h in range(out_ref.shape[0]):
        cols = slice(h * HD, (h + 1) * HD)
        for j, ref in enumerate((q_ref, k_ref)):
            x = ref[:, cols].astype(f32)
            turned = x * c + pltpu.roll(x, HD // 2, 1) * s
            out_ref[h, :tokens, j * HD : (j + 1) * HD] = turned.astype(bf16)
        out_ref[h, :tokens, 2 * HD :] = v_ref[:, cols]
        out_ref[h, tokens:, :] = extra_ref[...]


def attention_kernel(off, tgt, zp, *refs):
    chunks = 4
    ys = refs[:chunks]
    left, right = refs[chunks : chunks + 2]
    pieces = refs[chunks + 2 : -14]
    out, kc, vc, qs, kw, vw, ob, send, mx, ac, idcol, gathered, ids, sems = refs[-14:]
    i = pl.program_id(0)
    sources = off.shape[0] - 1
    slot_rows = LIVE_MOST * BLK
    coef = math.log2(math.e) / math.sqrt(HD)
    total = off[sources]

    @pl.when(i == 0)
    def _():
        copies = []
        row = 0
        for n, piece in enumerate(pieces):
            to = gathered.at[pl.ds(row, piece.shape[0])]
            copies.append(pltpu.make_async_copy(piece, to, sems.at[n]))
            row += piece.shape[0]
        for copy in copies:
            copy.start()
        vc[:, HD:] = jnp.ones((vc.shape[0], HD), bf16)
        vw[:, HD:] = jnp.ones((vw.shape[0], HD), bf16)
        for k, y in enumerate(ys):
            chunk = zp[0] ^ k
            dst = pl.ds(pl.multiple_of(chunk * TOK, TOK), TOK)
            qs[dst, :] = y[:TOK, :HD]
            dst = pl.ds(pl.multiple_of(PAD + chunk * TOK, PAD), TOK)
            kw[dst, :] = y[:TOK, HD : 2 * HD]
            vw[dst, :HD] = y[:TOK, 2 * HD :]
            line = y[TOK:, :].astype(f32)
            at = pl.multiple_of(PAD + chunk * TOK, PAD)
            ids[:, pl.ds(at, 3 * HD)] = line[0:1, :]
            at = pl.multiple_of(PAD + chunk * TOK + 3 * HD, HD)
            ids[:, pl.ds(at, HD)] = line[1:2, :HD]
        end = PAD + chunks * TOK
        gap = PAD - HALO
        kw[:gap, :] = jnp.zeros((gap, HD), bf16)
        vw[:gap, :HD] = jnp.zeros((gap, HD), bf16)
        kw[gap:PAD, :] = left[:HALO, :HD]
        vw[gap:PAD, :HD] = left[:HALO, HD:]
        kw[end : end + HALO, :] = right[:HALO, :HD]
        vw[end : end + HALO, :HD] = right[:HALO, HD:]
        ids[:, :PAD] = left[HALO:, :].astype(f32)[0:1, :]
        ids[:, end:] = right[HALO:, :].astype(f32)[0:1, :]
        kw[end + HALO :, :] = jnp.zeros((gap, HD), bf16)
        vw[end + HALO :, :HD] = jnp.zeros((gap, HD), bf16)
        send[...] = jnp.zeros(send.shape, f32)
        for copy in copies:
            copy.wait()

        def copy_source(s, carry):
            dst = pl.ds(pl.multiple_of(off[s], BLK), slot_rows)
            src = pl.ds(pl.multiple_of(s * slot_rows, BLK), slot_rows)
            kc[dst, :] = gathered[src, :HD]
            vc[dst, :HD] = gathered[src, HD:]
            return carry

        lax.fori_loop(0, sources, copy_source, 0, unroll=2)
        tail = pl.ds(pl.multiple_of(total, BLK), KT)
        kc[tail, :] = jnp.zeros((KT, HD), bf16)
        vc[tail, :HD] = jnp.zeros((KT, HD), bf16)

    base = pl.multiple_of(i * TOK, TOK)
    sub = 256
    parts = TOK // sub
    wide = sub + 2 * PAD
    for b in range(parts):
        line = ids[:, pl.ds(pl.multiple_of(base + PAD + b * sub, sub), sub)]
        idcol[b * sub : (b + 1) * sub, :] = jnp.transpose(jnp.broadcast_to(line, (128, sub)))

    def scores(b, keys):
        q = qs[pl.ds(pl.multiple_of(base + b * sub, sub), sub), :]
        return lax.dot_general(q, keys, (((1,), (1,)), ((), ())), preferred_element_type=f32)

    def weigh(s, m):
        new = jnp.max(s, axis=1, keepdims=True)
        if m is not None:
            new = jnp.maximum(m, new)
        return new, jnp.exp2(s * coef - new * coef).astype(bf16)

    for b in range(parts):
        rows = pl.ds(pl.multiple_of(base + b * sub, sub), wide)
        s = scores(b, kw[rows, :])
        near = ids[:, rows]
        s = jnp.where(idcol[b * sub : (b + 1) * sub, :1] == near, s, NEG)
        new, w = weigh(s, None)
        mx[b * sub : (b + 1) * sub, :] = new
        ac[b * sub : (b + 1) * sub, :] = jnp.dot(w, vw[rows, :], preferred_element_type=f32)

    def visit(start, size, masked):
        rows = pl.ds(pl.multiple_of(start, size // 2), size)
        keys, values = kc[rows, :], vc[rows, :]

        def mask(s):
            if not masked:
                return s
            col = lax.broadcasted_iota(jnp.int32, s.shape, 1)
            return jnp.where(col < total - start, s, NEG)

        def absorb(b, s):
            here = pl.ds(pl.multiple_of(b * sub, sub), sub)
            m = mx[here, :]
            new, w = weigh(s, m)
            mx[here, :] = new
            part = jnp.dot(w, values, preferred_element_type=f32)
            ac[here, :] = ac[here, :] * jnp.exp2((m - new) * coef) + part

        if masked:

            def rows_of(b, carry):
                absorb(b, mask(scores(b, keys)))
                return carry

            lax.fori_loop(0, parts, rows_of, 0)
        else:
            ahead = scores(0, keys)
            for b in range(parts):
                s = ahead
                if b + 1 < parts:
                    ahead = scores(b + 1, keys)
                absorb(b, s)

    def loop(j, carry):
        visit(j * KT, KT, False)
        return carry

    full = total // KT
    rest = total - full * KT
    lax.fori_loop(0, full, loop, 0)

    for least, size in ((0, KT // 4), (KT // 4, KT)):

        @pl.when((rest > least) & (rest <= size))
        def _():
            visit(full * KT, size, True)

    ob[...] = ac[:, :HD] / ac[:, HD:]

    def place(r, carry):
        dst = tgt[(i ^ zp[0]) * (TOK // 4) + r] * 4
        send[pl.ds(pl.multiple_of(dst, 4), 4), :] = ob[pl.ds(pl.multiple_of(r * 4, 4), 4), :]
        return carry

    lax.fori_loop(0, TOK // 4, place, 0, unroll=8)

    @pl.when(i == pl.num_programs(0) - 1)
    def _():
        out[...] = send[...].astype(bf16)


def attend(off, tgt, zp, ys, left, right, pieces, slots):
    chunks = len(ys)
    sources = off.shape[0] - 1
    cache_most = sources * LIVE_MOST * BLK
    whole = pl.BlockSpec(memory_space=pltpu.VMEM)
    return pl.pallas_call(
        attention_kernel,
        out_shape=jax.ShapeDtypeStruct((slots * 4, HD), bf16),
        grid_spec=pltpu.PrefetchScalarGridSpec(
            num_scalar_prefetch=3,
            grid=(chunks,),
            in_specs=[whole] * (chunks + 2)
            + [pl.BlockSpec(memory_space=pl.ANY)] * len(pieces),
            out_specs=whole,
            scratch_shapes=[
                pltpu.VMEM((cache_most + KT, HD), bf16),
                pltpu.VMEM((cache_most + KT, 2 * HD), bf16),
                pltpu.VMEM((chunks * TOK, HD), bf16),
                pltpu.VMEM((chunks * TOK + 2 * PAD, HD), bf16),
                pltpu.VMEM((chunks * TOK + 2 * PAD, 2 * HD), bf16),
                pltpu.VMEM((TOK, HD), f32),
                pltpu.VMEM((slots * 4, HD), f32),
                pltpu.VMEM((TOK, 1), f32),
                pltpu.VMEM((TOK, 2 * HD), f32),
                pltpu.VMEM((TOK, 128), f32),
                pltpu.VMEM((cache_most, 2 * HD), bf16),
                pltpu.VMEM((1, chunks * TOK + 2 * PAD), f32),
                pltpu.SemaphoreType.DMA((len(pieces),)),
            ],
        ),
        compiler_params=pltpu.CompilerParams(
            dimension_semantics=("arbitrary",), vmem_limit_bytes=48 << 20
        ),
        cost_estimate=pl.CostEstimate(
            flops=4 * 2048 * 7168 * 128, bytes_accessed=8 << 20, transcendentals=2048 * 7168
        ),
    )(off, tgt, zp, *ys, left, right, *pieces)


def project_half(core, halves, weights, scale, att, proj):
    c = core[0]
    groups = halves[0].shape[0] // (8 * 48)

    @pl.when(pl.program_id(0) == 0)
    def _():
        for k, a in enumerate(halves):

            def move(g, carry):
                to = pl.ds(pl.multiple_of((g * 2 + (c ^ k)) * 48, 16), 48)
                for p in range(8):
                    src = pl.ds(pl.multiple_of(g * 384 + p * 48, 16), 48)
                    att[c ^ (p // 4), to, (p % 4) * HD : (p % 4 + 1) * HD] = a[src, :]
                return carry

            lax.fori_loop(0, groups, move, 0)

    total = jnp.dot(att[0], weights[0][...], preferred_element_type=f32)
    total = total + jnp.dot(att[1], weights[1][...], preferred_element_type=f32)
    total = total * scale[...]
    rows = total.shape[0]
    for d in range(total.shape[1] // HD):
        proj[d * rows : (d + 1) * rows, :] = total[:, d * HD : (d + 1) * HD]


def near_kernel(core, a0, a1, w0, w1, res, scale, out, att, proj, res32):
    b = pl.program_id(0)

    @pl.when(b == 0)
    def _():
        res32[...] = res[...].astype(f32)

    project_half(core, (a0, a1), (w0, w1), scale, att, proj)
    slots = out.shape[0] // 4
    per = out.shape[1] // HD
    for d in range(per):
        for t in range(4):
            new = proj[pl.ds(d * 4 * slots + t, slots, stride=4), :]
            old = res32[pl.ds(t * 8 + b * per + d, slots, stride=32), :]
            out[t * slots : (t + 1) * slots, d * HD : (d + 1) * HD] = old + new


def far_kernel(core, a0, a1, w0, w1, base, scale, mix, out, att, proj):
    project_half(core, (a0, a1), (w0, w1), scale, att, proj)
    slots = out.shape[0]
    for d in range(base.shape[1] // HD):
        parts = []
        for t in range(4):
            new = proj[pl.ds(d * 4 * slots + t, slots, stride=4), :]
            old = base[t * slots : (t + 1) * slots, d * HD : (d + 1) * HD]
            parts.append((old + new).astype(bf16))
        rows = jnp.concatenate(parts, axis=1)
        out[:, d * 4 * HD : (d + 1) * 4 * HD] = jnp.dot(
            rows, mix[...], preferred_element_type=f32
        ).astype(bf16)


def project(core, atts, weights, rest, scale, slots, near):
    width = weights[0].shape[1]
    part = 256
    whole = pl.BlockSpec(memory_space=pltpu.VMEM)
    blocks = lambda rows, columns: pl.BlockSpec((rows, columns), lambda b, *_: (0, b))
    specs = [whole] * 2 + [blocks(weights[0].shape[0], part)] * 2
    scratch = [
        pltpu.VMEM((2, slots * 4, 4 * HD), bf16),
        pltpu.VMEM((slots * 4 * part // HD, HD), f32),
    ]
    if near:
        specs += [whole, blocks(1, part)]
        scratch.append(pltpu.VMEM((slots * 32, HD), f32))
        out_shape = jax.ShapeDtypeStruct((slots * 4, width), f32)
        out_specs = blocks(slots * 4, part)
        given = (rest, scale)
    else:
        source = np.arange(4 * HD)
        mix = np.zeros((4 * HD, 4 * HD), np.float32)
        mix[source, (source % HD) * 4 + source // HD] = 1.0
        specs += [blocks(slots * 4, part), blocks(1, part), whole]
        out_shape = jax.ShapeDtypeStruct((slots, 4 * width), bf16)
        out_specs = blocks(slots, 4 * part)
        given = (rest, scale, jnp.asarray(mix, bf16))
    return pl.pallas_call(
        near_kernel if near else far_kernel,
        out_shape=out_shape,
        grid_spec=pltpu.PrefetchScalarGridSpec(
            num_scalar_prefetch=1,
            grid=(width // part,),
            in_specs=specs,
            out_specs=out_specs,
            scratch_shapes=scratch,
        ),
        compiler_params=pltpu.CompilerParams(
            dimension_semantics=("arbitrary",), vmem_limit_bytes=40 << 20
        ),
        cost_estimate=pl.CostEstimate(
            flops=2 * 768 * 1024 * 1024, bytes_accessed=10 << 20, transcendentals=0
        ),
    )(core, *atts, *weights, *given)


def swap(x, axis, k):
    n = lax.axis_size(axis)
    return lax.ppermute(x, axis, [(i, i ^ k) for i in range(n)])


def tie(x, *others):
    return lax.optimization_barrier((x, *others))[0]


def shards(
    queries,
    keys_new,
    values_new,
    residual,
    layer_scale,
    out_weight,
    segment_ids,
    cache_keys,
    cache_values,
    block_live,
    recompute_block,
    recompute_hidden,
    key_weight,
    owners,
):
    tokens, columns = queries.shape
    heads = columns // HD
    n_head = lax.axis_size(HEAD)
    n_seq = lax.axis_size(SEQ)
    seq = lax.axis_index(SEQ)
    zp, c = (lax.axis_index(n) for n in ("zp", "c"))
    head = lax.axis_index(HEAD)
    merged_rows = tokens // 4
    n_group = n_seq // heads
    whole = pl.BlockSpec(memory_space=pltpu.VMEM)

    width = residual.shape[1]

    def weight_rows(j):
        return lax.dynamic_slice(out_weight, (0, (head ^ j) * width), (columns, width))

    weight_x = swap(weight_rows(2), HEAD, 2)

    marks = segment_ids + 1
    before = lax.ppermute(marks[tokens - PAD :], SEQ, [(i, i + 1) for i in range(n_seq - 1)])
    near = jnp.concatenate([before, marks])
    same = marks[:, None] == near[None, :]
    index = jnp.arange(PAD + tokens, dtype=jnp.int32)
    first = jnp.min(jnp.where(same, index[None, :], PAD + tokens), axis=1)
    cosine, sine = rope_parts(PAD + jnp.arange(tokens, dtype=jnp.int32) - first)

    extra = jnp.concatenate([marks, owners[:, 0]])
    extra = jnp.pad(extra, (0, BLK * 3 * HD - extra.shape[0])).astype(bf16).reshape(BLK, 3 * HD)
    qkv = pl.pallas_call(
        rope_kernel,
        out_shape=jax.ShapeDtypeStruct((heads, tokens + BLK, 3 * HD), bf16),
        in_specs=[whole] * 6,
        out_specs=whole,
    )(
        queries,
        keys_new,
        values_new,
        jnp.concatenate([cosine, cosine], axis=1),
        jnp.concatenate([-sine, sine], axis=1),
        extra,
    )

    cache_rows = cache_keys.shape[0]
    block = recompute_block[0]
    fresh = jnp.dot(recompute_hidden, key_weight, preferred_element_type=f32)
    fresh_rows = seq * cache_rows + block * BLK + jnp.arange(BLK, dtype=jnp.int32)
    fresh = rotate(fresh.reshape(BLK, heads, HD), *rope_parts(fresh_rows % SEG_MOST))
    fresh = fresh.reshape(BLK, columns).astype(bf16)
    refreshed = lax.dynamic_update_slice(cache_keys, fresh, (block * BLK, 0))

    live = block_live > 0
    n_blocks = block_live.shape[0]
    blocks = jnp.arange(n_blocks, dtype=jnp.int32)
    rank = jnp.sum(jnp.where(blocks[None, :] < blocks[:, None], live[None, :], False), axis=1)
    hit = live[None, :] & (rank[None, :] == jnp.arange(LIVE_MOST, dtype=jnp.int32)[:, None])
    order = jnp.sum(jnp.where(hit, blocks[None, :], 0), axis=1)
    order = jnp.concatenate([order, jnp.sum(live.astype(jnp.int32), keepdims=True)])
    kv = pl.pallas_call(
        pack_kernel,
        out_shape=jax.ShapeDtypeStruct((heads, LIVE_MOST * BLK, 2 * HD), bf16),
        grid_spec=pltpu.PrefetchScalarGridSpec(
            num_scalar_prefetch=1, grid=(), in_specs=[whole] * 2, out_specs=whole
        ),
    )(order, refreshed, cache_values)

    def spread(x, j):
        pairs = []
        for a in range(2):
            for b in range(heads):
                for d in range(2):
                    pairs.append(((a * heads + b) * 2 + d, (d * heads + (b ^ j)) * 2 + a))
        part = lax.dynamic_index_in_dim(x, zp ^ j, 0, keepdims=False)
        return lax.ppermute(part, ("zh", "zp", "c"), pairs)

    kv = tie(kv, before)
    cached = [spread(kv, j) for j in range(heads)]
    kv4 = jnp.concatenate(cached, axis=0)

    ys = [spread(qkv, j) for j in range(heads)]

    kv4 = tie(kv4, qkv, weight_x)
    kv8 = jnp.concatenate([kv4, swap(kv4, "xh", 1)], axis=0)
    kv32 = lax.all_gather(kv8, "y", axis=0, tiled=True)

    def slots_of(owner_rows):
        r = jnp.arange(merged_rows, dtype=jnp.int32)
        equal = owner_rows[:, :, None] == owner_rows[:, None, :]
        return jnp.sum((equal & (r[None, None, :] < r[None, :, None])).astype(jnp.int32), axis=2)

    own_target = owners[:, 0] * CAP + slots_of(owners[:, 0][None, :])[0]
    choose = (jnp.arange(n_seq * CAP, dtype=jnp.int32)[:, None] == own_target[None, :]).astype(bf16)
    residual = tie(residual, kv8, qkv)
    res = jnp.dot(
        choose, residual.reshape(merged_rows, 4 * width), preferred_element_type=f32
    ).astype(bf16)
    res = res.reshape(n_seq, CAP * 4 * width // HD, HD)

    out_weight = tie(out_weight, kv8, qkv)
    rows_c, rows_xc = weight_rows(1), weight_rows(3)
    edges = tie(tuple(ys), res, rows_c, rows_xc)

    def edge(low, j, line, pairs):
        part = jnp.stack([t[low : low + HALO, HD:] for t in edges])
        part = lax.dynamic_index_in_dim(part, j, 0, keepdims=False)
        line = lax.dynamic_index_in_dim(jnp.stack([line(t[tokens : tokens + 2]) for t in edges]), j, 0)
        part = jnp.concatenate([part, jnp.pad(line, ((0, BLK - 1), (0, 0)))], axis=0)
        return lax.ppermute(part, ("xh", "y", "c"), pairs)

    ahead = [(i, i + 1) for i in range(n_group - 1)]
    none = jnp.zeros((PAD - HALO,), bf16)
    lead = tokens - HALO
    left = edge(
        lead,
        zp ^ (heads - 1),
        lambda t: jnp.concatenate([none, t[0, lead:], t[1, : tokens - 3 * HD]]),
        ahead,
    )
    right = edge(
        0, zp, lambda t: jnp.concatenate([t[0, :HALO], none]), [(j, i) for i, j in ahead]
    )

    pieces = [kv32, swap(tie(kv32, left, right), "c", 1)]

    def live_blocks(piece):
        firsts = piece.reshape(-1, LIVE_MOST, BLK, 2 * HD)[:, :, 0, 0]
        return jnp.sum(jnp.isfinite(firsts).astype(jnp.int32), axis=1)

    live_near = live_blocks(pieces[0])
    counts = jnp.concatenate([live_near, live_blocks(pieces[1])])
    every = jnp.arange(n_seq, dtype=jnp.int32)
    ends = jnp.arange(n_seq + 1, dtype=jnp.int32)
    off = jnp.sum(jnp.where(every[None, :] < ends[:, None], counts[None, :] * BLK, 0), axis=1)

    group_owners = jnp.stack([t[tokens + 1, HD : HD + merged_rows] for t in ys]).astype(jnp.int32)
    peer = (jnp.arange(heads, dtype=jnp.int32) ^ zp)[:, None]
    tgt = (group_owners * (heads * CAP) + peer * CAP + slots_of(group_owners)).reshape(-1)

    rows_c, rows_xc = tie((rows_c, rows_xc), left, right)
    weights = [
        weight_rows(0),
        swap(rows_c, HEAD, 1),
        weight_x,
        swap(rows_xc, HEAD, 3),
    ]

    res = lax.all_to_all(tie(res, left, right), SEQ, split_axis=0, concat_axis=0, tiled=True)

    one = zp[None].astype(jnp.int32)
    sent = attend(off, tgt, one, ys, left, right, pieces, n_seq * heads * CAP)
    sent, res, *weights = lax.optimization_barrier((sent, res, *weights))
    got = lax.all_to_all(
        sent.reshape(n_seq, heads * CAP * 4, HD), SEQ, split_axis=0, concat_axis=0, tiled=True
    ).reshape(n_seq * heads * CAP * 4, HD)
    res = res.reshape(n_seq * CAP * 4 * width // HD, HD)
    got_c = swap(got, HEAD, 1)
    got_x = swap(got, HEAD, 2)
    core = c[None].astype(jnp.int32)
    gain = layer_scale[None, :]
    slots = n_seq * CAP
    base = project(core, (got, got_c), weights[:2], res, gain, slots, True)
    got_xc = swap(tie(got_x, base), HEAD, 1)
    delivered = project(core, (got_x, got_xc), weights[2:], base, gain, slots, False)
    return (delivered, refreshed)


def solution(mesh):
    devices = np.asarray(mesh.devices).reshape(2, 4, 2, 4, 2, 2)
    fine = Mesh(devices, SEQ + HEAD)
    in_specs = (
        P(SEQ, HEAD),
        P(SEQ, HEAD),
        P(SEQ, HEAD),
        P(SEQ, HEAD),
        P(HEAD),
        P(HEAD, None),
        P(SEQ),
        P(SEQ, HEAD),
        P(SEQ, HEAD),
        P(SEQ),
        P(SEQ),
        P(SEQ, None),
        P(None, HEAD),
        P(SEQ, None),
    )
    out_specs = (P(SEQ, HEAD), P(SEQ, HEAD))
    return jax.shard_map(shards, mesh=fine, in_specs=in_specs, out_specs=out_specs, check_vma=False)
```

```python
import math

import jax
import jax.numpy as jnp
import numpy as np
from jax import lax
from jax.experimental import pallas as pl
from jax.experimental.pallas import tpu as pltpu
from jax.sharding import Mesh, PartitionSpec as P

HD = 128
BLK = 16
SEG_MOST = 201
LIVE_MOST = 6
CAP = 3
HALO = 208
PAD = 256
TOK = 512
KT = 2048
NEG = -1e30
SEQ = ("xh", "y", "zh", "zp")
HEAD = ("xl", "c")
bf16 = jnp.bfloat16
f32 = jnp.float32


def rope_parts(positions):
    half = HD // 2
    freqs = 100.0 ** (-jnp.arange(half, dtype=f32) / half)
    angles = positions.astype(f32)[:, None] * freqs[None, :]
    return jnp.cos(angles), jnp.sin(angles)


def rotate(vectors, cosine, sine):
    half = HD // 2
    a, b = vectors[..., :half], vectors[..., half:]
    c, s = cosine[:, None, :], sine[:, None, :]
    return jnp.concatenate([a * c - b * s, b * c + a * s], axis=-1)


def pack_kernel(idx, k_ref, v_ref, out_ref):
    heads = out_ref.shape[0]
    for j in range(LIVE_MOST):
        rows = pl.ds(pl.multiple_of(idx[j] * BLK, BLK), BLK)
        k = jnp.where(j < idx[LIVE_MOST], k_ref[rows, :], jnp.inf).astype(bf16)
        v = v_ref[rows, :]
        for p in range(heads):
            out_ref[p, j * BLK : (j + 1) * BLK, :HD] = k[:, p * HD : (p + 1) * HD]
            out_ref[p, j * BLK : (j + 1) * BLK, HD:] = v[:, p * HD : (p + 1) * HD]


def rope_kernel(q_ref, k_ref, v_ref, c_ref, s_ref, extra_ref, out_ref):
    tokens = q_ref.shape[0]
    c = c_ref[...]
    s = s_ref[...]
    for h in range(out_ref.shape[0]):
        cols = slice(h * HD, (h + 1) * HD)
        for j, ref in enumerate((q_ref, k_ref)):
            x = ref[:, cols].astype(f32)
            turned = x * c + pltpu.roll(x, HD // 2, 1) * s
            out_ref[h, :tokens, j * HD : (j + 1) * HD] = turned.astype(bf16)
        out_ref[h, :tokens, 2 * HD :] = v_ref[:, cols]
        out_ref[h, tokens:, :] = extra_ref[...]


def attention_kernel(off, tgt, zp, *refs):
    chunks = 4
    given = refs[:chunks]
    left, right = refs[chunks : chunks + 2]
    pieces = refs[chunks + 2 : -15]
    out, kc, vc, qs, kw, vw, ob, send, mx, ac, idcol, gathered, ids, ybuf, sems = refs[-15:]
    i = pl.program_id(0)
    sources = off.shape[0] - 1
    slot_rows = LIVE_MOST * BLK
    coef = math.log2(math.e) / math.sqrt(HD)
    total = off[sources]

    @pl.when(i == 0)
    def _():
        copies = []
        row = 0
        for n, piece in enumerate(pieces):
            to = gathered.at[pl.ds(row, piece.shape[0])]
            copies.append(pltpu.make_async_copy(piece, to, sems.at[n]))
            row += piece.shape[0]
        loads = []
        for n, y in enumerate(given):
            loads.append(pltpu.make_async_copy(y, ybuf.at[n], sems.at[len(pieces) + n]))
        for copy in loads + copies:
            copy.start()
        vc[:, HD:] = jnp.ones((vc.shape[0], HD), bf16)
        vw[:, HD:] = jnp.ones((vw.shape[0], HD), bf16)
        for copy in loads:
            copy.wait()
        for k in range(chunks):
            y = ybuf.at[k]
            chunk = zp[0] ^ k
            dst = pl.ds(pl.multiple_of(chunk * TOK, TOK), TOK)
            qs[dst, :] = y[:TOK, :HD]
            dst = pl.ds(pl.multiple_of(PAD + chunk * TOK, PAD), TOK)
            kw[dst, :] = y[:TOK, HD : 2 * HD]
            vw[dst, :HD] = y[:TOK, 2 * HD :]
            line = y[TOK:, :].astype(f32)
            at = pl.multiple_of(PAD + chunk * TOK, PAD)
            ids[:, pl.ds(at, 3 * HD)] = line[0:1, :]
            at = pl.multiple_of(PAD + chunk * TOK + 3 * HD, HD)
            ids[:, pl.ds(at, HD)] = line[1:2, :HD]
        end = PAD + chunks * TOK
        gap = PAD - HALO
        kw[:gap, :] = jnp.zeros((gap, HD), bf16)
        vw[:gap, :HD] = jnp.zeros((gap, HD), bf16)
        kw[gap:PAD, :] = left[:HALO, :HD]
        vw[gap:PAD, :HD] = left[:HALO, HD:]
        kw[end : end + HALO, :] = right[:HALO, :HD]
        vw[end : end + HALO, :HD] = right[:HALO, HD:]
        ids[:, :PAD] = left[HALO:, :].astype(f32)[0:1, :]
        ids[:, end:] = right[HALO:, :].astype(f32)[0:1, :]
        kw[end + HALO :, :] = jnp.zeros((gap, HD), bf16)
        vw[end + HALO :, :HD] = jnp.zeros((gap, HD), bf16)
        send[...] = jnp.zeros(send.shape, f32)
        for copy in copies:
            copy.wait()

        def copy_source(s, carry):
            dst = pl.ds(pl.multiple_of(off[s], BLK), slot_rows)
            src = pl.ds(pl.multiple_of(s * slot_rows, BLK), slot_rows)
            kc[dst, :] = gathered[src, :HD]
            vc[dst, :HD] = gathered[src, HD:]
            return carry

        lax.fori_loop(0, sources, copy_source, 0, unroll=2)
        tail = pl.ds(pl.multiple_of(total, BLK), KT)
        kc[tail, :] = jnp.zeros((KT, HD), bf16)
        vc[tail, :HD] = jnp.zeros((KT, HD), bf16)

    base = pl.multiple_of(i * TOK, TOK)
    sub = 256
    parts = TOK // sub
    wide = sub + 2 * PAD
    for b in range(parts):
        line = ids[:, pl.ds(pl.multiple_of(base + PAD + b * sub, sub), sub)]
        idcol[b * sub : (b + 1) * sub, :] = jnp.transpose(jnp.broadcast_to(line, (128, sub)))

    def scores(b, keys):
        q = qs[pl.ds(pl.multiple_of(base + b * sub, sub), sub), :]
        return lax.dot_general(q, keys, (((1,), (1,)), ((), ())), preferred_element_type=f32)

    def weigh(s, m):
        new = jnp.max(s, axis=1, keepdims=True)
        if m is not None:
            new = jnp.maximum(m, new)
        return new, jnp.exp2(s * coef - new * coef).astype(bf16)

    for b in range(parts):
        rows = pl.ds(pl.multiple_of(base + b * sub, sub), wide)
        s = scores(b, kw[rows, :])
        near = ids[:, rows]
        s = jnp.where(idcol[b * sub : (b + 1) * sub, :1] == near, s, NEG)
        new, w = weigh(s, None)
        mx[b * sub : (b + 1) * sub, :] = new
        ac[b * sub : (b + 1) * sub, :] = jnp.dot(w, vw[rows, :], preferred_element_type=f32)

    def visit(start, size, masked):
        rows = pl.ds(pl.multiple_of(start, size // 2), size)
        keys, values = kc[rows, :], vc[rows, :]

        def mask(s):
            if not masked:
                return s
            col = lax.broadcasted_iota(jnp.int32, s.shape, 1)
            return jnp.where(col < total - start, s, NEG)

        def absorb(b, s):
            here = pl.ds(pl.multiple_of(b * sub, sub), sub)
            m = mx[here, :]
            new, w = weigh(s, m)
            mx[here, :] = new
            part = jnp.dot(w, values, preferred_element_type=f32)
            ac[here, :] = ac[here, :] * jnp.exp2((m - new) * coef) + part

        if masked:

            def rows_of(b, carry):
                absorb(b, mask(scores(b, keys)))
                return carry

            lax.fori_loop(0, parts, rows_of, 0)
        else:
            ahead = scores(0, keys)
            for b in range(parts):
                s = ahead
                if b + 1 < parts:
                    ahead = scores(b + 1, keys)
                absorb(b, s)

    def loop(j, carry):
        visit(j * KT, KT, False)
        return carry

    full = total // KT
    rest = total - full * KT
    lax.fori_loop(0, full, loop, 0)

    for least, size in ((0, KT // 4), (KT // 4, KT)):

        @pl.when((rest > least) & (rest <= size))
        def _():
            visit(full * KT, size, True)

    ob[...] = ac[:, :HD] / ac[:, HD:]

    def place(r, carry):
        dst = tgt[(i ^ zp[0]) * (TOK // 4) + r] * 4
        send[pl.ds(pl.multiple_of(dst, 4), 4), :] = ob[pl.ds(pl.multiple_of(r * 4, 4), 4), :]
        return carry

    lax.fori_loop(0, TOK // 4, place, 0, unroll=8)

    @pl.when(i == pl.num_programs(0) - 1)
    def _():
        out[...] = send[...].astype(bf16)


def attend(off, tgt, zp, ys, left, right, pieces, slots):
    chunks = len(ys)
    sources = off.shape[0] - 1
    cache_most = sources * LIVE_MOST * BLK
    whole = pl.BlockSpec(memory_space=pltpu.VMEM)
    return pl.pallas_call(
        attention_kernel,
        out_shape=jax.ShapeDtypeStruct((slots * 4, HD), bf16),
        grid_spec=pltpu.PrefetchScalarGridSpec(
            num_scalar_prefetch=3,
            grid=(chunks,),
            in_specs=[pl.BlockSpec(memory_space=pl.ANY)] * chunks
            + [whole] * 2
            + [pl.BlockSpec(memory_space=pl.ANY)] * len(pieces),
            out_specs=whole,
            scratch_shapes=[
                pltpu.VMEM((cache_most + KT, HD), bf16),
                pltpu.VMEM((cache_most + KT, 2 * HD), bf16),
                pltpu.VMEM((chunks * TOK, HD), bf16),
                pltpu.VMEM((chunks * TOK + 2 * PAD, HD), bf16),
                pltpu.VMEM((chunks * TOK + 2 * PAD, 2 * HD), bf16),
                pltpu.VMEM((TOK, HD), f32),
                pltpu.VMEM((slots * 4, HD), f32),
                pltpu.VMEM((TOK, 1), f32),
                pltpu.VMEM((TOK, 2 * HD), f32),
                pltpu.VMEM((TOK, 128), f32),
                pltpu.VMEM((cache_most, 2 * HD), bf16),
                pltpu.VMEM((1, chunks * TOK + 2 * PAD), f32),
                pltpu.VMEM((chunks, *ys[0].shape), bf16),
                pltpu.SemaphoreType.DMA((len(pieces) + chunks,)),
            ],
        ),
        compiler_params=pltpu.CompilerParams(
            dimension_semantics=("arbitrary",), vmem_limit_bytes=48 << 20
        ),
        cost_estimate=pl.CostEstimate(
            flops=4 * 2048 * 7168 * 128, bytes_accessed=8 << 20, transcendentals=2048 * 7168
        ),
    )(off, tgt, zp, *ys, left, right, *pieces)


def project_half(core, halves, weights, scale, att, proj):
    c = core[0]
    groups = halves[0].shape[0] // (8 * 48)

    @pl.when(pl.program_id(0) == 0)
    def _():
        for k, a in enumerate(halves):

            def move(g, carry):
                to = pl.ds(pl.multiple_of((g * 2 + (c ^ k)) * 48, 16), 48)
                for p in range(8):
                    src = pl.ds(pl.multiple_of(g * 384 + p * 48, 16), 48)
                    att[c ^ (p // 4), to, (p % 4) * HD : (p % 4 + 1) * HD] = a[src, :]
                return carry

            lax.fori_loop(0, groups, move, 0)

    total = jnp.dot(att[0], weights[0][...], preferred_element_type=f32)
    total = total + jnp.dot(att[1], weights[1][...], preferred_element_type=f32)
    total = total * scale[...]
    rows = total.shape[0]
    for d in range(total.shape[1] // HD):
        proj[d * rows : (d + 1) * rows, :] = total[:, d * HD : (d + 1) * HD]


def near_kernel(core, a0, a1, w0, w1, res, scale, out, att, proj, res32):
    b = pl.program_id(0)

    @pl.when(b == 0)
    def _():
        res32[...] = res[...].astype(f32)

    project_half(core, (a0, a1), (w0, w1), scale, att, proj)
    slots = out.shape[0] // 4
    per = out.shape[1] // HD
    for d in range(per):
        for t in range(4):
            new = proj[pl.ds(d * 4 * slots + t, slots, stride=4), :]
            old = res32[pl.ds(t * 8 + b * per + d, slots, stride=32), :]
            out[t * slots : (t + 1) * slots, d * HD : (d + 1) * HD] = old + new


def far_kernel(core, a0, a1, w0, w1, base, scale, mix, out, att, proj):
    project_half(core, (a0, a1), (w0, w1), scale, att, proj)
    slots = out.shape[0]
    for d in range(base.shape[1] // HD):
        parts = []
        for t in range(4):
            new = proj[pl.ds(d * 4 * slots + t, slots, stride=4), :]
            old = base[t * slots : (t + 1) * slots, d * HD : (d + 1) * HD]
            parts.append((old + new).astype(bf16))
        rows = jnp.concatenate(parts, axis=1)
        out[:, d * 4 * HD : (d + 1) * 4 * HD] = jnp.dot(
            rows, mix[...], preferred_element_type=f32
        ).astype(bf16)


def project(core, atts, weights, rest, scale, slots, near):
    width = weights[0].shape[1]
    part = 256
    whole = pl.BlockSpec(memory_space=pltpu.VMEM)
    blocks = lambda rows, columns: pl.BlockSpec((rows, columns), lambda b, *_: (0, b))
    specs = [whole] * 2 + [blocks(weights[0].shape[0], part)] * 2
    scratch = [
        pltpu.VMEM((2, slots * 4, 4 * HD), bf16),
        pltpu.VMEM((slots * 4 * part // HD, HD), f32),
    ]
    if near:
        specs += [whole, blocks(1, part)]
        scratch.append(pltpu.VMEM((slots * 32, HD), f32))
        out_shape = jax.ShapeDtypeStruct((slots * 4, width), f32)
        out_specs = blocks(slots * 4, part)
        given = (rest, scale)
    else:
        source = np.arange(4 * HD)
        mix = np.zeros((4 * HD, 4 * HD), np.float32)
        mix[source, (source % HD) * 4 + source // HD] = 1.0
        specs += [blocks(slots * 4, part), blocks(1, part), whole]
        out_shape = jax.ShapeDtypeStruct((slots, 4 * width), bf16)
        out_specs = blocks(slots, 4 * part)
        given = (rest, scale, jnp.asarray(mix, bf16))
    return pl.pallas_call(
        near_kernel if near else far_kernel,
        out_shape=out_shape,
        grid_spec=pltpu.PrefetchScalarGridSpec(
            num_scalar_prefetch=1,
            grid=(width // part,),
            in_specs=specs,
            out_specs=out_specs,
            scratch_shapes=scratch,
        ),
        compiler_params=pltpu.CompilerParams(
            dimension_semantics=("arbitrary",), vmem_limit_bytes=40 << 20
        ),
        cost_estimate=pl.CostEstimate(
            flops=2 * 768 * 1024 * 1024, bytes_accessed=10 << 20, transcendentals=0
        ),
    )(core, *atts, *weights, *given)


def swap(x, axis, k):
    n = lax.axis_size(axis)
    return lax.ppermute(x, axis, [(i, i ^ k) for i in range(n)])


def tie(x, *others):
    return lax.optimization_barrier((x, *others))[0]


def shards(
    queries,
    keys_new,
    values_new,
    residual,
    layer_scale,
    out_weight,
    segment_ids,
    cache_keys,
    cache_values,
    block_live,
    recompute_block,
    recompute_hidden,
    key_weight,
    owners,
):
    tokens, columns = queries.shape
    heads = columns // HD
    n_head = lax.axis_size(HEAD)
    n_seq = lax.axis_size(SEQ)
    seq = lax.axis_index(SEQ)
    zp, c = (lax.axis_index(n) for n in ("zp", "c"))
    head = lax.axis_index(HEAD)
    merged_rows = tokens // 4
    n_group = n_seq // heads
    whole = pl.BlockSpec(memory_space=pltpu.VMEM)

    width = residual.shape[1]

    def weight_rows(j):
        return lax.dynamic_slice(out_weight, (0, (head ^ j) * width), (columns, width))

    weight_x = swap(weight_rows(2), HEAD, 2)

    marks = segment_ids + 1
    before = lax.ppermute(marks[tokens - PAD :], SEQ, [(i, i + 1) for i in range(n_seq - 1)])
    near = jnp.concatenate([before, marks])
    same = marks[:, None] == near[None, :]
    index = jnp.arange(PAD + tokens, dtype=jnp.int32)
    first = jnp.min(jnp.where(same, index[None, :], PAD + tokens), axis=1)
    cosine, sine = rope_parts(PAD + jnp.arange(tokens, dtype=jnp.int32) - first)

    extra = jnp.concatenate([marks, owners[:, 0]])
    extra = jnp.pad(extra, (0, BLK * 3 * HD - extra.shape[0])).astype(bf16).reshape(BLK, 3 * HD)
    qkv = pl.pallas_call(
        rope_kernel,
        out_shape=jax.ShapeDtypeStruct((heads, tokens + BLK, 3 * HD), bf16),
        in_specs=[whole] * 6,
        out_specs=whole,
    )(
        queries,
        keys_new,
        values_new,
        jnp.concatenate([cosine, cosine], axis=1),
        jnp.concatenate([-sine, sine], axis=1),
        extra,
    )

    cache_rows = cache_keys.shape[0]
    block = recompute_block[0]
    fresh = jnp.dot(recompute_hidden, key_weight, preferred_element_type=f32)
    fresh_rows = seq * cache_rows + block * BLK + jnp.arange(BLK, dtype=jnp.int32)
    fresh = rotate(fresh.reshape(BLK, heads, HD), *rope_parts(fresh_rows % SEG_MOST))
    fresh = fresh.reshape(BLK, columns).astype(bf16)
    refreshed = lax.dynamic_update_slice(cache_keys, fresh, (block * BLK, 0))

    live = block_live > 0
    n_blocks = block_live.shape[0]
    blocks = jnp.arange(n_blocks, dtype=jnp.int32)
    rank = jnp.sum(jnp.where(blocks[None, :] < blocks[:, None], live[None, :], False), axis=1)
    hit = live[None, :] & (rank[None, :] == jnp.arange(LIVE_MOST, dtype=jnp.int32)[:, None])
    order = jnp.sum(jnp.where(hit, blocks[None, :], 0), axis=1)
    order = jnp.concatenate([order, jnp.sum(live.astype(jnp.int32), keepdims=True)])
    kv = pl.pallas_call(
        pack_kernel,
        out_shape=jax.ShapeDtypeStruct((heads, LIVE_MOST * BLK, 2 * HD), bf16),
        grid_spec=pltpu.PrefetchScalarGridSpec(
            num_scalar_prefetch=1, grid=(), in_specs=[whole] * 2, out_specs=whole
        ),
    )(order, refreshed, cache_values)

    def spread(x, j):
        pairs = []
        for a in range(2):
            for b in range(heads):
                for d in range(2):
                    pairs.append(((a * heads + b) * 2 + d, (d * heads + (b ^ j)) * 2 + a))
        part = lax.dynamic_index_in_dim(x, zp ^ j, 0, keepdims=False)
        return lax.ppermute(part, ("zh", "zp", "c"), pairs)

    kv = tie(kv, before)
    cached = [spread(kv, j) for j in range(heads)]
    kv4 = jnp.concatenate(cached, axis=0)

    ys = [spread(qkv, j) for j in range(heads)]

    kv4 = tie(kv4, qkv, weight_x)
    kv8 = jnp.concatenate([kv4, swap(kv4, "xh", 1)], axis=0)
    kv32 = lax.all_gather(kv8, "y", axis=0, tiled=True)

    def slots_of(owner_rows):
        r = jnp.arange(merged_rows, dtype=jnp.int32)
        equal = owner_rows[:, :, None] == owner_rows[:, None, :]
        return jnp.sum((equal & (r[None, None, :] < r[None, :, None])).astype(jnp.int32), axis=2)

    own_target = owners[:, 0] * CAP + slots_of(owners[:, 0][None, :])[0]
    choose = (jnp.arange(n_seq * CAP, dtype=jnp.int32)[:, None] == own_target[None, :]).astype(bf16)
    residual = tie(residual, kv8, qkv)
    res = jnp.dot(
        choose, residual.reshape(merged_rows, 4 * width), preferred_element_type=f32
    ).astype(bf16)
    res = res.reshape(n_seq, CAP * 4 * width // HD, HD)

    out_weight = tie(out_weight, kv8, qkv)
    rows_c, rows_xc = weight_rows(1), weight_rows(3)
    edges = tie(tuple(ys), res, rows_c, rows_xc)

    def edge(low, j, line, pairs):
        part = jnp.stack([t[low : low + HALO, HD:] for t in edges])
        part = lax.dynamic_index_in_dim(part, j, 0, keepdims=False)
        line = lax.dynamic_index_in_dim(jnp.stack([line(t[tokens : tokens + 2]) for t in edges]), j, 0)
        part = jnp.concatenate([part, jnp.pad(line, ((0, BLK - 1), (0, 0)))], axis=0)
        return lax.ppermute(part, ("xh", "y", "c"), pairs)

    ahead = [(i, i + 1) for i in range(n_group - 1)]
    none = jnp.zeros((PAD - HALO,), bf16)
    lead = tokens - HALO
    left = edge(
        lead,
        zp ^ (heads - 1),
        lambda t: jnp.concatenate([none, t[0, lead:], t[1, : tokens - 3 * HD]]),
        ahead,
    )
    right = edge(
        0, zp, lambda t: jnp.concatenate([t[0, :HALO], none]), [(j, i) for i, j in ahead]
    )

    pieces = [kv32, swap(tie(kv32, left, right), "c", 1)]

    def live_blocks(piece):
        firsts = piece.reshape(-1, LIVE_MOST, BLK, 2 * HD)[:, :, 0, 0]
        return jnp.sum(jnp.isfinite(firsts).astype(jnp.int32), axis=1)

    live_near = live_blocks(pieces[0])
    counts = jnp.concatenate([live_near, live_blocks(pieces[1])])
    every = jnp.arange(n_seq, dtype=jnp.int32)
    ends = jnp.arange(n_seq + 1, dtype=jnp.int32)
    off = jnp.sum(jnp.where(every[None, :] < ends[:, None], counts[None, :] * BLK, 0), axis=1)

    group_owners = jnp.stack([t[tokens + 1, HD : HD + merged_rows] for t in ys]).astype(jnp.int32)
    peer = (jnp.arange(heads, dtype=jnp.int32) ^ zp)[:, None]
    tgt = (group_owners * (heads * CAP) + peer * CAP + slots_of(group_owners)).reshape(-1)

    rows_c, rows_xc = tie((rows_c, rows_xc), left, right)
    weights = [
        weight_rows(0),
        swap(rows_c, HEAD, 1),
        weight_x,
        swap(rows_xc, HEAD, 3),
    ]

    res = lax.all_to_all(tie(res, left, right), SEQ, split_axis=0, concat_axis=0, tiled=True)

    one = zp[None].astype(jnp.int32)
    sent = attend(off, tgt, one, ys, left, right, pieces, n_seq * heads * CAP)
    sent, res, *weights = lax.optimization_barrier((sent, res, *weights))
    got = lax.all_to_all(
        sent.reshape(n_seq, heads * CAP * 4, HD), SEQ, split_axis=0, concat_axis=0, tiled=True
    ).reshape(n_seq * heads * CAP * 4, HD)
    res = res.reshape(n_seq * CAP * 4 * width // HD, HD)
    got_c = swap(got, HEAD, 1)
    got_x = swap(got, HEAD, 2)
    core = c[None].astype(jnp.int32)
    gain = layer_scale[None, :]
    slots = n_seq * CAP
    base = project(core, (got, got_c), weights[:2], res, gain, slots, True)
    got_xc = swap(tie(got_x, base), HEAD, 1)
    delivered = project(core, (got_x, got_xc), weights[2:], base, gain, slots, False)
    return (delivered, refreshed)


def solution(mesh):
    devices = np.asarray(mesh.devices).reshape(2, 4, 2, 4, 2, 2)
    fine = Mesh(devices, SEQ + HEAD)
    in_specs = (
        P(SEQ, HEAD),
        P(SEQ, HEAD),
        P(SEQ, HEAD),
        P(SEQ, HEAD),
        P(HEAD),
        P(HEAD, None),
        P(SEQ),
        P(SEQ, HEAD),
        P(SEQ, HEAD),
        P(SEQ),
        P(SEQ),
        P(SEQ, None),
        P(None, HEAD),
        P(SEQ, None),
    )
    out_specs = (P(SEQ, HEAD), P(SEQ, HEAD))
    return jax.shard_map(shards, mesh=fine, in_specs=in_specs, out_specs=out_specs, check_vma=False)
```
